32 devices in a mesh: gx: 2 (over x), gy: 4 (over z), gz: 4 (over y, core).
Axes of the slice: x: 2, y: 2, z: 4, core: 2. Of those that a mesh axis runs over, the one named last changes fastest.
Arguments:
- fields: float32 [12, 16, 32, 512], P(None, 'gx', 'gy', 'gz'), as said below
- reacting: int32 [16, 32, 512], P('gx', 'gy', 'gz'), may hold values from 0 to 1, as said below
- panel_map: int32 [2, 16, 512], P(None, 'gx', 'gz'), may hold values from 0 to 255, as said below
- layer_one: bfloat16 [1600, 12], replicated, may hold values from -4 to 4
- layer_two: bfloat16 [800, 1600], replicated, may hold values from -0.21875 to 0.21875
- layer_three: bfloat16 [400, 800], replicated, may hold values from -0.3125 to 0.3125
- layer_four: bfloat16 [12, 400], replicated, may hold values from -0.3125 to 0.3125
Outputs:
- new_fields: float32 [12, 16, 32, 512], P(None, 'gx', 'gy', 'gz')
- impulse: float32 [256], P(('gx', 'gy', 'gz'))
The draws below stay inside these ranges and needn't reach their ends.
Inputs may be any that keep to these rules, and one draw needn't show every extreme that they name: `fields`: component 0 (density) lies between 0.3 and 3.3; the velocities (components 1 to 3 over component 0) between -1.2 and 1.2; the pressure 0.4 (component 4 - |momentum|^2 / (2 density)) between 0.3 and 5; components 5 to 11 are 0.01 to 0.14 times component 0. Each device's aligned block of 8 x 8 x 128 cells holds at most 128 reacting cells. The blocks that share their ranges along the second and third dimensions hold exactly 64 reacting cells each on average, and one in eight of them, and at least one, hold exactly 128. `panel_map`: every panel is a patch of 8 x 8 cells of one wall, shifted by 4 cells along the first dimension and closed around it; panels are numbered in a random order and each number is used once.
All inputs are finite; a program needn't handle non-finite values.
Results may differ from the reference program's by a relative error of at most 0.0014.
Values may be sent and summed in bfloat16 or wider, within the bound.
No kernel may reach another device: no remote copies, remote signals or barrier semaphores. Data moves between devices by JAX's collectives and lax.ppermute only.
A program may use at most 64 MiB of HBM per device.

```python
import math
import jax
import jax.numpy as jnp
from jax import lax

CX = 8
CY = 8
CZ = 128
BAL = 64
COMPS = 12
H1 = 1600
H2 = 800
H3 = 400
PATCH = 8
NX = 16
NY = 32
NZ = 512
REACTING = 2048
PANELS = 256


HEAT_RATIO = 1.4


def draw_fields(key, part):
    sub_keys = jax.random.split(key, 4)
    shape_grid = (NX, NY, NZ)
    log_density = jax.random.uniform(sub_keys[0], shape_grid, jnp.float32, math.log(0.5), math.log(2.0))
    log_pressure = jax.random.uniform(sub_keys[1], shape_grid, jnp.float32, math.log(0.5), math.log(3.0))
    fractions = jax.random.uniform(sub_keys[3], (COMPS - 5,) + shape_grid, jnp.float32, 0.01, 0.14)
    velocity = jnp.clip(0.4 * jax.random.normal(sub_keys[2], (3,) + shape_grid, jnp.float32), -1.2, 1.2)
    density = jnp.exp(log_density)
    pressure = jnp.exp(log_pressure)
    energy = pressure / (HEAT_RATIO - 1.0) + 0.5 * density * jnp.sum(velocity * velocity, axis=0)
    return jnp.concatenate([density[None], density[None] * velocity, energy[None], density[None] * fractions], axis=0).astype(jnp.float32)


def draw_reacting(key, part):
    gx_count = NX // CX
    gy_count = NY // CY
    gz_count = NZ // CZ
    capacity = BAL * min(4, gx_count)
    hot_count = max(gx_count // 8, 1)
    cold_count = gx_count - hot_count
    rest_rows = gx_count * BAL - hot_count * capacity
    base_rows = rest_rows // cold_count
    extra_rows = rest_rows % cold_count
    groups = gy_count * gz_count
    sub_keys = jax.random.split(key, 3)
    ranks = jnp.arange(gx_count, dtype=jnp.int32)
    cold_rank = ranks - hot_count
    pair_index = jnp.maximum(cold_rank, 0) // 2
    sign_pair = jnp.where(cold_rank % 2 == 0, 1, -1) * jnp.where((cold_rank == cold_count - 1) & (cold_count % 2 == 1), 0, 1)
    pair_shift = jax.random.randint(sub_keys[0], (groups, gx_count // 2 + 1), 0, base_rows // 2 + 1, dtype=jnp.int32)
    cold_rows = base_rows + (cold_rank < extra_rows).astype(jnp.int32)[None, :] + sign_pair[None, :] * pair_shift[:, pair_index]
    by_rank = jnp.where(ranks[None, :] < hot_count, capacity, cold_rows).astype(jnp.int32)
    orders = jax.vmap(lambda sub_key: jax.random.permutation(sub_key, gx_count))(jax.random.split(sub_keys[1], groups))
    by_device = jnp.zeros((groups, gx_count), jnp.int32).at[jnp.arange(groups)[:, None], orders].set(by_rank)
    cell_count = CX * CY * CZ
    cell_order = jax.vmap(lambda sub_key: jax.random.permutation(sub_key, cell_count))(jax.random.split(sub_keys[2], groups * gx_count))
    cell_order = cell_order.reshape(groups, gx_count, cell_count)
    react_flags = (cell_order < by_device[:, :, None]).astype(jnp.int32)
    blocks = react_flags.reshape(gy_count, gz_count, gx_count, CX, CY, CZ)
    return blocks.transpose(2, 3, 0, 4, 1, 5).reshape(NX, NY, NZ)


def draw_panel_map(key, part):
    across = NX // PATCH
    along = NZ // PATCH
    panel_total = 2 * across * along
    shuffle = jax.random.permutation(key, panel_total)
    wall_side = jnp.arange(2, dtype=jnp.int32)[:, None, None]
    x_cells = jnp.arange(NX, dtype=jnp.int32)[None, :, None]
    z_cells = jnp.arange(NZ, dtype=jnp.int32)[None, None, :]
    patch_index = wall_side * across * along + (x_cells + PATCH // 2) // PATCH % across * along + z_cells // PATCH
    return shuffle[patch_index].astype(jnp.int32)


def bell_draw(key, dims, width, bound, held_as=jnp.bfloat16):
    array = width * jax.random.normal(key, dims, jnp.float32)
    return jnp.clip(array, min=-bound, max=bound).astype(held_as)


def setup_inputs(seed: int = 0) -> dict:
    arg_keys = jax.random.split(jax.random.key(seed), 8)
    fields = draw_fields(jax.random.fold_in(arg_keys[7], 71), 0)
    reacting = draw_reacting(jax.random.fold_in(arg_keys[7], 71), 0)
    panel_map = draw_panel_map(jax.random.fold_in(arg_keys[7], 71), 0)
    layer_one = bell_draw(arg_keys[3], (H1, COMPS), 1.0, 4.0)
    layer_two = bell_draw(arg_keys[4], (H2, H1), (H1 // 2) ** -0.5, 0.21875)
    layer_three = bell_draw(arg_keys[5], (H3, H2), (H2 // 2) ** -0.5, 0.3125)
    layer_four = bell_draw(arg_keys[6], (COMPS, H3), H3 ** -0.5, 0.3125)
    return dict(fields=fields, reacting=reacting, panel_map=panel_map, layer_one=layer_one, layer_two=layer_two, layer_three=layer_three, layer_four=layer_four)


HEAT_RATIO = 1.4
TIME_STEP = 0.1
CHEM_STEP = 0.25
WENO_EPS = 1e-06

def take_slab(array_in, begin_at, length_of, flux_axis):
    return lax.slice_in_dim(array_in, begin_at, begin_at + length_of, axis=flux_axis)

def weno_face(upwind_two, upwind_one, center, downwind_one, downwind_two):
    cand_zero = (2.0 * upwind_two - 7.0 * upwind_one + 11.0 * center) / 6.0
    cand_one = (-upwind_one + 5.0 * center + 2.0 * downwind_one) / 6.0
    cand_two = (2.0 * center + 5.0 * downwind_one - downwind_two) / 6.0
    smooth_zero = 13.0 / 12.0 * (upwind_two - 2.0 * upwind_one + center) ** 2 + 0.25 * (upwind_two - 4.0 * upwind_one + 3.0 * center) ** 2
    smooth_one = 13.0 / 12.0 * (upwind_one - 2.0 * center + downwind_one) ** 2 + 0.25 * (upwind_one - downwind_one) ** 2
    smooth_two = 13.0 / 12.0 * (center - 2.0 * downwind_one + downwind_two) ** 2 + 0.25 * (3.0 * center - 4.0 * downwind_one + downwind_two) ** 2
    weight_zero = 0.1 / (WENO_EPS + smooth_zero) ** 2
    weight_one = 0.6 / (WENO_EPS + smooth_one) ** 2
    weight_two = 0.3 / (WENO_EPS + smooth_two) ** 2
    weight_sum = weight_zero + weight_one + weight_two
    return (weight_zero * cand_zero + weight_one * cand_one + weight_two * cand_two) / weight_sum

def to_recon(fields):
    density = fields[0]
    velocity = fields[1:4] / density[None]
    pressure = (HEAT_RATIO - 1.0) * (fields[4] - 0.5 * density * lax.optimization_barrier(jnp.sum(velocity * velocity, axis=0)))
    fractions = fields[5:] / density[None]
    return jnp.concatenate([jnp.log(density)[None], velocity, jnp.log(pressure)[None], fractions], axis=0)

def normal_of(normal, ndims):
    return (jnp.arange(3) == normal).reshape((3,) + (1,) * (ndims - 1))

def side_terms(recon, normal):
    density = jnp.exp(recon[0])
    velocity = recon[1:4]
    pressure = jnp.exp(recon[4])
    fractions = recon[5:]
    speed_n = velocity[normal]
    energy = pressure / (HEAT_RATIO - 1.0) + 0.5 * density * lax.optimization_barrier(jnp.sum(velocity * velocity, axis=0))
    conserved = jnp.concatenate([density[None], density[None] * velocity, energy[None], density[None] * fractions], axis=0)
    mass_flux = density * speed_n
    normal_mask = normal_of(normal, recon.ndim)
    momentum_flux = mass_flux[None] * velocity + jnp.where(normal_mask, pressure[None], 0.0)
    flux_terms = jnp.concatenate([mass_flux[None], momentum_flux, ((energy + pressure) * speed_n)[None], mass_flux[None] * fractions], axis=0)
    sound_speed = jnp.sqrt(HEAT_RATIO * pressure / density)
    return (density, velocity, pressure, fractions, energy, conserved, flux_terms, speed_n, sound_speed)

def star_state(density, velocity, pressure, fractions, energy, speed_n, wave_speed, contact, normal_mask):
    relative = wave_speed - speed_n
    factor = density * relative / (wave_speed - contact)
    star_velocity = jnp.where(normal_mask, contact[None], velocity)
    star_energy = energy / density + (contact - speed_n) * (contact + pressure / (density * relative))
    return jnp.concatenate([factor[None], factor[None] * star_velocity, (factor * star_energy)[None], factor[None] * fractions], axis=0)

def hllc_flux(left_recon, right_recon, normal):
    left_density, left_velocity, left_pressure, left_fractions, left_energy, left_cons, left_flux, left_speed, left_sound = side_terms(left_recon, normal)
    right_density, right_velocity, right_pressure, right_fractions, right_energy, right_cons, right_flux, right_speed, right_sound = side_terms(right_recon, normal)
    wave_left = jnp.minimum(left_speed - left_sound, right_speed - right_sound)
    wave_right = jnp.maximum(left_speed + left_sound, right_speed + right_sound)
    left_rel = wave_left - left_speed
    right_rel = wave_right - right_speed
    contact = (right_pressure - left_pressure + left_density * left_speed * left_rel - right_density * right_speed * right_rel) / (left_density * left_rel - right_density * right_rel)
    normal_mask = normal_of(normal, left_recon.ndim)
    star_left = star_state(left_density, left_velocity, left_pressure, left_fractions, left_energy, left_speed, wave_left, contact, normal_mask)
    star_right = star_state(right_density, right_velocity, right_pressure, right_fractions, right_energy, right_speed, wave_right, contact, normal_mask)
    left_star_flux = left_flux + wave_left[None] * (star_left - left_cons)
    right_star_flux = right_flux + wave_right[None] * (star_right - right_cons)
    return jnp.where(wave_left[None] >= 0, left_flux, jnp.where(contact[None] >= 0, left_star_flux, jnp.where(wave_right[None] > 0, right_star_flux, right_flux)))

def face_flux(padded, normal):
    flux_axis = normal + 1
    face_count = padded.shape[flux_axis] - 5
    stencil = [take_slab(padded, offset, face_count, flux_axis) for offset in range(6)]
    left_state = weno_face(stencil[0], stencil[1], stencil[2], stencil[3], stencil[4])
    right_state = weno_face(stencil[5], stencil[4], stencil[3], stencil[2], stencil[1])
    return hllc_flux(left_state, right_state, normal)

def mirror_walls(padded, normal, at_first, at_last):
    flux_axis = normal + 1
    cell_count = padded.shape[flux_axis] - 6
    flip_sign = jnp.where(jnp.arange(padded.shape[0]) == 1 + normal, -1.0, 1.0).astype(padded.dtype).reshape((-1, 1, 1, 1))
    ghost_low = jnp.flip(take_slab(padded, 3, 3, flux_axis), flux_axis) * flip_sign
    ghost_high = jnp.flip(take_slab(padded, cell_count, 3, flux_axis), flux_axis) * flip_sign
    low_side = jnp.where(at_first, ghost_low, take_slab(padded, 0, 3, flux_axis))
    high_side = jnp.where(at_last, ghost_high, take_slab(padded, cell_count + 3, 3, flux_axis))
    return jnp.concatenate([low_side, take_slab(padded, 3, cell_count, flux_axis), high_side], axis=flux_axis)

def chem_rates(features, layer_one, layer_two, layer_three, layer_four):
    hidden_one = jax.nn.gelu(jnp.dot(layer_one, features, preferred_element_type=jnp.float32)).astype(jnp.bfloat16)
    hidden_two = jax.nn.gelu(jnp.dot(layer_two, hidden_one, preferred_element_type=jnp.float32)).astype(jnp.bfloat16)
    hidden_three = jax.nn.gelu(jnp.dot(layer_three, hidden_two, preferred_element_type=jnp.float32)).astype(jnp.bfloat16)
    return jnp.dot(layer_four, hidden_three, preferred_element_type=jnp.float32).astype(jnp.bfloat16)

def reference(fields, reacting, panel_map, layer_one, layer_two, layer_three, layer_four):
    recon_fields = to_recon(fields)
    update = jnp.zeros_like(fields)
    wall_faces = None
    for normal in range(3):
        widths = [(0, 0)] * 4
        widths[normal + 1] = (3, 3)
        padded = mirror_walls(jnp.pad(recon_fields, widths), normal, True, True)
        split_axis = 3 if normal == 0 else 1
        extent = padded.shape[split_axis]
        pieces = math.gcd(extent, 64)
        blocked = jnp.moveaxis(padded, split_axis, 0)
        blocked = blocked.reshape((pieces, extent // pieces) + blocked.shape[1:])

        def one_block(one_piece):
            local_block = jnp.moveaxis(one_piece, 0, split_axis)
            face_fluxes = face_flux(local_block, normal)
            cell_count = face_fluxes.shape[normal + 1] - 1
            change = take_slab(face_fluxes, 1, cell_count, normal + 1) - take_slab(face_fluxes, 0, cell_count, normal + 1)
            edge_faces = jnp.concatenate([take_slab(face_fluxes, 0, 1, normal + 1), take_slab(face_fluxes, cell_count, 1, normal + 1)], axis=normal + 1)
            return (jnp.moveaxis(change, split_axis, 0), jnp.moveaxis(edge_faces, split_axis, 0))
        changes, edges_all = lax.map(one_block, blocked)
        change = jnp.moveaxis(changes.reshape((extent,) + changes.shape[2:]), 0, split_axis)
        update = update + change
        if normal == 1:
            wall_faces = jnp.moveaxis(edges_all.reshape((extent,) + edges_all.shape[2:]), 0, split_axis)
    cell_total = reacting.size
    flat_recon = recon_fields.reshape(COMPS, cell_total)
    where_rows = jnp.nonzero(reacting.reshape(cell_total), size=REACTING)[0].astype(jnp.int32)
    features = flat_recon[:, where_rows].astype(jnp.bfloat16)
    block_rows = math.gcd(REACTING, 4096)
    block_count = REACTING // block_rows
    feature_blocks = jnp.moveaxis(features.reshape(COMPS, block_count, block_rows), 1, 0)
    rate_blocks = lax.map(lambda row_block: chem_rates(row_block, layer_one, layer_two, layer_three, layer_four), feature_blocks)
    rate_rows = jnp.moveaxis(rate_blocks, 0, 1).reshape(COMPS, REACTING)
    source = jnp.zeros((COMPS, cell_total), jnp.float32).at[:, where_rows].add(rate_rows.astype(jnp.float32))
    new_fields = fields - TIME_STEP * update + CHEM_STEP * source.reshape(fields.shape)
    wall_push = jnp.moveaxis(wall_faces[2], 1, 0)
    impulse = jax.ops.segment_sum(wall_push.reshape(-1), panel_map.reshape(-1), num_segments=PANELS) / float(PATCH * PATCH)
    return (new_fields, impulse)
```

```python
import jax
import jax.numpy as jnp
from jax import lax
from jax.experimental import pallas as pl
from jax.experimental.pallas import tpu as pltpu
from jax.sharding import PartitionSpec as P

BAL = 64
COMPS = 12
PATCH = 8

HEAT_RATIO = 1.4
TIME_STEP = 0.1
CHEM_STEP = 0.25
WENO_EPS = 1e-06
EPS = WENO_EPS * 4.0 / 36.0
AXES = ("gx", "gy", "gz")
F32 = jnp.float32
BF16 = jnp.bfloat16
VM = pl.BlockSpec(memory_space=pltpu.VMEM)
SM = pl.BlockSpec(memory_space=pltpu.SMEM)


def weno_line(v):
    n = len(v)
    d = [(v[j + 1] - v[j]) * (1.0 / 6.0) for j in range(n - 1)]
    d3 = [3.0 * x for x in d]
    q = {}
    for e in range(1, n - 1):
        s = d[e] - d[e - 1]
        q[e] = (13.0 / 3.0) * (s * s) + EPS
    upper, lower = {}, {}
    for e in range(2, n - 2):
        dm, dp = d[e - 1], d[e]
        t0 = d3[e - 1] - d[e - 2]
        t1 = dm + dp
        t2 = d3[e] - d[e + 1]
        b0 = q[e - 1] + t0 * t0
        b1 = q[e] + t1 * t1
        b2 = q[e + 1] + t2 * t2
        m01, m02, m12 = b0 * b1, b0 * b2, b1 * b2
        s01, s02, s12 = m01 * m01, m02 * m02, m12 * m12
        w1, w01, w12 = 6.0 * s02, 3.0 * s01, 3.0 * s12
        if e < n - 3:
            num = s12 * (t0 + t0 - dm) + w1 * (t1 + dp) + w01 * (t2 + dp)
            upper[e] = v[e] + num / (s12 + w1 + w01)
        if e > 2:
            num = s01 * (t2 + t2 - dp) + w1 * (t1 + dm) + w12 * (t0 + dm)
            lower[e] = v[e] - num / (s01 + w1 + w12)
    return upper, lower


def weno_one(v):
    d = [(v[j + 1] - v[j]) * (1.0 / 6.0) for j in range(4)]
    s = [d[j + 1] - d[j] for j in range(3)]
    q = [(13.0 / 3.0) * (x * x) + EPS for x in s]
    dm, dp = d[1], d[2]
    t0, t1, t2 = 3.0 * dm - d[0], dm + dp, 3.0 * dp - d[3]
    b0, b1, b2 = q[0] + t0 * t0, q[1] + t1 * t1, q[2] + t2 * t2
    m01, m02, m12 = b0 * b1, b0 * b2, b1 * b2
    w0, w1, w2 = m12 * m12, 6.0 * (m02 * m02), 3.0 * (m01 * m01)
    num = w0 * (t0 + t0 - dm) + w1 * (t1 + dp) + w2 * (t2 + dp)
    return v[2] + num / (w0 + w1 + w2)


def hllc(left, right, normal):
    n = 1 + normal

    def side(x):
        rho = jnp.exp(x[0])
        g = jnp.exp(0.5 * (x[4] - x[0]))
        h = g * g
        return rho, h, rho * h, (HEAT_RATIO**0.5) * g, x[n]

    rho_l, h_l, p_l, c_l, u_l = side(left)
    rho_r, h_r, p_r, c_r, u_r = side(right)
    s_l = jnp.minimum(u_l - c_l, u_r - c_r)
    s_r = jnp.maximum(u_l + c_l, u_r + c_r)
    m_l = rho_l * (s_l - u_l)
    m_r = rho_r * (s_r - u_r)
    s = (p_r - p_l + u_l * m_l - u_r * m_r) / (m_l - m_r)
    use_l = (s >= 0) | (s_l >= 0)
    pick = [jnp.where(use_l, a, b) for a, b in zip(left, right)]
    rho = jnp.where(use_l, rho_l, rho_r)
    h = jnp.where(use_l, h_l, h_r)
    p = jnp.where(use_l, p_l, p_r)
    wave = jnp.where(use_l, s_l, s_r)
    act = jnp.where(use_l, jnp.minimum(s_l, 0.0), jnp.maximum(s_r, 0.0))
    u = pick[n]
    rel = s - u
    ratio = rel / (wave - s)
    mass = rho * (u + act * ratio)
    k = rho * act * (1.0 + ratio) * rel
    square = pick[1] * pick[1] + pick[2] * pick[2] + pick[3] * pick[3]
    enthalpy = (1.0 / (HEAT_RATIO - 1.0) + 1.0) * h + 0.5 * square
    flux = [mass * x for x in pick]
    flux[0] = mass
    flux[n] = flux[n] + (p + k)
    flux[4] = enthalpy * mass + k * s
    return flux


def rows8(index):
    return pl.ds(pl.multiple_of(index * 8, 8), 8)


def face_states(load_line, left_ref, right_ref, faces):
    def one(c, carry):
        upper, lower = weno_line(load_line(c))
        for f in range(faces):
            left_ref[rows8(c * faces + f), :] = upper[f + 2]
            right_ref[rows8(c * faces + f), :] = lower[f + 3]
        return carry

    lax.fori_loop(0, COMPS, one, 0)


def line_changes(left_ref, right_ref, faces, normal, emit):
    before = None
    for f in range(faces):
        left = [left_ref[pl.ds((c * faces + f) * 8, 8), :] for c in range(COMPS)]
        right = [right_ref[pl.ds((c * faces + f) * 8, 8), :] for c in range(COMPS)]
        flux = hllc(left, right, normal)
        if before is not None:
            for c in range(COMPS):
                emit(c, f - 1, flux[c] - before[c])
        before = flux


def half_lanes(shape):
    return lax.broadcasted_iota(jnp.int32, shape, 1) < 64


def swap_halves(x):
    return pltpu.roll(x, 64, 1)


def pack_kernel(pair_x, flags, f_ref, map_ref, r_ref, zt_ref, *refs):
    refs = list(refs)
    x_refs = [refs.pop(0) for _ in range(1 if pair_x else 2)]
    ylo_ref, yhi_ref, zlo_ref, zhi_ref, table_ref, buf = refs
    planes, ylen = 8, 8
    for x in range(planes):
        def at(c):
            return f_ref[pl.ds(c * 64 + x * 8, 8), :]

        rho = at(0)
        inv = 1.0 / rho
        u = [at(c) * inv for c in (1, 2, 3)]
        p = (HEAT_RATIO - 1.0) * (
            at(4) - 0.5 * rho * (u[0] * u[0] + u[1] * u[1] + u[2] * u[2])
        )
        out = [jnp.log(rho)] + u + [jnp.log(p)] + [at(c) * inv for c in range(5, COMPS)]
        for c in range(COMPS):
            r_ref[pl.ds(c * 64 + x * 8, 8), :] = out[c]
    for c in range(0, COMPS, 2):
        lo = jnp.concatenate([r_ref[pl.ds((c + i) * 64, 24), :] for i in (0, 1)], axis=0)
        hi = jnp.concatenate([r_ref[pl.ds((c + i) * 64 + 40, 24), :] for i in (0, 1)], axis=0)
        if pair_x:
            both = [jnp.where(flags[0] == 1, hi, lo)]
        else:
            both = [lo, hi]
        for ref, x in zip(x_refs, both):
            ref[pl.ds(c * 24, 48), :] = x.astype(BF16)
        def row(i, y):
            return r_ref[pl.ds((c + i) * 64 + y, 8, stride=8), :]

        ylo_ref[pl.ds(c * 24, 48), :] = jnp.concatenate(
            [row(i, y) for i in (0, 1) for y in range(3)], axis=0
        ).astype(BF16)
        yhi_ref[pl.ds(c * 24, 48), :] = jnp.concatenate(
            [row(i, y) for i in (0, 1) for y in range(ylen - 3, ylen)], axis=0
        ).astype(BF16)
    low = half_lanes((64, 128))
    for c in range(0, COMPS, 2):
        t = jnp.transpose(r_ref[pl.ds(c * 64, 128), :])
        top, bottom = t[:64], t[64:]
        even = jnp.where(low, top, swap_halves(bottom))
        odd = jnp.where(low, swap_halves(top), bottom)
        for i, x in ((0, even), (1, odd)):
            zt_ref[pl.ds((c + i) * 64, 64), :] = x
            zlo_ref[pl.ds((c + i) * 3, 3), :] = x[:3]
            zhi_ref[pl.ds((c + i) * 3, 3), :] = x[61:]
    pushes = []
    for wall in range(2):
        rows = (0, 1, 2) if wall == 0 else (ylen - 1, ylen - 2, ylen - 3)
        state = []
        for c in (0, 2, 4):
            a = [r_ref[pl.ds(c * 64 + y, 8, stride=8), :] for y in rows]
            sign = -1.0 if c == 2 else 1.0
            state.append(weno_one([a[2], a[1], a[0], sign * a[0], sign * a[1]]))
        rho = jnp.exp(state[0])
        p = jnp.exp(state[2])
        out_speed = -state[1] if wall == 0 else state[1]
        speed = jnp.abs(out_speed) + jnp.sqrt(HEAT_RATIO * p / rho)
        push = p + rho * out_speed * (out_speed + speed)
        x = jnp.where(flags[2 + wall] == 1, push, 0.0)
        for s in (1, 2, 4):
            x = x + pltpu.roll(x, 128 - s, 1)
        for s in (1, 2):
            x = x + pltpu.roll(x, 8 - s, 0)
        pushes.append(x)
    ids = map_ref[...].astype(F32)
    tall = jnp.concatenate(pushes + [ids, jnp.zeros((96, 128), F32)], axis=0)
    buf[...] = jnp.transpose(tall)
    groups = [buf[pl.ds(64 * g, 8, stride=8), :] for g in range(2)]
    lane = lax.broadcasted_iota(jnp.int32, (8, 128), 1).astype(F32)
    columns = []
    for g in groups:
        for col in (0, 4, 8, 12):
            columns.append(
                (
                    jnp.broadcast_to(g[:, col : col + 1], (8, 128)),
                    jnp.broadcast_to(g[:, 16 + col : 17 + col], (8, 128)),
                )
            )
    for j in range(table_ref.shape[0]):
        total = jnp.zeros((8, 128), F32)
        for load, panel in columns:
            total = total + jnp.where(panel == lane + 128.0 * j, load, 0.0)
        table_ref[pl.ds(j, 1), :] = jnp.sum(total, axis=0, keepdims=True)


def pack(fields, panels, flags, pair_x, table_rows):
    halo = jax.ShapeDtypeStruct((COMPS * 24, 128), BF16)
    edge = jax.ShapeDtypeStruct((COMPS * 3, 128), F32)
    whole = jax.ShapeDtypeStruct((COMPS * 64, 128), F32)
    outs = [whole, whole] + [halo] * (1 if pair_x else 2) + [halo, halo, edge, edge]
    outs.append(jax.ShapeDtypeStruct((table_rows, 128), F32))
    return pl.pallas_call(
        lambda *a: pack_kernel(pair_x, *a),
        out_shape=outs,
        in_specs=[SM, VM, VM],
        out_specs=[VM] * len(outs),
        scratch_shapes=[pltpu.VMEM((128, 128), F32)],
        name="pack",
    )(flags, fields, panels)


def chem_kernel(slots, r_ref, react_ref, w1_ref, w2_ref, w3_ref, w4_ref, out_ref):
    def dot(a, b):
        return jnp.dot(a, b, preferred_element_type=F32)

    def iota(shape, dim):
        return lax.broadcasted_iota(jnp.int32, shape, dim)

    def where1(mask):
        return jnp.where(mask, 1.0, 0.0).astype(BF16)

    react = react_ref[...].astype(F32)
    react_b = react.astype(BF16)
    upper = where1(iota((128, 128), 0) <= iota((128, 128), 1))
    within = dot(react_b, upper)
    count = dot(react_b, jnp.ones((128, 128), BF16))
    below = where1(iota((64, 64), 1) < iota((64, 64), 0))
    offset = dot(below, count.astype(BF16))
    rank = (react * (within + offset)).astype(BF16)
    slot_lane = iota((64, slots), 1).astype(F32)
    off_col, cnt_col = offset[:, :1], count[:, :1]
    row_slot = where1((slot_lane >= off_col) & (slot_lane < off_col + cnt_col))
    nt = (((1,), (1,)), ((), ()))
    count_row = lax.dot_general(
        jnp.ones((8, 128), BF16), react_b, nt, preferred_element_type=F32
    )
    offset_row = lax.dot_general(
        count_row.astype(BF16), below, nt, preferred_element_type=F32
    )
    slot_sub = iota((slots, 64), 0).astype(F32)
    slot_row = where1(
        (slot_sub >= offset_row[:1]) & (slot_sub < offset_row[:1] + count_row[:1])
    )
    lane_hit = dot(slot_row, rank) == iota((slots, 128), 0).astype(F32) + 1.0
    feat = jnp.zeros((slots, 128), F32)
    for c in range(COMPS):
        rows = dot(slot_row, r_ref[pl.ds(c * 64, 64), :].astype(BF16))
        hit = jnp.where(lane_hit, rows, 0.0).astype(BF16)
        feat = feat + dot(hit, where1(iota((128, 128), 1) == c))
    h = jnp.transpose(feat)[:COMPS].astype(BF16)
    for w_ref in (w1_ref, w2_ref, w3_ref):
        h = jax.nn.gelu(dot(w_ref[...], h)).astype(BF16)
    rates = dot(w4_ref[...], h)
    rates = jnp.concatenate([rates, jnp.zeros((128 - COMPS, slots), F32)], axis=0)
    rates_t = jnp.transpose(rates).astype(BF16)
    for c in range(COMPS):
        spread = dot(rates_t, where1(iota((128, 128), 0) == c))
        spread = jnp.where(lane_hit, spread, 0.0).astype(BF16)
        out_ref[pl.ds(c * 64, 64), :] = dot(row_slot, spread)


def chem(recon, react, layers, slots):
    return pl.pallas_call(
        lambda *a: chem_kernel(slots, *a),
        out_shape=jax.ShapeDtypeStruct(recon.shape, F32),
        in_specs=[VM] * 6,
        out_specs=VM,
        name="chem",
    )(recon, react, *layers)


def halo_lines(ref, scratch, own, sign_comp, at_wall, order):
    for c in range(0, COMPS, 2):
        block = ref[pl.ds(c * 24, 48), :].astype(F32)
        for i in (0, 1):
            for k in range(3):
                mirror = own(c + i, order[k])
                if c + i == sign_comp:
                    mirror = -mirror
                got = block[(i * 3 + k) * 8 : (i * 3 + k + 1) * 8]
                scratch[pl.ds(((c + i) * 3 + k) * 8, 8), :] = jnp.where(at_wall, mirror, got)


def flux_x_kernel(flags, r_ref, lo_ref, hi_ref, out_ref, lo_s, hi_s, left, right):
    def own(c, x):
        return r_ref[pl.ds(c * 64 + x * 8, 8), :]

    halo_lines(lo_ref, lo_s, own, 1, flags[0] == 1, (2, 1, 0))
    halo_lines(hi_ref, hi_s, own, 1, flags[1] == 1, (7, 6, 5))

    def line(c):
        return (
            [lo_s[rows8(c * 3 + k), :] for k in range(3)]
            + [r_ref[rows8(c * 8 + x), :] for x in range(8)]
            + [hi_s[rows8(c * 3 + k), :] for k in range(3)]
        )

    face_states(line, left, right, 9)

    def emit(c, x, change):
        out_ref[pl.ds(c * 64 + x * 8, 8), :] = change

    line_changes(left, right, 9, 0, emit)


def flux_y_kernel(flags, r_ref, lo_ref, hi_ref, acc_ref, out_ref, lo_s, hi_s, left, right):
    def own(c, y):
        return r_ref[pl.ds(c * 64 + y, 8, stride=8), :]

    halo_lines(lo_ref, lo_s, own, 2, flags[2] == 1, (2, 1, 0))
    halo_lines(hi_ref, hi_s, own, 2, flags[3] == 1, (7, 6, 5))

    def line(c):
        return (
            [lo_s[rows8(c * 3 + k), :] for k in range(3)]
            + [r_ref[pl.ds(c * 64 + y, 8, stride=8), :] for y in range(8)]
            + [hi_s[rows8(c * 3 + k), :] for k in range(3)]
        )

    face_states(line, left, right, 9)

    def emit(c, y, change):
        at = pl.ds(c * 64 + y, 8, stride=8)
        out_ref[at, :] = acc_ref[at, :] + change

    line_changes(left, right, 9, 1, emit)


def flux_z_kernel(
    flags, f_ref, zt_ref, lo_ref, hi_ref, acc_ref, src_ref, out_ref, ext, left, right, back
):
    low3, low = half_lanes((3, 128)), half_lanes((64, 128))
    for c in range(COMPS):
        sign = -1.0 if c == 3 else 1.0
        own = zt_ref[pl.ds(c * 64, 64), :]
        first, last = own[:3], own[61:]
        mirror_lo = sign * jnp.concatenate([first[2:3], first[1:2], first[0:1]], axis=0)
        mirror_hi = sign * jnp.concatenate([last[2:3], last[1:2], last[0:1]], axis=0)
        below = jnp.where(flags[4] == 1, mirror_lo, swap_halves(lo_ref[pl.ds(c * 3, 3), :]))
        above = jnp.where(flags[5] == 1, mirror_hi, swap_halves(hi_ref[pl.ds(c * 3, 3), :]))
        ext[pl.ds(c * 72, 3), :] = jnp.where(low3, below, swap_halves(last))
        ext[pl.ds(c * 72 + 3, 64), :] = own
        ext[pl.ds(c * 72 + 67, 3), :] = jnp.where(low3, swap_halves(first), above)

    def line(c):
        return [ext[pl.ds(c * 72 + e, 8, stride=8), :] for e in range(14)]

    face_states(line, left, right, 9)

    def emit(c, z, change):
        back[pl.ds(c * 64 + z, 8, stride=8), :] = change

    line_changes(left, right, 9, 2, emit)
    for c in range(0, COMPS, 2):
        even, odd = back[pl.ds(c * 64, 64), :], back[pl.ds(c * 64 + 64, 64), :]
        t = jnp.concatenate(
            [jnp.where(low, even, swap_halves(odd)), jnp.where(low, swap_halves(even), odd)],
            axis=0,
        )
        at = pl.ds(c * 64, 128)
        change = acc_ref[at, :] + jnp.transpose(t)
        out_ref[at, :] = f_ref[at, :] - TIME_STEP * change + CHEM_STEP * src_ref[at, :]


def state_scratch():
    return [pltpu.VMEM((COMPS * 9 * 8, 128), F32)] * 2


def halo_scratch():
    return [pltpu.VMEM((COMPS * 24, 128), F32)] * 2


def flux_x(flags, recon, lo, hi):
    return pl.pallas_call(
        flux_x_kernel,
        out_shape=jax.ShapeDtypeStruct(recon.shape, F32),
        in_specs=[SM] + [VM] * 3,
        out_specs=VM,
        scratch_shapes=halo_scratch() + state_scratch(),
        name="flux_x",
    )(flags, recon, lo, hi)


def flux_y(flags, recon, lo, hi, acc):
    return pl.pallas_call(
        flux_y_kernel,
        out_shape=jax.ShapeDtypeStruct(recon.shape, F32),
        in_specs=[SM] + [VM] * 4,
        out_specs=VM,
        scratch_shapes=halo_scratch() + state_scratch(),
        name="flux_y",
    )(flags, recon, lo, hi, acc)


def flux_z(flags, fields, turned, lo, hi, acc, source):
    return pl.pallas_call(
        flux_z_kernel,
        out_shape=jax.ShapeDtypeStruct(fields.shape, F32),
        in_specs=[SM] + [VM] * 6,
        out_specs=VM,
        scratch_shapes=[pltpu.VMEM((COMPS * 72, 128), F32)]
        + state_scratch()
        + [pltpu.VMEM(fields.shape, F32)],
        name="flux_z",
    )(flags, fields, turned, lo, hi, acc, source)


def sum_over(table, axis):
    size = lax.axis_size(axis)
    if size & (size - 1):
        return lax.psum(table, axis)
    step = 1
    while step < size:
        table = table + lax.ppermute(table, axis, [(i, i ^ step) for i in range(size)])
        step *= 2
    return table


def body(fields, reacting, panel_map, layer_one, layer_two, layer_three, layer_four):
    shape = fields.shape
    sizes = [lax.axis_size(a) for a in AXES]
    index = [lax.axis_index(a) for a in AXES]
    flags = jnp.stack(
        [f.astype(jnp.int32) for i, n in zip(index, sizes) for f in (i == 0, i == n - 1)]
    )
    pair_x = sizes[0] == 2
    panels_all = 2 * (shape[1] * sizes[0] // PATCH) * (shape[3] * sizes[2] // PATCH)
    flat = fields.reshape(-1, shape[3])
    packed = pack(flat, panel_map.reshape(-1, shape[3]), flags, pair_x, panels_all // 128)
    recon, turned = packed[:2]
    y_lo, y_hi, z_lo, z_hi, table = packed[-5:]

    def move(x, axis, up):
        n = lax.axis_size(axis)
        pairs = [(i, i + 1) if up else (i + 1, i) for i in range(n - 1)]
        return lax.ppermute(x, axis, pairs)

    if pair_x:
        x_below = x_above = lax.ppermute(packed[2], "gx", [(0, 1), (1, 0)])
    else:
        x_below, x_above = move(packed[3], "gx", True), move(packed[2], "gx", False)
    y_below, y_above = move(y_hi, "gy", True), move(y_lo, "gy", False)
    z_below, z_above = move(z_hi, "gz", True), move(z_lo, "gz", False)
    layers = (layer_one, layer_two, layer_three, layer_four)
    slots = BAL * min(4, sizes[0])
    source = chem(recon, reacting.reshape(-1, shape[3]), layers, slots)
    acc = flux_x(flags, recon, x_below, x_above)
    acc = flux_y(flags, recon, y_below, y_above, acc)
    new = flux_z(flags, flat, turned, z_below, z_above, acc, source)
    for axis in ("gx", "gz", "gy"):
        table = sum_over(table, axis)
    own = panels_all // (sizes[0] * sizes[1] * sizes[2])
    place = (index[0] * sizes[1] + index[1]) * sizes[2] + index[2]
    result = lax.dynamic_slice_in_dim(table.reshape(-1), place * own, own)
    return new.reshape(shape), result / float(PATCH * PATCH)


def solution(mesh):
    return jax.shard_map(
        body,
        mesh=mesh,
        in_specs=(
            P(None, "gx", "gy", "gz"),
            P("gx", "gy", "gz"),
            P(None, "gx", "gz"),
            P(),
            P(),
            P(),
            P(),
        ),
        out_specs=(P(None, "gx", "gy", "gz"), P(("gx", "gy", "gz"))),
        check_vma=False,
    )
```

```python
import jax
import jax.numpy as jnp
from jax import lax
from jax.experimental import pallas as pl
from jax.experimental.pallas import tpu as pltpu
from jax.sharding import PartitionSpec as P

BAL = 64
COMPS = 12
PATCH = 8

HEAT_RATIO = 1.4
TIME_STEP = 0.1
CHEM_STEP = 0.25
WENO_EPS = 1e-06
EPS = WENO_EPS * 4.0 / 36.0
AXES = ("gx", "gy", "gz")
F32 = jnp.float32
BF16 = jnp.bfloat16
GRANT = pltpu.CompilerParams(vmem_limit_bytes=12 * 2**20)
VM = pl.BlockSpec(memory_space=pltpu.VMEM)
SM = pl.BlockSpec(memory_space=pltpu.SMEM)
ANY = pl.BlockSpec(memory_space=pl.ANY)


def weno_line(v):
    n = len(v)
    d = [(v[j + 1] - v[j]) * (1.0 / 6.0) for j in range(n - 1)]
    d3 = [3.0 * x for x in d]
    q = {}
    for e in range(1, n - 1):
        s = d[e] - d[e - 1]
        q[e] = (13.0 / 3.0) * (s * s) + EPS
    upper, lower = {}, {}
    for e in range(2, n - 2):
        dm, dp = d[e - 1], d[e]
        t0 = d3[e - 1] - d[e - 2]
        t1 = dm + dp
        t2 = d3[e] - d[e + 1]
        b0 = q[e - 1] + t0 * t0
        b1 = q[e] + t1 * t1
        b2 = q[e + 1] + t2 * t2
        m01, m02, m12 = b0 * b1, b0 * b2, b1 * b2
        s01, s02, s12 = m01 * m01, m02 * m02, m12 * m12
        w1, w01, w12 = 6.0 * s02, 3.0 * s01, 3.0 * s12
        if e < n - 3:
            num = s12 * (t0 + t0 - dm) + w1 * (t1 + dp) + w01 * (t2 + dp)
            upper[e] = v[e] + num / (s12 + w1 + w01)
        if e > 2:
            num = s01 * (t2 + t2 - dp) + w1 * (t1 + dm) + w12 * (t0 + dm)
            lower[e] = v[e] - num / (s01 + w1 + w12)
    return upper, lower


def weno_one(v):
    d = [(v[j + 1] - v[j]) * (1.0 / 6.0) for j in range(4)]
    s = [d[j + 1] - d[j] for j in range(3)]
    q = [(13.0 / 3.0) * (x * x) + EPS for x in s]
    dm, dp = d[1], d[2]
    t0, t1, t2 = 3.0 * dm - d[0], dm + dp, 3.0 * dp - d[3]
    b0, b1, b2 = q[0] + t0 * t0, q[1] + t1 * t1, q[2] + t2 * t2
    m01, m02, m12 = b0 * b1, b0 * b2, b1 * b2
    w0, w1, w2 = m12 * m12, 6.0 * (m02 * m02), 3.0 * (m01 * m01)
    num = w0 * (t0 + t0 - dm) + w1 * (t1 + dp) + w2 * (t2 + dp)
    return v[2] + num / (w0 + w1 + w2)


def hllc(left, right, normal):
    n = 1 + normal

    def side(x):
        rho = jnp.exp(x[0])
        g = jnp.exp(0.5 * (x[4] - x[0]))
        h = g * g
        return rho, h, rho * h, (HEAT_RATIO**0.5) * g, x[n]

    rho_l, h_l, p_l, c_l, u_l = side(left)
    rho_r, h_r, p_r, c_r, u_r = side(right)
    s_l = jnp.minimum(u_l - c_l, u_r - c_r)
    s_r = jnp.maximum(u_l + c_l, u_r + c_r)
    m_l = rho_l * (s_l - u_l)
    m_r = rho_r * (s_r - u_r)
    s = (p_r - p_l + u_l * m_l - u_r * m_r) / (m_l - m_r)
    use_l = (s >= 0) | (s_l >= 0)
    pick = [jnp.where(use_l, a, b) for a, b in zip(left, right)]
    rho = jnp.where(use_l, rho_l, rho_r)
    h = jnp.where(use_l, h_l, h_r)
    p = jnp.where(use_l, p_l, p_r)
    wave = jnp.where(use_l, s_l, s_r)
    act = jnp.where(use_l, jnp.minimum(s_l, 0.0), jnp.maximum(s_r, 0.0))
    u = pick[n]
    rel = s - u
    ratio = rel / (wave - s)
    mass = rho * (u + act * ratio)
    k = rho * act * (1.0 + ratio) * rel
    square = pick[1] * pick[1] + pick[2] * pick[2] + pick[3] * pick[3]
    enthalpy = (1.0 / (HEAT_RATIO - 1.0) + 1.0) * h + 0.5 * square
    flux = [mass * x for x in pick]
    flux[0] = mass
    flux[n] = flux[n] + (p + k)
    flux[4] = enthalpy * mass + k * s
    return flux


def rows8(index):
    return pl.ds(pl.multiple_of(index * 8, 8), 8)


def face_states(load_line, left_ref, right_ref, faces):
    def one(c, carry):
        upper, lower = weno_line(load_line(c))
        for f in range(faces):
            left_ref[rows8(c * faces + f), :] = upper[f + 2]
            right_ref[rows8(c * faces + f), :] = lower[f + 3]
        return carry

    lax.fori_loop(0, COMPS, one, 0)


def line_changes(left_ref, right_ref, faces, normal, emit):
    before = None
    for f in range(faces):
        left = [left_ref[pl.ds((c * faces + f) * 8, 8), :] for c in range(COMPS)]
        right = [right_ref[pl.ds((c * faces + f) * 8, 8), :] for c in range(COMPS)]
        flux = hllc(left, right, normal)
        if before is not None:
            for c in range(COMPS):
                emit(c, f - 1, flux[c] - before[c])
        before = flux


def half_lanes(shape):
    return lax.broadcasted_iota(jnp.int32, shape, 1) < 64


def swap_halves(x):
    return pltpu.roll(x, 64, 1)


def split3(x):
    hi = x.astype(BF16).astype(F32)
    mid = (x - hi).astype(BF16).astype(F32)
    return hi, mid, x - hi - mid


def pack_kernel(pair_x, flags, f_hbm, map_hbm, r_ref, zt_ref, *refs):
    x_refs, refs = refs[:2 - pair_x], refs[2 - pair_x :]
    y_refs, z_refs, table_ref, buf, f_ref, map_ref, sems = refs[:2], refs[2:4], *refs[4:]
    copies = [
        pltpu.make_async_copy(f_hbm, f_ref, sems.at[0]),
        pltpu.make_async_copy(map_hbm, map_ref, sems.at[1]),
    ]
    for copy in copies:
        copy.start()
    copies[0].wait()
    for x in range(8):
        def at(c):
            return f_ref[pl.ds(c * 64 + x * 8, 8), :]

        rho = at(0)
        inv = 1.0 / rho
        u = [at(c) * inv for c in (1, 2, 3)]
        p = (HEAT_RATIO - 1.0) * (
            at(4) - 0.5 * rho * (u[0] * u[0] + u[1] * u[1] + u[2] * u[2])
        )
        out = [jnp.log(rho)] + u + [jnp.log(p)] + [at(c) * inv for c in range(5, COMPS)]
        for c in range(COMPS):
            r_ref[pl.ds(c * 64 + x * 8, 8), :] = out[c]
    pushes = []
    for wall in range(2):
        rows = (0, 1, 2) if wall == 0 else (7, 6, 5)
        state = []
        for c in (0, 2, 4):
            a = [r_ref[pl.ds(c * 64 + y, 8, stride=8), :] for y in rows]
            sign = -1.0 if c == 2 else 1.0
            state.append(weno_one([a[2], a[1], a[0], sign * a[0], sign * a[1]]))
        rho = jnp.exp(state[0])
        p = jnp.exp(state[2])
        out_speed = -state[1] if wall == 0 else state[1]
        speed = jnp.abs(out_speed) + jnp.sqrt(HEAT_RATIO * p / rho)
        push = p + rho * out_speed * (out_speed + speed)
        x = jnp.where(flags[2 + wall] == 1, push, 0.0)
        for s in (1, 2, 4):
            x = x + pltpu.roll(x, 128 - s, 1)
        for s in (1, 2):
            x = x + pltpu.roll(x, 8 - s, 0)
        pushes.append(x)
    copies[1].wait()
    ids = map_ref[...].astype(F32)
    tall = jnp.concatenate(pushes + [ids, jnp.zeros((96, 128), F32)], axis=0)
    buf[...] = jnp.transpose(tall)
    groups = [buf[pl.ds(64 * g, 8, stride=8), :] for g in range(2)]
    lane = lax.broadcasted_iota(jnp.int32, (8, 128), 1).astype(F32)
    columns = []
    for g in groups:
        for col in (0, 4, 8, 12):
            columns.append(
                (
                    jnp.broadcast_to(g[:, col : col + 1], (8, 128)),
                    jnp.broadcast_to(g[:, 16 + col : 17 + col], (8, 128)),
                )
            )
    table = []
    for j in range(table_ref.shape[0]):
        total = jnp.zeros((8, 128), F32)
        for load, panel in columns:
            total = total + jnp.where(panel == lane + 128.0 * j, load, 0.0)
        table.append(jnp.sum(total, axis=0, keepdims=True))
        table_ref[pl.ds(j, 1), :] = table[j]
    for c in range(0, COMPS, 2):
        def row(i, y):
            return r_ref[pl.ds((c + i) * 64 + y, 8, stride=8), :]

        lo = jnp.concatenate([r_ref[pl.ds((c + i) * 64, 24), :] for i in (0, 1)], axis=0)
        hi = jnp.concatenate([r_ref[pl.ds((c + i) * 64 + 40, 24), :] for i in (0, 1)], axis=0)
        store_layers(x_refs, c, lo, hi, flags[6])
        lo = jnp.concatenate([row(i, y) for i in (0, 1) for y in range(3)], axis=0)
        hi = jnp.concatenate([row(i, y) for i in (0, 1) for y in range(5, 8)], axis=0)
        store_layers(y_refs, c, lo, hi, flags[7])
    for ref in (*x_refs, *y_refs):
        rows = ref.shape[0] - COMPS * 24
        if rows:
            pieces = [piece[j] for piece in zip(*map(split3, table)) for j in range(len(table))]
            if rows > len(pieces):
                pieces.append(jnp.zeros((rows - len(pieces), 128), F32))
            ref[pl.ds(COMPS * 24, rows), :] = jnp.concatenate(pieces, axis=0).astype(BF16)
    low = half_lanes((64, 128))
    for c in range(0, COMPS, 2):
        t = jnp.transpose(r_ref[pl.ds(c * 64, 128), :])
        top, bottom = t[:64], t[64:]
        even = jnp.where(low, top, swap_halves(bottom))
        odd = jnp.where(low, swap_halves(top), bottom)
        for i, x in ((0, even), (1, odd)):
            zt_ref[pl.ds((c + i) * 64, 64), :] = x
            for m, ref in enumerate(z_refs):
                up = flags[8] == m
                ref[pl.ds((c + i) * 3, 3), :] = jnp.where(up, x[61:], x[:3])
    for ref in z_refs:
        rows = ref.shape[0] - COMPS * 3
        ref[pl.ds(COMPS * 3, rows), :] = jnp.zeros((rows, 128), F32)


def store_layers(refs, c, lo, hi, parity):
    for m, ref in enumerate(refs):
        ref[pl.ds(c * 24, 48), :] = jnp.where(parity == m, hi, lo).astype(BF16)


def pack(fields, panels, flags, pair_x, table_rows):
    load_rows = -(-3 * table_rows // 16) * 16
    layer_x = jax.ShapeDtypeStruct((COMPS * 24 + (load_rows if pair_x else 0), 128), BF16)
    layer_y = jax.ShapeDtypeStruct((COMPS * 24 + load_rows, 128), BF16)
    edge = jax.ShapeDtypeStruct((40 + -(-table_rows // 8) * 8, 128), F32)
    whole = jax.ShapeDtypeStruct((COMPS * 64, 128), F32)
    outs = [whole, whole] + [layer_x] * (2 - pair_x) + [layer_y] * 2 + [edge] * 2
    outs.append(jax.ShapeDtypeStruct((table_rows, 128), F32))
    return pl.pallas_call(
        lambda *a: pack_kernel(int(pair_x), *a),
        out_shape=outs,
        in_specs=[SM, ANY, ANY],
        out_specs=[VM] * len(outs),
        scratch_shapes=[
            pltpu.VMEM((128, 128), F32),
            pltpu.VMEM(fields.shape, F32),
            pltpu.VMEM(panels.shape, jnp.int32),
            pltpu.SemaphoreType.DMA((2,)),
        ],
        compiler_params=GRANT,
        cost_estimate=cost(2),
        name="pack",
    )(flags, fields, panels)


def cost(us):
    return pl.CostEstimate(flops=0, transcendentals=0, bytes_accessed=int(us * 3.5e6))


def dot(a, b):
    return jnp.dot(a, b, preferred_element_type=F32)


def iota(shape, dim):
    return lax.broadcasted_iota(jnp.int32, shape, dim)


def where1(mask):
    return jnp.where(mask, 1.0, 0.0).astype(BF16)


def chem_in_kernel(slots, r_ref, react_ref, w1_ref, h_ref, row_ref, hit_ref):
    react = react_ref[...].astype(F32)
    react_b = react.astype(BF16)
    upper = where1(iota((128, 128), 0) <= iota((128, 128), 1))
    within = dot(react_b, upper)
    count = dot(react_b, jnp.ones((128, 128), BF16))
    below = where1(iota((64, 64), 1) < iota((64, 64), 0))
    offset = dot(below, count.astype(BF16))
    rank = (react * (within + offset)).astype(BF16)
    slot_lane = iota((64, slots), 1).astype(F32)
    off_col, cnt_col = offset[:, :1], count[:, :1]
    row_ref[...] = where1((slot_lane >= off_col) & (slot_lane < off_col + cnt_col))
    nt = (((1,), (1,)), ((), ()))
    count_row = lax.dot_general(
        jnp.ones((8, 128), BF16), react_b, nt, preferred_element_type=F32
    )
    offset_row = lax.dot_general(
        count_row.astype(BF16), below, nt, preferred_element_type=F32
    )
    slot_sub = iota((slots, 64), 0).astype(F32)
    slot_row = where1(
        (slot_sub >= offset_row[:1]) & (slot_sub < offset_row[:1] + count_row[:1])
    )
    lane_hit = dot(slot_row, rank) == iota((slots, 128), 0).astype(F32) + 1.0
    hit_ref[...] = where1(lane_hit)
    feat = jnp.zeros((slots, 128), F32)
    for c in range(COMPS):
        rows = dot(slot_row, r_ref[pl.ds(c * 64, 64), :].astype(BF16))
        hit = jnp.where(lane_hit, rows, 0.0).astype(BF16)
        feat = feat + dot(hit, where1(iota((128, 128), 1) == c))
    feat = jnp.transpose(feat)[:COMPS].astype(BF16)
    tn = (((0,), (0,)), ((), ()))
    one = lax.dot_general(w1_ref[...], feat, tn, preferred_element_type=F32)
    h_ref[...] = jax.nn.gelu(one).astype(BF16)


def chem_in(recon, react, layer_one, slots):
    return pl.pallas_call(
        lambda *a: chem_in_kernel(slots, *a),
        out_shape=[
            jax.ShapeDtypeStruct((layer_one.shape[1], slots), BF16),
            jax.ShapeDtypeStruct((64, slots), BF16),
            jax.ShapeDtypeStruct((slots, 128), BF16),
        ],
        in_specs=[VM] * 3,
        out_specs=[VM] * 3,
        compiler_params=GRANT,
        cost_estimate=cost(2),
        name="chem_in",
    )(recon, react, layer_one)


def chem_mid_kernel(h_ref, w2_ref, w3_ref, out_ref):
    two = jax.nn.gelu(dot(w2_ref[...], h_ref[...])).astype(BF16)
    out_ref[...] = jax.nn.gelu(dot(w3_ref[...], two)).astype(BF16)


def chem_mid(hidden, layer_two, layer_three):
    return pl.pallas_call(
        chem_mid_kernel,
        out_shape=jax.ShapeDtypeStruct((layer_three.shape[0], hidden.shape[1]), BF16),
        in_specs=[VM] * 3,
        out_specs=VM,
        compiler_params=GRANT,
        cost_estimate=cost(2),
        name="chem_mid",
    )(hidden, layer_two, layer_three)


def chem_out_kernel(h_ref, w4_ref, row_ref, hit_ref, out_ref):
    rates = dot(w4_ref[...], h_ref[...])
    slots = rates.shape[1]
    rates = jnp.concatenate([rates, jnp.zeros((128 - COMPS, slots), F32)], axis=0)
    rates_t = jnp.transpose(rates).astype(BF16)
    hit, row_slot = hit_ref[...].astype(F32), row_ref[...]
    for c in range(COMPS):
        spread = hit * dot(rates_t, where1(iota((128, 128), 0) == c))
        out_ref[pl.ds(c * 64, 64), :] = dot(row_slot, spread.astype(BF16))


def chem_out(hidden, layer_four, row_slot, hit):
    return pl.pallas_call(
        chem_out_kernel,
        out_shape=jax.ShapeDtypeStruct((COMPS * 64, 128), F32),
        in_specs=[VM] * 4,
        out_specs=VM,
        compiler_params=GRANT,
        cost_estimate=cost(2),
        name="chem_out",
    )(hidden, layer_four, row_slot, hit)


def halo_lines(refs, scratch, own, sign_comp, at_wall, order, second):
    for c in range(0, COMPS, 2):
        block = refs[0][pl.ds(c * 24, 48), :].astype(F32)
        if len(refs) == 2:
            block = jnp.where(second, refs[1][pl.ds(c * 24, 48), :].astype(F32), block)
        for i in (0, 1):
            for k in range(3):
                mirror = own(c + i, order[k])
                if c + i == sign_comp:
                    mirror = -mirror
                got = block[(i * 3 + k) * 8 : (i * 3 + k + 1) * 8]
                scratch[pl.ds(((c + i) * 3 + k) * 8, 8), :] = jnp.where(at_wall, mirror, got)


def flux_x_kernel(count, flags, r_ref, *refs):
    layers, (out_ref, token, lo_s, hi_s, left, right) = refs[:count], refs[count:]

    def own(c, x):
        return r_ref[pl.ds(c * 64 + x * 8, 8), :]

    halo_lines(layers, lo_s, own, 1, flags[0] == 1, (2, 1, 0), flags[6] == 0)
    halo_lines(layers, hi_s, own, 1, flags[1] == 1, (7, 6, 5), flags[6] == 1)

    def line(c):
        return (
            [lo_s[rows8(c * 3 + k), :] for k in range(3)]
            + [r_ref[rows8(c * 8 + x), :] for x in range(8)]
            + [hi_s[rows8(c * 3 + k), :] for k in range(3)]
        )

    face_states(line, left, right, 9)

    def emit(c, x, change):
        out_ref[pl.ds(c * 64 + x * 8, 8), :] = change

    line_changes(left, right, 9, 0, emit)
    token[...] = jnp.zeros(token.shape, F32)


def flux_y_kernel(
    count, flags, f_hbm, r_ref, acc_ref, src_ref, *refs
):
    layers, (out_ref, lo_s, hi_s, left, right, f_ref, sem) = refs[:count], refs[count:]
    copy = pltpu.make_async_copy(f_hbm, f_ref, sem)
    copy.start()

    def own(c, y):
        return r_ref[pl.ds(c * 64 + y, 8, stride=8), :]

    halo_lines(layers, lo_s, own, 2, flags[2] == 1, (2, 1, 0), flags[7] == 0)
    halo_lines(layers, hi_s, own, 2, flags[3] == 1, (7, 6, 5), flags[7] == 1)

    def line(c):
        return (
            [lo_s[rows8(c * 3 + k), :] for k in range(3)]
            + [r_ref[pl.ds(c * 64 + y, 8, stride=8), :] for y in range(8)]
            + [hi_s[rows8(c * 3 + k), :] for k in range(3)]
        )

    face_states(line, left, right, 9)
    copy.wait()

    def emit(c, y, change):
        at = pl.ds(c * 64 + y, 8, stride=8)
        out_ref[at, :] = (
            f_ref[at, :] - TIME_STEP * (acc_ref[at, :] + change) + CHEM_STEP * src_ref[at, :]
        )

    line_changes(left, right, 9, 1, emit)


def flux_z_kernel(count, flags, zt_ref, acc_ref, *refs):
    layers, (out_ref, token, ext, left, right, back) = refs[:count], refs[count:]
    low3, low = half_lanes((3, 128)), half_lanes((64, 128))

    def got(c, second):
        x = layers[0][pl.ds(c * 3, 3), :]
        if count == 2:
            x = jnp.where(second, layers[1][pl.ds(c * 3, 3), :], x)
        return swap_halves(x)

    for c in range(COMPS):
        sign = -1.0 if c == 3 else 1.0
        own = zt_ref[pl.ds(c * 64, 64), :]
        first, last = own[:3], own[61:]
        mirror_lo = sign * jnp.concatenate([first[2:3], first[1:2], first[0:1]], axis=0)
        mirror_hi = sign * jnp.concatenate([last[2:3], last[1:2], last[0:1]], axis=0)
        below = jnp.where(flags[4] == 1, mirror_lo, got(c, flags[8] == 0))
        above = jnp.where(flags[5] == 1, mirror_hi, got(c, flags[8] == 1))
        ext[pl.ds(c * 72, 3), :] = jnp.where(low3, below, swap_halves(last))
        ext[pl.ds(c * 72 + 3, 64), :] = own
        ext[pl.ds(c * 72 + 67, 3), :] = jnp.where(low3, swap_halves(first), above)

    def line(c):
        return [ext[pl.ds(c * 72 + e, 8, stride=8), :] for e in range(14)]

    face_states(line, left, right, 9)

    def emit(c, z, change):
        back[pl.ds(c * 64 + z, 8, stride=8), :] = change

    line_changes(left, right, 9, 2, emit)
    for c in range(0, COMPS, 2):
        even, odd = back[pl.ds(c * 64, 64), :], back[pl.ds(c * 64 + 64, 64), :]
        t = jnp.concatenate(
            [jnp.where(low, even, swap_halves(odd)), jnp.where(low, swap_halves(even), odd)],
            axis=0,
        )
        at = pl.ds(c * 64, 128)
        out_ref[at, :] = acc_ref[at, :] + jnp.transpose(t)
    token[...] = jnp.zeros(token.shape, F32)


def state_scratch():
    return [pltpu.VMEM((COMPS * 9 * 8, 128), F32)] * 2


def halo_scratch():
    return [pltpu.VMEM((COMPS * 24, 128), F32)] * 2


def token_shape(table):
    return jax.ShapeDtypeStruct(table.shape, F32)


def flux_x(flags, recon, layers, table):
    return pl.pallas_call(
        lambda *a: flux_x_kernel(len(layers), *a),
        out_shape=[jax.ShapeDtypeStruct(recon.shape, F32), token_shape(table)],
        in_specs=[SM] + [VM] * (1 + len(layers)),
        out_specs=[VM] * 2,
        scratch_shapes=halo_scratch() + state_scratch(),
        compiler_params=GRANT,
        cost_estimate=cost(2),
        name="flux_x",
    )(flags, recon, *layers)


def flux_y(flags, fields, recon, acc, source, layers):
    return pl.pallas_call(
        lambda *a: flux_y_kernel(len(layers), *a),
        out_shape=jax.ShapeDtypeStruct(recon.shape, F32),
        in_specs=[SM, ANY] + [VM] * (3 + len(layers)),
        out_specs=VM,
        scratch_shapes=halo_scratch()
        + state_scratch()
        + [pltpu.VMEM(fields.shape, F32), pltpu.SemaphoreType.DMA],
        compiler_params=GRANT,
        cost_estimate=cost(2),
        name="flux_y",
    )(flags, fields, recon, acc, source, *layers)


def flux_z(flags, turned, acc, layers, table):
    return pl.pallas_call(
        lambda *a: flux_z_kernel(len(layers), *a),
        out_shape=[jax.ShapeDtypeStruct(acc.shape, F32), token_shape(table)],
        in_specs=[SM] + [VM] * (2 + len(layers)),
        out_specs=[VM] * 2,
        scratch_shapes=[pltpu.VMEM((COMPS * 72, 128), F32)]
        + state_scratch()
        + [pltpu.VMEM(acc.shape, F32)],
        compiler_params=GRANT,
        cost_estimate=cost(3),
        name="flux_z",
    )(flags, turned, acc, *layers)


def swap(x, axis, second):
    n = lax.axis_size(axis)
    pairs = [(i, i + 1) for i in range(int(second), n - 1, 2)]
    if second and n == 4:
        pairs.append((0, n - 1))
    return lax.ppermute(x, axis, [(a, b) for a, b in pairs] + [(b, a) for a, b in pairs])


def sum_over(table, axis):
    size = lax.axis_size(axis)
    if size & (size - 1):
        return lax.psum(table, axis)
    step = 1
    while step < size:
        table = table + lax.ppermute(table, axis, [(i, i ^ step) for i in range(size)])
        step *= 2
    return table


def split_table(table):
    hi = lax.reduce_precision(table, 8, 7)
    mid = lax.reduce_precision(table - hi, 8, 7)
    return jnp.concatenate([hi, mid, table - hi - mid], axis=0).astype(BF16)


def join_table(rows, height):
    rows = rows[: 3 * height].astype(F32)
    return rows[:height] + rows[height : 2 * height] + rows[2 * height :]


def body(fields, reacting, panel_map, layer_one, layer_two, layer_three, layer_four):
    shape = fields.shape
    sizes = [lax.axis_size(a) for a in AXES]
    index = [lax.axis_index(a) for a in AXES]
    flags = [f for i, n in zip(index, sizes) for f in (i == 0, i == n - 1)]
    flags = jnp.stack([f.astype(jnp.int32) for f in flags] + [i % 2 for i in index])
    pair_x = sizes[0] == 2
    panels_all = 2 * (shape[1] * sizes[0] // PATCH) * (shape[3] * sizes[2] // PATCH)
    height = panels_all // 128
    flat = fields.reshape(-1, shape[3])
    packed = pack(flat, panel_map.reshape(-1, shape[3]), flags, pair_x, height)
    recon, turned, table = packed[0], packed[1], packed[-1]
    xs, ys, zs = packed[2:-5], packed[-5:-3], packed[-3:-1]
    slots = BAL * min(4, sizes[0])
    layer_rows, edge_rows = COMPS * 24, 40

    got = [swap(x, "gx", m) for m, x in enumerate(xs)]
    hidden, row_slot, hit = chem_in(recon, reacting.reshape(-1, shape[3]), layer_one.T, slots)
    if pair_x:
        table = table + join_table(got[0][layer_rows:], height)
    else:
        table = sum_over(table, "gx")
    ride_z, ride_y = sizes[2] in (2, 4), sizes[1] in (2, 4)
    if not ride_z:
        table = sum_over(table, "gz")
    z_got = [swap(lax.dynamic_update_slice(zs[0], table, (edge_rows, 0)), "gz", 0)]
    acc, token = flux_x(flags, recon, got, table)
    if ride_z:
        table = table + z_got[0][edge_rows : edge_rows + height] + token
    if sizes[2] > 2:
        z_got.append(swap(lax.dynamic_update_slice(zs[1], table, (edge_rows, 0)), "gz", 1))
        if ride_z:
            table = table + z_got[1][edge_rows : edge_rows + height]
    hidden = chem_mid(hidden, layer_two, layer_three)
    if not ride_y:
        table = sum_over(table, "gy")
    y_got = [swap(lax.dynamic_update_slice(ys[0], split_table(table), (layer_rows, 0)), "gy", 0)]
    acc, token = flux_z(flags, turned, acc, z_got, table)
    if ride_y:
        table = table + join_table(y_got[0][layer_rows:], height) + token
    if sizes[1] > 2:
        y_got.append(
            swap(lax.dynamic_update_slice(ys[1], split_table(table), (layer_rows, 0)), "gy", 1)
        )
        if ride_y:
            table = table + join_table(y_got[1][layer_rows:], height)
    source = chem_out(hidden, layer_four, row_slot, hit)
    new = flux_y(flags, flat, recon, acc, source, y_got)
    own = panels_all // (sizes[0] * sizes[1] * sizes[2])
    place = (index[0] * sizes[1] + index[1]) * sizes[2] + index[2]
    result = lax.dynamic_slice_in_dim(table.reshape(-1), place * own, own)
    return new.reshape(shape), result / float(PATCH * PATCH)


def solution(mesh):
    return jax.shard_map(
        body,
        mesh=mesh,
        in_specs=(
            P(None, "gx", "gy", "gz"),
            P("gx", "gy", "gz"),
            P(None, "gx", "gz"),
            P(),
            P(),
            P(),
            P(),
        ),
        out_specs=(P(None, "gx", "gy", "gz"), P(("gx", "gy", "gz"))),
        check_vma=False,
    )
```

```python
import jax
import jax.numpy as jnp
from jax import lax
from jax.experimental import pallas as pl
from jax.experimental.pallas import tpu as pltpu
from jax.sharding import PartitionSpec as P

BAL = 64
COMPS = 12
PATCH = 8

HEAT_RATIO = 1.4
TIME_STEP = 0.1
CHEM_STEP = 0.25
WENO_EPS = 1e-06
EPS = WENO_EPS * 4.0 / 36.0
AXES = ("gx", "gy", "gz")
F32 = jnp.float32
BF16 = jnp.bfloat16
GRANT = pltpu.CompilerParams(vmem_limit_bytes=12 * 2**20)
VM = pl.BlockSpec(memory_space=pltpu.VMEM)
SM = pl.BlockSpec(memory_space=pltpu.SMEM)
HBM = pl.BlockSpec(memory_space=pltpu.HBM)


def weno_line(v):
    n = len(v)
    d = [(v[j + 1] - v[j]) * (1.0 / 6.0) for j in range(n - 1)]
    d3 = [3.0 * x for x in d]
    q = {}
    for e in range(1, n - 1):
        s = d[e] - d[e - 1]
        q[e] = (13.0 / 3.0) * (s * s) + EPS
    upper, lower = {}, {}
    for e in range(2, n - 2):
        dm, dp = d[e - 1], d[e]
        t0 = d3[e - 1] - d[e - 2]
        t1 = dm + dp
        t2 = d3[e] - d[e + 1]
        b0 = q[e - 1] + t0 * t0
        b1 = q[e] + t1 * t1
        b2 = q[e + 1] + t2 * t2
        m01, m02, m12 = b0 * b1, b0 * b2, b1 * b2
        s01, s02, s12 = m01 * m01, m02 * m02, m12 * m12
        w1, w01, w12 = 6.0 * s02, 3.0 * s01, 3.0 * s12
        if e < n - 3:
            num = s12 * (t0 + t0 - dm) + w1 * (t1 + dp) + w01 * (t2 + dp)
            upper[e] = v[e] + num / (s12 + w1 + w01)
        if e > 2:
            num = s01 * (t2 + t2 - dp) + w1 * (t1 + dm) + w12 * (t0 + dm)
            lower[e] = v[e] - num / (s01 + w1 + w12)
    return upper, lower


def weno_one(v):
    d = [(v[j + 1] - v[j]) * (1.0 / 6.0) for j in range(4)]
    s = [d[j + 1] - d[j] for j in range(3)]
    q = [(13.0 / 3.0) * (x * x) + EPS for x in s]
    dm, dp = d[1], d[2]
    t0, t1, t2 = 3.0 * dm - d[0], dm + dp, 3.0 * dp - d[3]
    b0, b1, b2 = q[0] + t0 * t0, q[1] + t1 * t1, q[2] + t2 * t2
    m01, m02, m12 = b0 * b1, b0 * b2, b1 * b2
    w0, w1, w2 = m12 * m12, 6.0 * (m02 * m02), 3.0 * (m01 * m01)
    num = w0 * (t0 + t0 - dm) + w1 * (t1 + dp) + w2 * (t2 + dp)
    return v[2] + num / (w0 + w1 + w2)


def hllc(left, right, normal):
    n = 1 + normal

    def side(x):
        rho = jnp.exp(x[0])
        g = jnp.exp(0.5 * (x[4] - x[0]))
        h = g * g
        return rho, h, rho * h, (HEAT_RATIO**0.5) * g, x[n]

    rho_l, h_l, p_l, c_l, u_l = side(left)
    rho_r, h_r, p_r, c_r, u_r = side(right)
    s_l = jnp.minimum(u_l - c_l, u_r - c_r)
    s_r = jnp.maximum(u_l + c_l, u_r + c_r)
    m_l = rho_l * (s_l - u_l)
    m_r = rho_r * (s_r - u_r)
    s = (p_r - p_l + u_l * m_l - u_r * m_r) / (m_l - m_r)
    use_l = (s >= 0) | (s_l >= 0)
    pick = [jnp.where(use_l, a, b) for a, b in zip(left, right)]
    rho = jnp.where(use_l, rho_l, rho_r)
    h = jnp.where(use_l, h_l, h_r)
    p = jnp.where(use_l, p_l, p_r)
    wave = jnp.where(use_l, s_l, s_r)
    act = jnp.where(use_l, jnp.minimum(s_l, 0.0), jnp.maximum(s_r, 0.0))
    u = pick[n]
    rel = s - u
    ratio = rel / (wave - s)
    mass = rho * (u + act * ratio)
    k = rho * act * (1.0 + ratio) * rel
    square = pick[1] * pick[1] + pick[2] * pick[2] + pick[3] * pick[3]
    enthalpy = (1.0 / (HEAT_RATIO - 1.0) + 1.0) * h + 0.5 * square
    flux = [mass * x for x in pick]
    flux[0] = mass
    flux[n] = flux[n] + (p + k)
    flux[4] = enthalpy * mass + k * s
    return flux


def rows8(index):
    return pl.ds(pl.multiple_of(index * 8, 8), 8)


def face_states(load_line, left_ref, right_ref, faces):
    def one(c, carry):
        upper, lower = weno_line(load_line(c))
        for f in range(faces):
            left_ref[rows8(c * faces + f), :] = upper[f + 2]
            right_ref[rows8(c * faces + f), :] = lower[f + 3]
        return carry

    lax.fori_loop(0, COMPS, one, 0)


def line_changes(left_ref, right_ref, faces, normal, emit):
    before = None
    for f in range(faces):
        left = [left_ref[pl.ds((c * faces + f) * 8, 8), :] for c in range(COMPS)]
        right = [right_ref[pl.ds((c * faces + f) * 8, 8), :] for c in range(COMPS)]
        flux = hllc(left, right, normal)
        if before is not None:
            for c in range(COMPS):
                emit(c, f - 1, flux[c] - before[c])
        before = flux


def half_lanes(shape):
    return lax.broadcasted_iota(jnp.int32, shape, 1) < 64


def swap_halves(x):
    return pltpu.roll(x, 64, 1)


def split3(x):
    hi = x.astype(BF16).astype(F32)
    mid = (x - hi).astype(BF16).astype(F32)
    return hi, mid, x - hi - mid


def pack_kernel(flags, f_hbm, map_hbm, f_ref, r_ref, y1_ref, y2_ref, table_ref, buf, map_ref, sems):
    copies = [
        pltpu.make_async_copy(f_hbm, f_ref, sems.at[0]),
        pltpu.make_async_copy(map_hbm, map_ref, sems.at[1]),
    ]
    for copy in copies:
        copy.start()
    copies[0].wait()
    for x in range(8):
        def at(c):
            return f_ref[pl.ds(c * 64 + x * 8, 8), :]

        rho = at(0)
        inv = 1.0 / rho
        u = [at(c) * inv for c in (1, 2, 3)]
        p = (HEAT_RATIO - 1.0) * (
            at(4) - 0.5 * rho * (u[0] * u[0] + u[1] * u[1] + u[2] * u[2])
        )
        out = [jnp.log(rho)] + u + [jnp.log(p)] + [at(c) * inv for c in range(5, COMPS)]
        for c in range(COMPS):
            r_ref[pl.ds(c * 64 + x * 8, 8), :] = out[c]
    pushes = []
    for wall in range(2):
        rows = (0, 1, 2) if wall == 0 else (7, 6, 5)
        state = []
        for c in (0, 2, 4):
            a = [r_ref[pl.ds(c * 64 + y, 8, stride=8), :] for y in rows]
            sign = -1.0 if c == 2 else 1.0
            state.append(weno_one([a[2], a[1], a[0], sign * a[0], sign * a[1]]))
        rho = jnp.exp(state[0])
        p = jnp.exp(state[2])
        out_speed = -state[1] if wall == 0 else state[1]
        speed = jnp.abs(out_speed) + jnp.sqrt(HEAT_RATIO * p / rho)
        push = p + rho * out_speed * (out_speed + speed)
        x = jnp.where(flags[2 + wall] == 1, push, 0.0)
        for s in (1, 2, 4):
            x = x + pltpu.roll(x, 128 - s, 1)
        for s in (1, 2):
            x = x + pltpu.roll(x, 8 - s, 0)
        pushes.append(x)
    copies[1].wait()
    ids = map_ref[...].astype(F32)
    tall = jnp.concatenate(pushes + [ids, jnp.zeros((96, 128), F32)], axis=0)
    buf[...] = jnp.transpose(tall)
    groups = [buf[pl.ds(64 * g, 8, stride=8), :] for g in range(2)]
    lane = lax.broadcasted_iota(jnp.int32, (8, 128), 1).astype(F32)
    columns = []
    for g in groups:
        for col in (0, 4, 8, 12):
            columns.append(
                (
                    jnp.broadcast_to(g[:, col : col + 1], (8, 128)),
                    jnp.broadcast_to(g[:, 16 + col : 17 + col], (8, 128)),
                )
            )
    table = []
    for j in range(table_ref.shape[0]):
        total = jnp.zeros((8, 128), F32)
        for load, panel in columns:
            total = total + jnp.where(panel == lane + 128.0 * j, load, 0.0)
        table.append(jnp.sum(total, axis=0, keepdims=True))
        table_ref[pl.ds(j, 1), :] = table[j]
    for c in range(0, COMPS, 2):
        def row(i, y):
            return r_ref[pl.ds((c + i) * 64 + y, 8, stride=8), :]

        lo = jnp.concatenate([row(i, y) for i in (0, 1) for y in range(3)], axis=0)
        hi = jnp.concatenate([row(i, y) for i in (0, 1) for y in range(5, 8)], axis=0)
        store_layers((y1_ref, y2_ref), c, lo, hi, flags[7])
    rows = y1_ref.shape[0] - COMPS * 24
    pieces = [piece[j] for piece in zip(*map(split3, table)) for j in range(len(table))]
    if rows > len(pieces):
        pieces.append(jnp.zeros((rows - len(pieces), 128), F32))
    y1_ref[pl.ds(COMPS * 24, rows), :] = jnp.concatenate(pieces, axis=0).astype(BF16)


def store_layers(refs, c, lo, hi, parity):
    for m, ref in enumerate(refs):
        ref[pl.ds(c * 24, 48), :] = jnp.where(parity == m, hi, lo).astype(BF16)


def merge_kernel(height, start, table_ref, got_ref, token_ref, x_ref, out_ref, sum_ref):
    rows = got_ref[pl.ds(COMPS * 24, 8), :] if height == 2 else got_ref[pl.ds(COMPS * 24, 3 * height), :]
    rows = rows.astype(F32)
    total = table_ref[...] + token_ref[...]
    for piece in range(3):
        total = total + rows[piece * height : (piece + 1) * height]
    sum_ref[...] = total
    pieces = list(split3(total))
    if x_ref.shape[0] - start > 3 * height:
        pieces.append(jnp.zeros((x_ref.shape[0] - start - 3 * height, 128), F32))
    out_ref[pl.ds(start, x_ref.shape[0] - start), :] = jnp.concatenate(pieces, axis=0).astype(BF16)


def merge(table, got, token, x):
    height = table.shape[0]
    return pl.pallas_call(
        lambda *a: merge_kernel(height, COMPS * 24, *a),
        out_shape=[jax.ShapeDtypeStruct(x.shape, x.dtype), token_shape(table)],
        in_specs=[VM] * 4,
        out_specs=[VM] * 2,
        input_output_aliases={3: 0},
        compiler_params=GRANT,
        cost_estimate=cost(0.2),
        name="merge",
    )(table, got, token, x)


def in_hbm(x):
    return pltpu.with_memory_space_constraint(x, pltpu.HBM)


def load_rows(height):
    return -(-3 * height // 16) * 16


def pack(fields, panels, flags, height):
    whole = jax.ShapeDtypeStruct((COMPS * 64, 128), F32)
    outs = [whole, whole]
    outs.append(jax.ShapeDtypeStruct((COMPS * 24 + load_rows(height), 128), BF16))
    outs.append(jax.ShapeDtypeStruct((COMPS * 24, 128), BF16))
    outs.append(jax.ShapeDtypeStruct((height, 128), F32))
    return pl.pallas_call(
        pack_kernel,
        out_shape=outs,
        in_specs=[SM, HBM, HBM],
        out_specs=[VM] * len(outs),
        scratch_shapes=[
            pltpu.VMEM((128, 128), F32),
            pltpu.VMEM(panels.shape, jnp.int32),
            pltpu.SemaphoreType.DMA((2,)),
        ],
        compiler_params=GRANT,
        cost_estimate=cost(2),
        name="pack",
    )(flags, in_hbm(fields), in_hbm(panels))


def turn_kernel(pair_x, slots, flags, r_ref, *refs):
    sources, refs = refs[:5], refs[5:]
    (zt_ref, *x_refs), refs = refs[: 3 - pair_x], refs[3 - pair_x :]
    z_refs, (h_ref, row_ref, hit_ref), kept, token = refs[:2], refs[2:5], refs[5:8], refs[8]
    react_ref, w1_ref, sems = refs[9:]
    copies = [
        pltpu.make_async_copy(a, b, sems.at[i])
        for i, (a, b) in enumerate(zip(sources, (react_ref, w1_ref, *kept)))
    ]
    for copy in copies:
        copy.start()
    for c in range(0, COMPS, 2):
        lo = jnp.concatenate([r_ref[pl.ds((c + i) * 64, 24), :] for i in (0, 1)], axis=0)
        hi = jnp.concatenate([r_ref[pl.ds((c + i) * 64 + 40, 24), :] for i in (0, 1)], axis=0)
        store_layers(x_refs, c, lo, hi, flags[6])
    low = half_lanes((64, 128))
    for c in range(0, COMPS, 2):
        t = jnp.transpose(r_ref[pl.ds(c * 64, 128), :])
        top, bottom = t[:64], t[64:]
        even = jnp.where(low, top, swap_halves(bottom))
        odd = jnp.where(low, swap_halves(top), bottom)
        for i, x in ((0, even), (1, odd)):
            zt_ref[pl.ds((c + i) * 64, 64), :] = x
            for m, ref in enumerate(z_refs):
                up = flags[8] == m
                ref[pl.ds((c + i) * 3, 3), :] = jnp.where(up, x[61:], x[:3])
    for ref, start in [(x, COMPS * 24) for x in x_refs] + [(z, COMPS * 3) for z in z_refs]:
        if ref.shape[0] > start:
            ref[pl.ds(start, ref.shape[0] - start), :] = jnp.zeros(
                (ref.shape[0] - start, 128), ref.dtype
            )
    copies[0].wait()
    copies[1].wait()
    chem_in_kernel(slots, r_ref, react_ref, w1_ref, h_ref, row_ref, hit_ref)
    token[...] = jnp.zeros(token.shape, F32)
    for copy in copies[2:]:
        copy.wait()


def turn(flags, recon, react, layers, slots, pair_x, height):
    def struct(like):
        return jax.ShapeDtypeStruct(like.shape, like.dtype)

    layer_x = jax.ShapeDtypeStruct((COMPS * 24 + (load_rows(height) if pair_x else 0), 128), BF16)
    edge = jax.ShapeDtypeStruct((40 + -(-height // 8) * 8, 128), F32)
    outs = [struct(recon)] + [layer_x] * (2 - pair_x) + [edge] * 2
    outs += [
        jax.ShapeDtypeStruct((layers[0].shape[1], slots), BF16),
        jax.ShapeDtypeStruct((64, slots), BF16),
        jax.ShapeDtypeStruct((slots, 128), BF16),
    ]
    outs += [struct(x) for x in layers[1:]] + [jax.ShapeDtypeStruct((height, 128), F32)]
    return pl.pallas_call(
        lambda *a: turn_kernel(int(pair_x), slots, *a),
        out_shape=outs,
        in_specs=[SM, VM] + [HBM] * 5,
        out_specs=[VM] * len(outs),
        scratch_shapes=[
            pltpu.VMEM(react.shape, react.dtype),
            pltpu.VMEM(layers[0].shape, layers[0].dtype),
            pltpu.SemaphoreType.DMA((5,)),
        ],
        compiler_params=GRANT,
        cost_estimate=cost(2),
        name="turn",
    )(flags, recon, in_hbm(react), *map(in_hbm, layers))


def cost(us):
    return pl.CostEstimate(flops=0, transcendentals=0, bytes_accessed=int(us * 3.5e6))


def dot(a, b):
    return jnp.dot(a, b, preferred_element_type=F32)


def iota(shape, dim):
    return lax.broadcasted_iota(jnp.int32, shape, dim)


def where1(mask):
    return jnp.where(mask, 1.0, 0.0).astype(BF16)


def chem_in_kernel(slots, r_ref, react_ref, w1_ref, h_ref, row_ref, hit_ref):
    react = react_ref[...].astype(F32)
    react_b = react.astype(BF16)
    upper = where1(iota((128, 128), 0) <= iota((128, 128), 1))
    within = dot(react_b, upper)
    count = dot(react_b, jnp.ones((128, 128), BF16))
    below = where1(iota((64, 64), 1) < iota((64, 64), 0))
    offset = dot(below, count.astype(BF16))
    rank = (react * (within + offset)).astype(BF16)
    slot_lane = iota((64, slots), 1).astype(F32)
    off_col, cnt_col = offset[:, :1], count[:, :1]
    row_ref[...] = where1((slot_lane >= off_col) & (slot_lane < off_col + cnt_col))
    nt = (((1,), (1,)), ((), ()))
    count_row = lax.dot_general(
        jnp.ones((8, 128), BF16), react_b, nt, preferred_element_type=F32
    )
    offset_row = lax.dot_general(
        count_row.astype(BF16), below, nt, preferred_element_type=F32
    )
    slot_sub = iota((slots, 64), 0).astype(F32)
    slot_row = where1(
        (slot_sub >= offset_row[:1]) & (slot_sub < offset_row[:1] + count_row[:1])
    )
    lane_hit = dot(slot_row, rank) == iota((slots, 128), 0).astype(F32) + 1.0
    hit_ref[...] = where1(lane_hit)
    feat = jnp.zeros((slots, 128), F32)
    for c in range(COMPS):
        rows = dot(slot_row, r_ref[pl.ds(c * 64, 64), :].astype(BF16))
        hit = jnp.where(lane_hit, rows, 0.0).astype(BF16)
        feat = feat + dot(hit, where1(iota((128, 128), 1) == c))
    feat = jnp.transpose(feat)[:COMPS].astype(BF16)
    tn = (((0,), (0,)), ((), ()))
    one = lax.dot_general(w1_ref[...], feat, tn, preferred_element_type=F32)
    h_ref[...] = jax.nn.gelu(one).astype(BF16)


def chem_kernel(h_ref, w2_ref, w3_ref, w4_ref, row_ref, hit_ref, out_ref, token):
    two = jax.nn.gelu(dot(w2_ref[...], h_ref[...])).astype(BF16)
    three = jax.nn.gelu(dot(w3_ref[...], two)).astype(BF16)
    rates = dot(w4_ref[...], three)
    slots = rates.shape[1]
    rates = jnp.concatenate([rates, jnp.zeros((128 - COMPS, slots), F32)], axis=0)
    rates_t = jnp.transpose(rates).astype(BF16)
    hit, row_slot = hit_ref[...].astype(F32), row_ref[...]
    for c in range(COMPS):
        spread = hit * dot(rates_t, where1(iota((128, 128), 0) == c))
        out_ref[pl.ds(c * 64, 64), :] = dot(row_slot, spread.astype(BF16))
    token[...] = jnp.zeros(token.shape, F32)


def chem(hidden, layers, row_slot, hit, table):
    return pl.pallas_call(
        chem_kernel,
        out_shape=[jax.ShapeDtypeStruct((COMPS * 64, 128), F32), token_shape(table)],
        in_specs=[VM] * 6,
        out_specs=[VM] * 2,
        compiler_params=GRANT,
        cost_estimate=cost(2),
        name="chem",
    )(hidden, *layers, row_slot, hit)


def halo_lines(refs, scratch, own, sign_comp, at_wall, order, second):
    for c in range(0, COMPS, 2):
        block = refs[0][pl.ds(c * 24, 48), :].astype(F32)
        if len(refs) == 2:
            block = jnp.where(second, refs[1][pl.ds(c * 24, 48), :].astype(F32), block)
        for i in (0, 1):
            for k in range(3):
                mirror = own(c + i, order[k])
                if c + i == sign_comp:
                    mirror = -mirror
                got = block[(i * 3 + k) * 8 : (i * 3 + k + 1) * 8]
                scratch[pl.ds(((c + i) * 3 + k) * 8, 8), :] = jnp.where(at_wall, mirror, got)


def flux_x_kernel(count, flags, r_ref, *refs):
    layers, (out_ref, token, lo_s, hi_s, left, right) = refs[:count], refs[count:]

    def own(c, x):
        return r_ref[pl.ds(c * 64 + x * 8, 8), :]

    halo_lines(layers, lo_s, own, 1, flags[0] == 1, (2, 1, 0), flags[6] == 0)
    halo_lines(layers, hi_s, own, 1, flags[1] == 1, (7, 6, 5), flags[6] == 1)

    def line(c):
        return (
            [lo_s[rows8(c * 3 + k), :] for k in range(3)]
            + [r_ref[rows8(c * 8 + x), :] for x in range(8)]
            + [hi_s[rows8(c * 3 + k), :] for k in range(3)]
        )

    face_states(line, left, right, 9)

    def emit(c, x, change):
        out_ref[pl.ds(c * 64 + x * 8, 8), :] = change

    line_changes(left, right, 9, 0, emit)
    token[...] = jnp.zeros(token.shape, F32)


def flux_y_kernel(count, flags, r_ref, acc_ref, *refs):
    layers, (out_ref, lo_s, hi_s, left, right) = refs[:count], refs[count:]

    def own(c, y):
        return r_ref[pl.ds(c * 64 + y, 8, stride=8), :]

    halo_lines(layers, lo_s, own, 2, flags[2] == 1, (2, 1, 0), flags[7] == 0)
    halo_lines(layers, hi_s, own, 2, flags[3] == 1, (7, 6, 5), flags[7] == 1)

    def line(c):
        return (
            [lo_s[rows8(c * 3 + k), :] for k in range(3)]
            + [r_ref[pl.ds(c * 64 + y, 8, stride=8), :] for y in range(8)]
            + [hi_s[rows8(c * 3 + k), :] for k in range(3)]
        )

    face_states(line, left, right, 9)

    def emit(c, y, change):
        at = pl.ds(c * 64 + y, 8, stride=8)
        out_ref[at, :] = acc_ref[at, :] + change

    line_changes(left, right, 9, 1, emit)


def flux_z_kernel(count, own_count, flags, f_ref, zt_ref, acc_ref, src_ref, table_ref, *refs):
    layers, (out_hbm, impulse_ref) = refs[:count], refs[count : count + 2]
    ext, left, right, back, out_ref, sems = refs[count + 2 :]
    place = flags[9] * own_count
    loads = jnp.broadcast_to(table_ref[pl.ds(place // 128, 1), :], (8, 128))
    loads = pltpu.roll(loads, (128 - place % 128) % 128, 1)
    impulse_ref[...] = loads[:1, :own_count] * (1.0 / (PATCH * PATCH))
    low3, low = half_lanes((3, 128)), half_lanes((64, 128))

    def got(c, second):
        x = layers[0][pl.ds(c * 3, 3), :]
        if count == 2:
            x = jnp.where(second, layers[1][pl.ds(c * 3, 3), :], x)
        return swap_halves(x)

    for c in range(COMPS):
        sign = -1.0 if c == 3 else 1.0
        own = zt_ref[pl.ds(c * 64, 64), :]
        first, last = own[:3], own[61:]
        mirror_lo = sign * jnp.concatenate([first[2:3], first[1:2], first[0:1]], axis=0)
        mirror_hi = sign * jnp.concatenate([last[2:3], last[1:2], last[0:1]], axis=0)
        below = jnp.where(flags[4] == 1, mirror_lo, got(c, flags[8] == 0))
        above = jnp.where(flags[5] == 1, mirror_hi, got(c, flags[8] == 1))
        ext[pl.ds(c * 72, 3), :] = jnp.where(low3, below, swap_halves(last))
        ext[pl.ds(c * 72 + 3, 64), :] = own
        ext[pl.ds(c * 72 + 67, 3), :] = jnp.where(low3, swap_halves(first), above)

    def line(c):
        return [ext[pl.ds(c * 72 + e, 8, stride=8), :] for e in range(14)]

    face_states(line, left, right, 9)

    def emit(c, z, change):
        back[pl.ds(c * 64 + z, 8, stride=8), :] = change

    line_changes(left, right, 9, 2, emit)
    copies = []
    for c in range(0, COMPS, 2):
        even, odd = back[pl.ds(c * 64, 64), :], back[pl.ds(c * 64 + 64, 64), :]
        t = jnp.concatenate(
            [jnp.where(low, even, swap_halves(odd)), jnp.where(low, swap_halves(even), odd)],
            axis=0,
        )
        at = pl.ds(c * 64, 128)
        change = acc_ref[at, :] + jnp.transpose(t)
        out_ref[at, :] = f_ref[at, :] - TIME_STEP * change + CHEM_STEP * src_ref[at, :]
        copies.append(pltpu.make_async_copy(out_ref.at[at], out_hbm.at[at], sems.at[c // 2]))
        copies[-1].start()
    for copy in copies:
        copy.wait()


def state_scratch():
    return [pltpu.VMEM((COMPS * 9 * 8, 128), F32)] * 2


def halo_scratch():
    return [pltpu.VMEM((COMPS * 24, 128), F32)] * 2


def token_shape(table):
    return jax.ShapeDtypeStruct(table.shape, F32)


def flux_x(flags, recon, layers, table):
    return pl.pallas_call(
        lambda *a: flux_x_kernel(len(layers), *a),
        out_shape=[jax.ShapeDtypeStruct(recon.shape, F32), token_shape(table)],
        in_specs=[SM] + [VM] * (1 + len(layers)),
        out_specs=[VM] * 2,
        scratch_shapes=halo_scratch() + state_scratch(),
        compiler_params=GRANT,
        cost_estimate=cost(2),
        name="flux_x",
    )(flags, recon, *layers)


def flux_y(flags, recon, acc, layers):
    return pl.pallas_call(
        lambda *a: flux_y_kernel(len(layers), *a),
        out_shape=jax.ShapeDtypeStruct(recon.shape, F32),
        in_specs=[SM] + [VM] * (2 + len(layers)),
        out_specs=VM,
        scratch_shapes=halo_scratch() + state_scratch(),
        compiler_params=GRANT,
        cost_estimate=cost(2),
        name="flux_y",
    )(flags, recon, acc, *layers)


def flux_z(flags, fields, turned, acc, source, table, layers, own_count):
    return pl.pallas_call(
        lambda *a: flux_z_kernel(len(layers), own_count, *a),
        out_shape=[
            jax.ShapeDtypeStruct(fields.shape, F32),
            jax.ShapeDtypeStruct((1, own_count), F32),
        ],
        in_specs=[SM] + [VM] * (5 + len(layers)),
        out_specs=[HBM, VM],
        scratch_shapes=[pltpu.VMEM((COMPS * 72, 128), F32)]
        + state_scratch()
        + [pltpu.VMEM(fields.shape, F32)] * 2
        + [pltpu.SemaphoreType.DMA((COMPS // 2,))],
        compiler_params=GRANT,
        cost_estimate=cost(3),
        name="flux_z",
    )(flags, fields, turned, acc, source, table, *layers)


def swap(x, axis, second, outer=False):
    n = lax.axis_size(axis)
    pairs = [(i, i + 1) for i in range(int(second), n - 1, 2)]
    if outer:
        pairs.append((0, n - 1))
    return lax.ppermute(x, axis, [(a, b) for a, b in pairs] + [(b, a) for a, b in pairs])


def sum_over(table, axis, step=1):
    size = lax.axis_size(axis)
    if size & (size - 1):
        return lax.psum(table, axis)
    while step < size:
        table = table + lax.ppermute(table, axis, [(i, i ^ step) for i in range(size)])
        step *= 2
    return table


def split_table(table):
    hi = lax.reduce_precision(table, 8, 7)
    mid = lax.reduce_precision(table - hi, 8, 7)
    return jnp.concatenate([hi, mid, table - hi - mid], axis=0).astype(BF16)


def join_table(rows, height):
    rows = rows[: 3 * height].astype(F32)
    return rows[:height] + rows[height : 2 * height] + rows[2 * height :]


def body(fields, reacting, panel_map, layer_one, layer_two, layer_three, layer_four):
    shape = fields.shape
    sizes = [lax.axis_size(a) for a in AXES]
    index = [lax.axis_index(a) for a in AXES]
    place = (index[0] * sizes[1] + index[1]) * sizes[2] + index[2]
    flags = [f for i, n in zip(index, sizes) for f in (i == 0, i == n - 1)]
    flags = jnp.stack([f.astype(jnp.int32) for f in flags] + [i % 2 for i in index] + [place])
    pair_x = sizes[0] == 2
    panels_all = 2 * (shape[1] * sizes[0] // PATCH) * (shape[3] * sizes[2] // PATCH)
    own = panels_all // (sizes[0] * sizes[1] * sizes[2])
    height = panels_all // 128
    slots = BAL * min(4, sizes[0])
    layer_rows, edge_rows = COMPS * 24, 40
    ride_y, ride_z = sizes[1] & (sizes[1] - 1) == 0, sizes[2] in (2, 4)

    flat = fields.reshape(-1, shape[3])
    flat, recon, y_first, y_second, table = pack(
        flat, panel_map.reshape(-1, shape[3]), flags, height
    )
    y_got = [swap(y_first, "gy", 0)]
    if sizes[1] > 2:
        y_got.append(swap(y_second, "gy", 1))
    layers = (layer_one.T, layer_two, layer_three, layer_four)
    turned, *xs, z_first, z_second, hidden, row_slot, hit, w2, w3, w4, token = turn(
        flags, recon, reacting.reshape(-1, shape[3]), layers, slots, pair_x, height
    )
    if pair_x and ride_y:
        merged, table = merge(table, y_got[0], token, xs[0])
        xs = [merged]
    else:
        table = table + token
        if ride_y:
            table = table + join_table(y_got[0][layer_rows:], height)
        else:
            table = lax.psum(table, "gy")
        if pair_x:
            xs = [lax.dynamic_update_slice(xs[0], split_table(table), (layer_rows, 0))]
    x_got = [swap(x, "gx", m) for m, x in enumerate(xs)]
    source, token = chem(hidden, (w2, w3, w4), row_slot, hit, table)
    if pair_x:
        table = table + join_table(x_got[0][layer_rows:], height)
    else:
        table = sum_over(table, "gx")
    table = table + token
    if not ride_z:
        table = sum_over(table, "gz")
    z_got = [swap(lax.dynamic_update_slice(z_first, table, (edge_rows, 0)), "gz", 0)]
    if ride_z:
        table = table + z_got[0][edge_rows : edge_rows + height]
    if sizes[2] > 2:
        z_second = lax.dynamic_update_slice(z_second, table, (edge_rows, 0))
        z_got.append(swap(z_second, "gz", 1, ride_z))
        if ride_z:
            table = table + z_got[1][edge_rows : edge_rows + height]
    acc, token = flux_x(flags, recon, x_got, table)
    table = table + token
    if ride_y:
        table = sum_over(table, "gy", 2)
    acc = flux_y(flags, recon, acc, y_got)
    new, impulse = flux_z(flags, flat, turned, acc, source, table, z_got, own)
    return new.reshape(shape), impulse.reshape(own)


def solution(mesh):
    return jax.shard_map(
        body,
        mesh=mesh,
        in_specs=(
            P(None, "gx", "gy", "gz"),
            P("gx", "gy", "gz"),
            P(None, "gx", "gz"),
            P(),
            P(),
            P(),
            P(),
        ),
        out_specs=(P(None, "gx", "gy", "gz"), P(("gx", "gy", "gz"))),
        check_vma=False,
    )
```

```python
import jax
import jax.numpy as jnp
from jax import lax
from jax.experimental import pallas as pl
from jax.experimental.pallas import tpu as pltpu
from jax.sharding import PartitionSpec as P


BAL = 64
COMPS = 12
PATCH = 8

HEAT_RATIO = 1.4
TIME_STEP = 0.1
CHEM_STEP = 0.25
WENO_EPS = 1e-06
EPS = WENO_EPS * 4.0 / 36.0
AXES = ("gx", "gy", "gz")
F32 = jnp.float32
BF16 = jnp.bfloat16
GRANT = pltpu.CompilerParams(vmem_limit_bytes=12 * 2**20)
VM = pl.BlockSpec(memory_space=pltpu.VMEM)
HBM = pl.BlockSpec(memory_space=pltpu.HBM)


def weno_line(v):
    n = len(v)
    d = [(v[j + 1] - v[j]) * (1.0 / 6.0) for j in range(n - 1)]
    d3 = [3.0 * x for x in d]
    q = {}
    for e in range(1, n - 1):
        s = d[e] - d[e - 1]
        q[e] = (13.0 / 3.0) * (s * s) + EPS
    upper, lower = {}, {}
    for e in range(2, n - 2):
        dm, dp = d[e - 1], d[e]
        t0 = d3[e - 1] - d[e - 2]
        t1 = dm + dp
        t2 = d3[e] - d[e + 1]
        b0 = q[e - 1] + t0 * t0
        b1 = q[e] + t1 * t1
        b2 = q[e + 1] + t2 * t2
        m01, m02, m12 = b0 * b1, b0 * b2, b1 * b2
        s01, s02, s12 = m01 * m01, m02 * m02, m12 * m12
        w1, w01, w12 = 6.0 * s02, 3.0 * s01, 3.0 * s12
        if e < n - 3:
            num = s12 * (t0 + t0 - dm) + w1 * (t1 + dp) + w01 * (t2 + dp)
            upper[e] = v[e] + num / (s12 + w1 + w01)
        if e > 2:
            num = s01 * (t2 + t2 - dp) + w1 * (t1 + dm) + w12 * (t0 + dm)
            lower[e] = v[e] - num / (s01 + w1 + w12)
    return upper, lower


def weno_one(v):
    d = [(v[j + 1] - v[j]) * (1.0 / 6.0) for j in range(4)]
    s = [d[j + 1] - d[j] for j in range(3)]
    q = [(13.0 / 3.0) * (x * x) + EPS for x in s]
    dm, dp = d[1], d[2]
    t0, t1, t2 = 3.0 * dm - d[0], dm + dp, 3.0 * dp - d[3]
    b0, b1, b2 = q[0] + t0 * t0, q[1] + t1 * t1, q[2] + t2 * t2
    m01, m02, m12 = b0 * b1, b0 * b2, b1 * b2
    w0, w1, w2 = m12 * m12, 6.0 * (m02 * m02), 3.0 * (m01 * m01)
    num = w0 * (t0 + t0 - dm) + w1 * (t1 + dp) + w2 * (t2 + dp)
    return v[2] + num / (w0 + w1 + w2)


def hllc(left, right, normal):
    n = 1 + normal

    def side(x):
        rho = jnp.exp(x[0])
        g = jnp.exp(0.5 * (x[4] - x[0]))
        h = g * g
        return rho, h, rho * h, (HEAT_RATIO**0.5) * g, x[n]

    rho_l, h_l, p_l, c_l, u_l = side(left)
    rho_r, h_r, p_r, c_r, u_r = side(right)
    s_l = jnp.minimum(u_l - c_l, u_r - c_r)
    s_r = jnp.maximum(u_l + c_l, u_r + c_r)
    m_l = rho_l * (s_l - u_l)
    m_r = rho_r * (s_r - u_r)
    s = (p_r - p_l + u_l * m_l - u_r * m_r) / (m_l - m_r)
    use_l = (s >= 0) | (s_l >= 0)
    pick = [jnp.where(use_l, a, b) for a, b in zip(left, right)]
    rho = jnp.where(use_l, rho_l, rho_r)
    h = jnp.where(use_l, h_l, h_r)
    p = jnp.where(use_l, p_l, p_r)
    wave = jnp.where(use_l, s_l, s_r)
    act = jnp.where(use_l, jnp.minimum(s_l, 0.0), jnp.maximum(s_r, 0.0))
    u = pick[n]
    rel = s - u
    ratio = rel / (wave - s)
    mass = rho * (u + act * ratio)
    k = rho * act * (1.0 + ratio) * rel
    square = pick[1] * pick[1] + pick[2] * pick[2] + pick[3] * pick[3]
    enthalpy = (1.0 / (HEAT_RATIO - 1.0) + 1.0) * h + 0.5 * square
    flux = [mass * x for x in pick]
    flux[0] = mass
    flux[n] = flux[n] + (p + k)
    flux[4] = enthalpy * mass + k * s
    return flux


def place_flags():
    sizes = [lax.axis_size(a) for a in AXES]
    index = [lax.axis_index(a) for a in AXES]
    place = (index[0] * sizes[1] + index[1]) * sizes[2] + index[2]
    flags = [f for i, n in zip(index, sizes) for f in (i == 0, i == n - 1)]
    return flags + [lax.rem(i, 2) for i in index] + [place]


def rows8(index):
    return pl.ds(pl.multiple_of(index * 8, 8), 8)


def face_states(load_line, left_ref, right_ref, faces):
    def one(c, carry):
        upper, lower = weno_line(load_line(c))
        for f in range(faces):
            left_ref[rows8(c * faces + f), :] = upper[f + 2]
            right_ref[rows8(c * faces + f), :] = lower[f + 3]
        return carry

    lax.fori_loop(0, COMPS, one, 0)


def line_changes(left_ref, right_ref, faces, normal, emit):
    before = None
    for f in range(faces):
        left = [left_ref[pl.ds((c * faces + f) * 8, 8), :] for c in range(COMPS)]
        right = [right_ref[pl.ds((c * faces + f) * 8, 8), :] for c in range(COMPS)]
        flux = hllc(left, right, normal)
        if before is not None:
            for c in range(COMPS):
                emit(c, f - 1, flux[c] - before[c])
        before = flux


def half_lanes(shape):
    return lax.broadcasted_iota(jnp.int32, shape, 1) < 64


def swap_halves(x):
    return pltpu.roll(x, 64, 1)


def split3(x):
    hi = x.astype(BF16).astype(F32)
    mid = (x - hi).astype(BF16).astype(F32)
    return hi, mid, x - hi - mid


def fetch(pairs, sems):
    copies = [pltpu.make_async_copy(a, b, sems.at[i]) for i, (a, b) in enumerate(pairs)]
    for copy in copies:
        copy.start()
    return copies


def pack_kernel(*refs):
    f_hbm, map_hbm, *sources = refs[:7]
    f_ref, r_ref, y1_ref, y2_ref, table_ref, *kept = refs[7:17]
    buf, map_ref, sems = refs[17:]
    half = kept[2].shape[0]
    sources[2] = sources[2].at[pl.ds(0, half)]
    copies = fetch([(f_hbm, f_ref), (map_hbm, map_ref), *zip(sources, kept)], sems)
    flags = place_flags()
    copies[0].wait()
    for x in range(8):
        def at(c):
            return f_ref[pl.ds(c * 64 + x * 8, 8), :]

        rho = at(0)
        inv = 1.0 / rho
        u = [at(c) * inv for c in (1, 2, 3)]
        p = (HEAT_RATIO - 1.0) * (
            at(4) - 0.5 * rho * (u[0] * u[0] + u[1] * u[1] + u[2] * u[2])
        )
        out = [jnp.log(rho)] + u + [jnp.log(p)] + [at(c) * inv for c in range(5, COMPS)]
        for c in range(COMPS):
            r_ref[pl.ds(c * 64 + x * 8, 8), :] = out[c]
    pushes = []
    for wall in range(2):
        rows = (0, 1, 2) if wall == 0 else (7, 6, 5)
        state = []
        for c in (0, 2, 4):
            a = [r_ref[pl.ds(c * 64 + y, 8, stride=8), :] for y in rows]
            sign = -1.0 if c == 2 else 1.0
            state.append(weno_one([a[2], a[1], a[0], sign * a[0], sign * a[1]]))
        rho = jnp.exp(state[0])
        p = jnp.exp(state[2])
        out_speed = -state[1] if wall == 0 else state[1]
        speed = jnp.abs(out_speed) + jnp.sqrt(HEAT_RATIO * p / rho)
        push = p + rho * out_speed * (out_speed + speed)
        x = jnp.where(flags[2 + wall], push, 0.0)
        for s in (1, 2, 4):
            x = x + pltpu.roll(x, 128 - s, 1)
        for s in (1, 2):
            x = x + pltpu.roll(x, 8 - s, 0)
        pushes.append(x)
    copies[1].wait()
    ids = map_ref[...].astype(F32)
    tall = jnp.concatenate(pushes + [ids, jnp.zeros((96, 128), F32)], axis=0)
    buf[...] = jnp.transpose(tall)
    groups = [buf[pl.ds(64 * g, 8, stride=8), :] for g in range(2)]
    lane = lax.broadcasted_iota(jnp.int32, (8, 128), 1).astype(F32)
    columns = []
    for g in groups:
        for col in (0, 4, 8, 12):
            columns.append(
                (
                    jnp.broadcast_to(g[:, col : col + 1], (8, 128)),
                    jnp.broadcast_to(g[:, 16 + col : 17 + col], (8, 128)),
                )
            )
    table = []
    for j in range(table_ref.shape[0]):
        total = jnp.zeros((8, 128), F32)
        for load, panel in columns:
            total = total + jnp.where(panel == lane + 128.0 * j, load, 0.0)
        table.append(jnp.sum(total, axis=0, keepdims=True))
        table_ref[pl.ds(j, 1), :] = table[j]
    for c in range(0, COMPS, 2):
        def row(i, y):
            return r_ref[pl.ds((c + i) * 64 + y, 8, stride=8), :]

        lo = jnp.concatenate([row(i, y) for i in (0, 1) for y in range(3)], axis=0)
        hi = jnp.concatenate([row(i, y) for i in (0, 1) for y in range(5, 8)], axis=0)
        store_layers((y1_ref, y2_ref), c, lo, hi, flags[7])
    rows = y1_ref.shape[0] - COMPS * 24
    pieces = [piece[j] for piece in zip(*map(split3, table)) for j in range(len(table))]
    if rows > len(pieces):
        pieces.append(jnp.zeros((rows - len(pieces), 128), F32))
    y1_ref[pl.ds(COMPS * 24, rows), :] = jnp.concatenate(pieces, axis=0).astype(BF16)
    for copy in copies[2:]:
        copy.wait()


def store_layers(refs, c, lo, hi, parity):
    for m, ref in enumerate(refs):
        ref[pl.ds(c * 24, 48), :] = jnp.where(parity == m, hi, lo).astype(BF16)


def put_table_kernel(table_ref, x_ref, out_ref):
    start = COMPS * 24
    rows = x_ref.shape[0] - start
    pieces = list(split3(table_ref[...]))
    used = 3 * table_ref.shape[0]
    if rows > used:
        pieces.append(jnp.zeros((rows - used, 128), F32))
    out_ref[pl.ds(start, rows), :] = jnp.concatenate(pieces, axis=0).astype(BF16)


def put_table(table, x):
    return pl.pallas_call(
        put_table_kernel,
        out_shape=jax.ShapeDtypeStruct(x.shape, x.dtype),
        in_specs=[VM] * 2,
        out_specs=VM,
        input_output_aliases={1: 0},
        compiler_params=GRANT,
        cost_estimate=cost(0.2),
        name="put_table",
    )(table, x)


def in_hbm(x):
    return pltpu.with_memory_space_constraint(x, pltpu.HBM)


def load_rows(height):
    return -(-3 * height // 16) * 16


def pack(fields, panels, react, layers, height):
    whole = jax.ShapeDtypeStruct((COMPS * 64, 128), F32)
    outs = [whole, whole]
    outs.append(jax.ShapeDtypeStruct((COMPS * 24 + load_rows(height), 128), BF16))
    outs.append(jax.ShapeDtypeStruct((COMPS * 24, 128), BF16))
    outs.append(jax.ShapeDtypeStruct((height, 128), F32))
    one, two, three, four = layers
    kept = [jax.ShapeDtypeStruct(x.shape, x.dtype) for x in (react, one, two, three, four)]
    kept[2] = jax.ShapeDtypeStruct((two.shape[0] // 2, two.shape[1]), two.dtype)
    outs += kept
    return pl.pallas_call(
        pack_kernel,
        out_shape=outs,
        in_specs=[HBM] * 7,
        out_specs=[VM] * len(outs),
        scratch_shapes=[
            pltpu.VMEM((128, 128), F32),
            pltpu.VMEM(panels.shape, jnp.int32),
            pltpu.SemaphoreType.DMA((7,)),
        ],
        compiler_params=GRANT,
        cost_estimate=cost(2),
        name="pack",
    )(*map(in_hbm, (fields, panels, react, *layers)))


def turn_kernel(pair_x, r_ref, zt_ref, *refs):
    x_refs, (z1_ref, z2_ref, token) = refs[: 2 - pair_x], refs[2 - pair_x :]
    z_refs = (z1_ref, z2_ref)
    flags = place_flags()
    for c in range(0, COMPS, 2):
        lo = jnp.concatenate([r_ref[pl.ds((c + i) * 64, 24), :] for i in (0, 1)], axis=0)
        hi = jnp.concatenate([r_ref[pl.ds((c + i) * 64 + 40, 24), :] for i in (0, 1)], axis=0)
        store_layers(x_refs, c, lo, hi, flags[6])
    low = half_lanes((64, 128))
    for c in range(0, COMPS, 2):
        t = jnp.transpose(r_ref[pl.ds(c * 64, 128), :])
        top, bottom = t[:64], t[64:]
        even = jnp.where(low, top, swap_halves(bottom))
        odd = jnp.where(low, swap_halves(top), bottom)
        for i, x in ((0, even), (1, odd)):
            zt_ref[pl.ds((c + i) * 64, 64), :] = x
            for m, ref in enumerate(z_refs):
                up = flags[8] == m
                ref[pl.ds((c + i) * 3, 3), :] = jnp.where(up, x[61:], x[:3])
    for ref, start in [(x, COMPS * 24) for x in x_refs] + [(z, COMPS * 3) for z in z_refs]:
        if ref.shape[0] > start:
            ref[pl.ds(start, ref.shape[0] - start), :] = jnp.zeros(
                (ref.shape[0] - start, 128), ref.dtype
            )
    token[...] = jnp.zeros(token.shape, F32)


def turn(recon, pair_x, height):
    layer_x = jax.ShapeDtypeStruct((COMPS * 24 + (load_rows(height) if pair_x else 0), 128), BF16)
    edge = jax.ShapeDtypeStruct((40 + -(-height // 8) * 8, 128), F32)
    outs = [jax.ShapeDtypeStruct(recon.shape, F32)] + [layer_x] * (2 - pair_x) + [edge] * 2
    outs.append(jax.ShapeDtypeStruct((height, 128), F32))
    return pl.pallas_call(
        lambda *a: turn_kernel(int(pair_x), *a),
        out_shape=outs,
        in_specs=[VM],
        out_specs=[VM] * len(outs),
        compiler_params=GRANT,
        cost_estimate=cost(1),
        name="turn",
    )(recon)


def cost(us):
    return pl.CostEstimate(flops=0, transcendentals=0, bytes_accessed=int(us * 3.5e6))


def dot(a, b):
    return jnp.dot(a, b, preferred_element_type=F32)


def iota(shape, dim):
    return lax.broadcasted_iota(jnp.int32, shape, dim)


def where1(mask):
    return jnp.where(mask, 1.0, 0.0).astype(BF16)


def chem_in_kernel(
    slots, r_ref, react_ref, w1_ref, w2_hbm, h_ref, row_ref, hit_ref, w2_ref, token, sems
):
    half = w2_ref.shape[0]
    (copy,) = fetch([(w2_hbm.at[pl.ds(half, half)], w2_ref)], sems)
    react = react_ref[...].astype(F32)
    react_b = react.astype(BF16)
    upper = where1(iota((128, 128), 0) <= iota((128, 128), 1))
    within = dot(react_b, upper)
    count = dot(react_b, jnp.ones((128, 128), BF16))
    below = where1(iota((64, 64), 1) < iota((64, 64), 0))
    offset = dot(below, count.astype(BF16))
    rank = (react * (within + offset)).astype(BF16)
    slot_lane = iota((64, slots), 1).astype(F32)
    off_col, cnt_col = offset[:, :1], count[:, :1]
    row_ref[...] = where1((slot_lane >= off_col) & (slot_lane < off_col + cnt_col))
    nt = (((1,), (1,)), ((), ()))
    count_row = lax.dot_general(
        jnp.ones((8, 128), BF16), react_b, nt, preferred_element_type=F32
    )
    offset_row = lax.dot_general(
        count_row.astype(BF16), below, nt, preferred_element_type=F32
    )
    slot_sub = iota((slots, 64), 0).astype(F32)
    slot_row = where1(
        (slot_sub >= offset_row[:1]) & (slot_sub < offset_row[:1] + count_row[:1])
    )
    lane_hit = dot(slot_row, rank) == iota((slots, 128), 0).astype(F32) + 1.0
    hit_ref[...] = where1(lane_hit)
    feat = jnp.zeros((slots, 128), F32)
    for c in range(COMPS):
        rows = dot(slot_row, r_ref[pl.ds(c * 64, 64), :].astype(BF16))
        hit = jnp.where(lane_hit, rows, 0.0).astype(BF16)
        feat = feat + dot(hit, where1(iota((128, 128), 1) == c))
    feat = jnp.transpose(feat)[:COMPS].astype(BF16)
    tn = (((0,), (0,)), ((), ()))
    one = lax.dot_general(w1_ref[...], feat, tn, preferred_element_type=F32)
    h_ref[...] = jax.nn.gelu(one).astype(BF16)
    token[...] = jnp.zeros(token.shape, F32)
    copy.wait()


def chem_in(recon, react, layer_one, layer_two, slots, table):
    return pl.pallas_call(
        lambda *a: chem_in_kernel(slots, *a),
        out_shape=[
            jax.ShapeDtypeStruct((layer_one.shape[1], slots), BF16),
            jax.ShapeDtypeStruct((64, slots), BF16),
            jax.ShapeDtypeStruct((slots, 128), BF16),
            jax.ShapeDtypeStruct((layer_two.shape[0] // 2, layer_two.shape[1]), BF16),
            token_shape(table),
        ],
        in_specs=[VM] * 3 + [HBM],
        out_specs=[VM] * 5,
        scratch_shapes=[pltpu.SemaphoreType.DMA((1,))],
        compiler_params=GRANT,
        cost_estimate=cost(1),
        name="chem_in",
    )(recon, react, layer_one, in_hbm(layer_two))


def chem_mid_kernel(h_ref, w2_ref, w2b_ref, w3_ref, out_ref, token):
    two = [jax.nn.gelu(dot(w[...], h_ref[...])).astype(BF16) for w in (w2_ref, w2b_ref)]
    two = jnp.concatenate(two, axis=0)
    out_ref[...] = jax.nn.gelu(dot(w3_ref[...], two)).astype(BF16)
    token[...] = jnp.zeros(token.shape, F32)


def chem_mid(hidden, halves, layer_three, table):
    return pl.pallas_call(
        chem_mid_kernel,
        out_shape=[
            jax.ShapeDtypeStruct((layer_three.shape[0], hidden.shape[1]), BF16),
            token_shape(table),
        ],
        in_specs=[VM] * 4,
        out_specs=[VM] * 2,
        compiler_params=GRANT,
        cost_estimate=cost(2),
        name="chem_mid",
    )(hidden, *halves, layer_three)


def chem_out_kernel(h_ref, w4_ref, row_ref, hit_ref, out_ref, token):
    rates = dot(w4_ref[...], h_ref[...])
    slots = rates.shape[1]
    rates = jnp.concatenate([rates, jnp.zeros((128 - COMPS, slots), F32)], axis=0)
    rates_t = jnp.transpose(rates).astype(BF16)
    hit, row_slot = hit_ref[...].astype(F32), row_ref[...]
    for c in range(COMPS):
        spread = hit * dot(rates_t, where1(iota((128, 128), 0) == c))
        out_ref[pl.ds(c * 64, 64), :] = dot(row_slot, spread.astype(BF16))
    token[...] = jnp.zeros(token.shape, F32)


def chem_out(hidden, layer_four, row_slot, hit, table):
    return pl.pallas_call(
        chem_out_kernel,
        out_shape=[jax.ShapeDtypeStruct((COMPS * 64, 128), F32), token_shape(table)],
        in_specs=[VM] * 4,
        out_specs=[VM] * 2,
        compiler_params=GRANT,
        cost_estimate=cost(1),
        name="chem_out",
    )(hidden, layer_four, row_slot, hit)


def halo_lines(refs, scratch, own, sign_comp, at_wall, order, second):
    for c in range(0, COMPS, 2):
        block = refs[0][pl.ds(c * 24, 48), :].astype(F32)
        if len(refs) == 2:
            block = jnp.where(second, refs[1][pl.ds(c * 24, 48), :].astype(F32), block)
        for i in (0, 1):
            for k in range(3):
                mirror = own(c + i, order[k])
                if c + i == sign_comp:
                    mirror = -mirror
                got = block[(i * 3 + k) * 8 : (i * 3 + k + 1) * 8]
                scratch[pl.ds(((c + i) * 3 + k) * 8, 8), :] = jnp.where(at_wall, mirror, got)


def flux_x_kernel(count, r_ref, acc_ref, *refs):
    flags = place_flags()
    layers, (out_ref, token, lo_s, hi_s, left, right) = refs[:count], refs[count:]

    def own(c, x):
        return r_ref[pl.ds(c * 64 + x * 8, 8), :]

    halo_lines(layers, lo_s, own, 1, flags[0], (2, 1, 0), flags[6] == 0)
    halo_lines(layers, hi_s, own, 1, flags[1], (7, 6, 5), flags[6] == 1)

    def line(c):
        return (
            [lo_s[rows8(c * 3 + k), :] for k in range(3)]
            + [r_ref[rows8(c * 8 + x), :] for x in range(8)]
            + [hi_s[rows8(c * 3 + k), :] for k in range(3)]
        )

    face_states(line, left, right, 9)

    def emit(c, x, change):
        at = pl.ds(c * 64 + x * 8, 8)
        out_ref[at, :] = acc_ref[at, :] + change

    line_changes(left, right, 9, 0, emit)
    token[...] = jnp.zeros(token.shape, F32)


def flux_y_kernel(count, r_ref, *refs):
    flags = place_flags()
    layers, (out_ref, token, lo_s, hi_s, left, right) = refs[:count], refs[count:]

    def own(c, y):
        return r_ref[pl.ds(c * 64 + y, 8, stride=8), :]

    halo_lines(layers, lo_s, own, 2, flags[2], (2, 1, 0), flags[7] == 0)
    halo_lines(layers, hi_s, own, 2, flags[3], (7, 6, 5), flags[7] == 1)

    def line(c):
        return (
            [lo_s[rows8(c * 3 + k), :] for k in range(3)]
            + [r_ref[pl.ds(c * 64 + y, 8, stride=8), :] for y in range(8)]
            + [hi_s[rows8(c * 3 + k), :] for k in range(3)]
        )

    face_states(line, left, right, 9)

    def emit(c, y, change):
        out_ref[pl.ds(c * 64 + y, 8, stride=8), :] = change

    line_changes(left, right, 9, 1, emit)
    token[...] = jnp.zeros(token.shape, F32)


def flux_z_kernel(count, own_count, f_ref, zt_ref, acc_ref, src_ref, table_ref, *refs):
    layers, (out_hbm, impulse_ref) = refs[:count], refs[count : count + 2]
    ext, left, right, back, out_ref, sems = refs[count + 2 :]
    flags = place_flags()
    place = flags[9] * own_count
    loads = jnp.broadcast_to(table_ref[pl.ds(place // 128, 1), :], (8, 128))
    loads = pltpu.roll(loads, (128 - place % 128) % 128, 1)
    impulse_ref[...] = loads[:1, :own_count] * (1.0 / (PATCH * PATCH))
    low3, low = half_lanes((3, 128)), half_lanes((64, 128))

    def got(c, second):
        x = layers[0][pl.ds(c * 3, 3), :]
        if count == 2:
            x = jnp.where(second, layers[1][pl.ds(c * 3, 3), :], x)
        return swap_halves(x)

    for c in range(COMPS):
        sign = -1.0 if c == 3 else 1.0
        own = zt_ref[pl.ds(c * 64, 64), :]
        first, last = own[:3], own[61:]
        mirror_lo = sign * jnp.concatenate([first[2:3], first[1:2], first[0:1]], axis=0)
        mirror_hi = sign * jnp.concatenate([last[2:3], last[1:2], last[0:1]], axis=0)
        below = jnp.where(flags[4], mirror_lo, got(c, flags[8] == 0))
        above = jnp.where(flags[5], mirror_hi, got(c, flags[8] == 1))
        ext[pl.ds(c * 72, 3), :] = jnp.where(low3, below, swap_halves(last))
        ext[pl.ds(c * 72 + 3, 64), :] = own
        ext[pl.ds(c * 72 + 67, 3), :] = jnp.where(low3, swap_halves(first), above)

    def line(c):
        return [ext[pl.ds(c * 72 + e, 8, stride=8), :] for e in range(14)]

    face_states(line, left, right, 9)

    def emit(c, z, change):
        back[pl.ds(c * 64 + z, 8, stride=8), :] = change

    line_changes(left, right, 9, 2, emit)
    copies = []
    for c in range(0, COMPS, 2):
        even, odd = back[pl.ds(c * 64, 64), :], back[pl.ds(c * 64 + 64, 64), :]
        t = jnp.concatenate(
            [jnp.where(low, even, swap_halves(odd)), jnp.where(low, swap_halves(even), odd)],
            axis=0,
        )
        at = pl.ds(c * 64, 128)
        change = acc_ref[at, :] + jnp.transpose(t)
        out_ref[at, :] = f_ref[at, :] - TIME_STEP * change + CHEM_STEP * src_ref[at, :]
        copies.append(pltpu.make_async_copy(out_ref.at[at], out_hbm.at[at], sems.at[c // 2]))
        copies[-1].start()
    for copy in copies:
        copy.wait()


def state_scratch():
    return [pltpu.VMEM((COMPS * 9 * 8, 128), F32)] * 2


def halo_scratch():
    return [pltpu.VMEM((COMPS * 24, 128), F32)] * 2


def token_shape(table):
    return jax.ShapeDtypeStruct(table.shape, F32)


def flux_x(recon, acc, layers, table):
    return pl.pallas_call(
        lambda *a: flux_x_kernel(len(layers), *a),
        out_shape=[jax.ShapeDtypeStruct(recon.shape, F32), token_shape(table)],
        in_specs=[VM] * (2 + len(layers)),
        out_specs=[VM] * 2,
        scratch_shapes=halo_scratch() + state_scratch(),
        compiler_params=GRANT,
        cost_estimate=cost(2),
        name="flux_x",
    )(recon, acc, *layers)


def flux_y(recon, layers, table):
    return pl.pallas_call(
        lambda *a: flux_y_kernel(len(layers), *a),
        out_shape=[jax.ShapeDtypeStruct(recon.shape, F32), token_shape(table)],
        in_specs=[VM] * (1 + len(layers)),
        out_specs=[VM] * 2,
        scratch_shapes=halo_scratch() + state_scratch(),
        compiler_params=GRANT,
        cost_estimate=cost(2),
        name="flux_y",
    )(recon, *layers)


def flux_z(fields, turned, acc, source, table, layers, own_count):
    return pl.pallas_call(
        lambda *a: flux_z_kernel(len(layers), own_count, *a),
        out_shape=[
            jax.ShapeDtypeStruct(fields.shape, F32),
            jax.ShapeDtypeStruct((1, own_count), F32),
        ],
        in_specs=[VM] * (5 + len(layers)),
        out_specs=[HBM, VM],
        scratch_shapes=[pltpu.VMEM((COMPS * 72, 128), F32)]
        + state_scratch()
        + [pltpu.VMEM(fields.shape, F32)] * 2
        + [pltpu.SemaphoreType.DMA((COMPS // 2,))],
        compiler_params=GRANT,
        cost_estimate=cost(3),
        name="flux_z",
    )(fields, turned, acc, source, table, *layers)


def swap(x, axis, second, outer=False):
    n = lax.axis_size(axis)
    pairs = [(i, i + 1) for i in range(int(second), n - 1, 2)]
    if outer:
        pairs.append((0, n - 1))
    return lax.ppermute(x, axis, [(a, b) for a, b in pairs] + [(b, a) for a, b in pairs])


def sum_over(table, axis, step=1):
    size = lax.axis_size(axis)
    if size & (size - 1):
        return lax.psum(table, axis)
    while step < size:
        table = table + lax.ppermute(table, axis, [(i, i ^ step) for i in range(size)])
        step *= 2
    return table


def join_table(rows, height):
    rows = rows[: 3 * height].astype(F32)
    return rows[:height] + rows[height : 2 * height] + rows[2 * height :]


def body(fields, reacting, panel_map, layer_one, layer_two, layer_three, layer_four):
    shape = fields.shape
    sizes = [lax.axis_size(a) for a in AXES]
    pair_x = sizes[0] == 2
    panels_all = 2 * (shape[1] * sizes[0] // PATCH) * (shape[3] * sizes[2] // PATCH)
    own = panels_all // (sizes[0] * sizes[1] * sizes[2])
    height = panels_all // 128
    slots = BAL * min(4, sizes[0])
    layer_rows, edge_rows = COMPS * 24, 40
    ride_y, ride_z = sizes[1] & (sizes[1] - 1) == 0, sizes[2] in (2, 4)

    flat = fields.reshape(-1, shape[3])
    panels, react = panel_map.reshape(-1, shape[3]), reacting.reshape(-1, shape[3])
    layers = (layer_one.T, layer_two, layer_three, layer_four)
    packed = pack(flat, panels, react, layers, height)
    flat, recon, y_first, y_second, table, react, one, two, three, four = packed
    y_got = [swap(y_first, "gy", 0)]
    if sizes[1] > 2:
        y_got.append(swap(y_second, "gy", 1))
    turned, *xs, z_first, z_second, token = turn(recon, pair_x, height)
    hidden, row_slot, hit, two_b, token_in = chem_in(recon, react, one, layer_two, slots, table)
    table = table + token + token_in
    if ride_y:
        table = table + join_table(y_got[0][layer_rows:], height)
        table = sum_over(table, "gy", 2)
    else:
        table = lax.psum(table, "gy")
    hidden, token = chem_mid(hidden, (two, two_b), three, table)
    table = table + token
    if pair_x:
        xs = [put_table(table, xs[0])]
    x_got = [swap(x, "gx", m) for m, x in enumerate(xs)]
    acc, token = flux_y(recon, y_got, table)
    if pair_x:
        table = table + join_table(x_got[0][layer_rows:], height)
    else:
        table = sum_over(table, "gx")
    table = table + token
    if not ride_z:
        table = sum_over(table, "gz")
    z_got = [swap(lax.dynamic_update_slice(z_first, table, (edge_rows, 0)), "gz", 0)]
    source, token = chem_out(hidden, four, row_slot, hit, table)
    if ride_z:
        table = table + z_got[0][edge_rows : edge_rows + height] + token
    if sizes[2] > 2:
        z_second = lax.dynamic_update_slice(z_second, table, (edge_rows, 0))
        z_got.append(swap(z_second, "gz", 1, ride_z))
        if ride_z:
            table = table + z_got[1][edge_rows : edge_rows + height]
    acc, token = flux_x(recon, acc, x_got, table)
    new, impulse = flux_z(flat, turned, acc, source, table + token, z_got, own)
    return new.reshape(shape), impulse.reshape(own)


def solution(mesh):
    return jax.shard_map(
        body,
        mesh=mesh,
        in_specs=(
            P(None, "gx", "gy", "gz"),
            P("gx", "gy", "gz"),
            P(None, "gx", "gz"),
            P(),
            P(),
            P(),
            P(),
        ),
        out_specs=(P(None, "gx", "gy", "gz"), P(("gx", "gy", "gz"))),
        check_vma=False,
    )
```

```python
import jax
import jax.numpy as jnp
from jax import lax
from jax.experimental import pallas as pl
from jax.experimental.pallas import tpu as pltpu
from jax.sharding import PartitionSpec as P


BAL = 64
COMPS = 12
PATCH = 8

HEAT_RATIO = 1.4
TIME_STEP = 0.1
CHEM_STEP = 0.25
WENO_EPS = 1e-06
EPS = WENO_EPS * 4.0 / 36.0
AXES = ("gx", "gy", "gz")
F32 = jnp.float32
BF16 = jnp.bfloat16
GRANT = pltpu.CompilerParams(vmem_limit_bytes=12 * 2**20)
VM = pl.BlockSpec(memory_space=pltpu.VMEM)
HBM = pl.BlockSpec(memory_space=pltpu.HBM)


def weno_line(v):
    n = len(v)
    d = [(v[j + 1] - v[j]) * (1.0 / 6.0) for j in range(n - 1)]
    d3 = [3.0 * x for x in d]
    q = {}
    for e in range(1, n - 1):
        s = d[e] - d[e - 1]
        q[e] = (13.0 / 3.0) * (s * s) + EPS
    upper, lower = {}, {}
    for e in range(2, n - 2):
        dm, dp = d[e - 1], d[e]
        t0 = d3[e - 1] - d[e - 2]
        t1 = dm + dp
        t2 = d3[e] - d[e + 1]
        b0 = q[e - 1] + t0 * t0
        b1 = q[e] + t1 * t1
        b2 = q[e + 1] + t2 * t2
        m01, m02, m12 = b0 * b1, b0 * b2, b1 * b2
        s01, s02, s12 = m01 * m01, m02 * m02, m12 * m12
        w1, w01, w12 = 6.0 * s02, 3.0 * s01, 3.0 * s12
        if e < n - 3:
            num = s12 * (t0 + t0 - dm) + w1 * (t1 + dp) + w01 * (t2 + dp)
            upper[e] = v[e] + num / (s12 + w1 + w01)
        if e > 2:
            num = s01 * (t2 + t2 - dp) + w1 * (t1 + dm) + w12 * (t0 + dm)
            lower[e] = v[e] - num / (s01 + w1 + w12)
    return upper, lower


def weno_one(v):
    d = [(v[j + 1] - v[j]) * (1.0 / 6.0) for j in range(4)]
    s = [d[j + 1] - d[j] for j in range(3)]
    q = [(13.0 / 3.0) * (x * x) + EPS for x in s]
    dm, dp = d[1], d[2]
    t0, t1, t2 = 3.0 * dm - d[0], dm + dp, 3.0 * dp - d[3]
    b0, b1, b2 = q[0] + t0 * t0, q[1] + t1 * t1, q[2] + t2 * t2
    m01, m02, m12 = b0 * b1, b0 * b2, b1 * b2
    w0, w1, w2 = m12 * m12, 6.0 * (m02 * m02), 3.0 * (m01 * m01)
    num = w0 * (t0 + t0 - dm) + w1 * (t1 + dp) + w2 * (t2 + dp)
    return v[2] + num / (w0 + w1 + w2)


def hllc(left, right, normal):
    n = 1 + normal

    def side(x):
        rho = jnp.exp(x[0])
        g = jnp.exp(0.5 * (x[4] - x[0]))
        h = g * g
        return rho, h, rho * h, (HEAT_RATIO**0.5) * g, x[n]

    rho_l, h_l, p_l, c_l, u_l = side(left)
    rho_r, h_r, p_r, c_r, u_r = side(right)
    s_l = jnp.minimum(u_l - c_l, u_r - c_r)
    s_r = jnp.maximum(u_l + c_l, u_r + c_r)
    m_l = rho_l * (s_l - u_l)
    m_r = rho_r * (s_r - u_r)
    s = (p_r - p_l + u_l * m_l - u_r * m_r) / (m_l - m_r)
    use_l = (s >= 0) | (s_l >= 0)
    pick = [jnp.where(use_l, a, b) for a, b in zip(left, right)]
    rho = jnp.where(use_l, rho_l, rho_r)
    h = jnp.where(use_l, h_l, h_r)
    p = jnp.where(use_l, p_l, p_r)
    wave = jnp.where(use_l, s_l, s_r)
    act = jnp.where(use_l, jnp.minimum(s_l, 0.0), jnp.maximum(s_r, 0.0))
    u = pick[n]
    rel = s - u
    ratio = rel / (wave - s)
    mass = rho * (u + act * ratio)
    k = rho * act * (1.0 + ratio) * rel
    square = pick[1] * pick[1] + pick[2] * pick[2] + pick[3] * pick[3]
    enthalpy = (1.0 / (HEAT_RATIO - 1.0) + 1.0) * h + 0.5 * square
    flux = [mass * x for x in pick]
    flux[0] = mass
    flux[n] = flux[n] + (p + k)
    flux[4] = enthalpy * mass + k * s
    return flux


def place_flags():
    sizes = [lax.axis_size(a) for a in AXES]
    index = [lax.axis_index(a) for a in AXES]
    place = (index[0] * sizes[1] + index[1]) * sizes[2] + index[2]
    flags = [f for i, n in zip(index, sizes) for f in (i == 0, i == n - 1)]
    return flags + [lax.rem(i, 2) for i in index] + [place]


def rows8(index):
    return pl.ds(pl.multiple_of(index * 8, 8), 8)


def face_states(load_line, left_ref, right_ref, faces):
    def one(c, carry):
        upper, lower = weno_line(load_line(c))
        for f in range(faces):
            left_ref[rows8(c * faces + f), :] = upper[f + 2]
            right_ref[rows8(c * faces + f), :] = lower[f + 3]
        return carry

    lax.fori_loop(0, COMPS, one, 0)


def line_changes(left_ref, right_ref, faces, normal, emit):
    before = None
    for f in range(faces):
        left = [left_ref[pl.ds((c * faces + f) * 8, 8), :] for c in range(COMPS)]
        right = [right_ref[pl.ds((c * faces + f) * 8, 8), :] for c in range(COMPS)]
        flux = hllc(left, right, normal)
        if before is not None:
            for c in range(COMPS):
                emit(c, f - 1, flux[c] - before[c])
        before = flux


def half_lanes(shape):
    return lax.broadcasted_iota(jnp.int32, shape, 1) < 64


def swap_halves(x):
    return pltpu.roll(x, 64, 1)


def split3(x):
    hi = x.astype(BF16).astype(F32)
    mid = (x - hi).astype(BF16).astype(F32)
    return hi, mid, x - hi - mid


def fetch(source, target, sem, parts=1):
    step = -(-source.shape[0] // (parts * 16)) * 16
    for start in range(0, source.shape[0], step):
        rows = pl.ds(start, min(step, source.shape[0] - start))
        pltpu.make_async_copy(source.at[rows], target.at[rows], sem).start()
    return pltpu.make_async_copy(source, target, sem).wait


def pack_kernel(*refs):
    f_hbm, map_hbm, *sources = refs[:7]
    f_ref, r_ref, y1_ref, y2_ref, table_ref, *kept = refs[7:17]
    buf, map_ref, sems = refs[17:]
    pairs = [(f_hbm, f_ref, 8), (map_hbm, map_ref, 1)]
    pairs += list(zip(sources, kept, (1, 1, 8, 4, 1)))
    waits = [fetch(a, b, sems.at[i], parts) for i, (a, b, parts) in enumerate(pairs)]
    flags = place_flags()
    waits[0]()
    for x in range(8):
        def at(c):
            return f_ref[pl.ds(c * 64 + x * 8, 8), :]

        rho = at(0)
        inv = 1.0 / rho
        u = [at(c) * inv for c in (1, 2, 3)]
        p = (HEAT_RATIO - 1.0) * (
            at(4) - 0.5 * rho * (u[0] * u[0] + u[1] * u[1] + u[2] * u[2])
        )
        out = [jnp.log(rho)] + u + [jnp.log(p)] + [at(c) * inv for c in range(5, COMPS)]
        for c in range(COMPS):
            r_ref[pl.ds(c * 64 + x * 8, 8), :] = out[c]
    pushes = []
    for wall in range(2):
        rows = (0, 1, 2) if wall == 0 else (7, 6, 5)
        state = []
        for c in (0, 2, 4):
            a = [r_ref[pl.ds(c * 64 + y, 8, stride=8), :] for y in rows]
            sign = -1.0 if c == 2 else 1.0
            state.append(weno_one([a[2], a[1], a[0], sign * a[0], sign * a[1]]))
        rho = jnp.exp(state[0])
        p = jnp.exp(state[2])
        out_speed = -state[1] if wall == 0 else state[1]
        speed = jnp.abs(out_speed) + jnp.sqrt(HEAT_RATIO * p / rho)
        push = p + rho * out_speed * (out_speed + speed)
        x = jnp.where(flags[2 + wall], push, 0.0)
        for s in (1, 2, 4):
            x = x + pltpu.roll(x, 128 - s, 1)
        for s in (1, 2):
            x = x + pltpu.roll(x, 8 - s, 0)
        pushes.append(x)
    waits[1]()
    ids = map_ref[...].astype(F32)
    tall = jnp.concatenate(pushes + [ids, jnp.zeros((96, 128), F32)], axis=0)
    buf[...] = jnp.transpose(tall)
    groups = [buf[pl.ds(64 * g, 8, stride=8), :] for g in range(2)]
    lane = lax.broadcasted_iota(jnp.int32, (8, 128), 1).astype(F32)
    columns = []
    for g in groups:
        for col in (0, 4, 8, 12):
            columns.append(
                (
                    jnp.broadcast_to(g[:, col : col + 1], (8, 128)),
                    jnp.broadcast_to(g[:, 16 + col : 17 + col], (8, 128)),
                )
            )
    table = []
    for j in range(table_ref.shape[0]):
        total = jnp.zeros((8, 128), F32)
        for load, panel in columns:
            total = total + jnp.where(panel == lane + 128.0 * j, load, 0.0)
        table.append(jnp.sum(total, axis=0, keepdims=True))
        table_ref[pl.ds(j, 1), :] = table[j]
    for c in range(0, COMPS, 2):
        def row(i, y):
            return r_ref[pl.ds((c + i) * 64 + y, 8, stride=8), :]

        lo = jnp.concatenate([row(i, y) for i in (0, 1) for y in range(3)], axis=0)
        hi = jnp.concatenate([row(i, y) for i in (0, 1) for y in range(5, 8)], axis=0)
        store_layers((y1_ref, y2_ref), c, lo, hi, flags[7])
    rows = y1_ref.shape[0] - COMPS * 24
    pieces = [piece[j] for piece in zip(*map(split3, table)) for j in range(len(table))]
    if rows > len(pieces):
        pieces.append(jnp.zeros((rows - len(pieces), 128), F32))
    y1_ref[pl.ds(COMPS * 24, rows), :] = jnp.concatenate(pieces, axis=0).astype(BF16)
    for wait in waits[2:]:
        wait()


def store_layers(refs, c, lo, hi, parity):
    for m, ref in enumerate(refs):
        ref[pl.ds(c * 24, 48), :] = jnp.where(parity == m, hi, lo).astype(BF16)


def put_table_kernel(table_ref, x_ref, out_ref):
    start = COMPS * 24
    rows = x_ref.shape[0] - start
    pieces = list(split3(table_ref[...]))
    used = 3 * table_ref.shape[0]
    if rows > used:
        pieces.append(jnp.zeros((rows - used, 128), F32))
    out_ref[pl.ds(start, rows), :] = jnp.concatenate(pieces, axis=0).astype(BF16)


def put_table(table, x):
    return pl.pallas_call(
        put_table_kernel,
        out_shape=jax.ShapeDtypeStruct(x.shape, x.dtype),
        in_specs=[VM] * 2,
        out_specs=VM,
        input_output_aliases={1: 0},
        compiler_params=GRANT,
        cost_estimate=cost(0.2),
        name="put_table",
    )(table, x)


def in_hbm(x):
    return pltpu.with_memory_space_constraint(x, pltpu.HBM)


def load_rows(height):
    return -(-3 * height // 16) * 16


def pack(fields, panels, react, layers, height):
    whole = jax.ShapeDtypeStruct((COMPS * 64, 128), F32)
    outs = [whole, whole]
    outs.append(jax.ShapeDtypeStruct((COMPS * 24 + load_rows(height), 128), BF16))
    outs.append(jax.ShapeDtypeStruct((COMPS * 24, 128), BF16))
    outs.append(jax.ShapeDtypeStruct((height, 128), F32))
    one, two, three, four = layers
    kept = [jax.ShapeDtypeStruct(x.shape, x.dtype) for x in (react, one, two, three, four)]
    outs += kept
    return pl.pallas_call(
        pack_kernel,
        out_shape=outs,
        in_specs=[HBM] * 7,
        out_specs=[VM] * len(outs),
        scratch_shapes=[
            pltpu.VMEM((128, 128), F32),
            pltpu.VMEM(panels.shape, jnp.int32),
            pltpu.SemaphoreType.DMA((7,)),
        ],
        compiler_params=GRANT,
        cost_estimate=cost(2),
        name="pack",
    )(*map(in_hbm, (fields, panels, react, *layers)))


def turn_kernel(pair_x, r_ref, zt_ref, *refs):
    x_refs, (z1_ref, z2_ref, token) = refs[: 2 - pair_x], refs[2 - pair_x :]
    z_refs = (z1_ref, z2_ref)
    flags = place_flags()
    for c in range(0, COMPS, 2):
        lo = jnp.concatenate([r_ref[pl.ds((c + i) * 64, 24), :] for i in (0, 1)], axis=0)
        hi = jnp.concatenate([r_ref[pl.ds((c + i) * 64 + 40, 24), :] for i in (0, 1)], axis=0)
        store_layers(x_refs, c, lo, hi, flags[6])
    low = half_lanes((64, 128))
    for c in range(0, COMPS, 2):
        t = jnp.transpose(r_ref[pl.ds(c * 64, 128), :])
        top, bottom = t[:64], t[64:]
        even = jnp.where(low, top, swap_halves(bottom))
        odd = jnp.where(low, swap_halves(top), bottom)
        for i, x in ((0, even), (1, odd)):
            zt_ref[pl.ds((c + i) * 64, 64), :] = x
            for m, ref in enumerate(z_refs):
                up = flags[8] == m
                ref[pl.ds((c + i) * 3, 3), :] = jnp.where(up, x[61:], x[:3])
    for ref, start in [(x, COMPS * 24) for x in x_refs] + [(z, COMPS * 3) for z in z_refs]:
        if ref.shape[0] > start:
            ref[pl.ds(start, ref.shape[0] - start), :] = jnp.zeros(
                (ref.shape[0] - start, 128), ref.dtype
            )
    token[...] = jnp.zeros(token.shape, F32)


def turn(recon, pair_x, height):
    layer_x = jax.ShapeDtypeStruct((COMPS * 24 + (load_rows(height) if pair_x else 0), 128), BF16)
    edge = jax.ShapeDtypeStruct((40 + -(-height // 8) * 8, 128), F32)
    outs = [jax.ShapeDtypeStruct(recon.shape, F32)] + [layer_x] * (2 - pair_x) + [edge] * 2
    outs.append(jax.ShapeDtypeStruct((height, 128), F32))
    return pl.pallas_call(
        lambda *a: turn_kernel(int(pair_x), *a),
        out_shape=outs,
        in_specs=[VM],
        out_specs=[VM] * len(outs),
        compiler_params=GRANT,
        cost_estimate=cost(1),
        name="turn",
    )(recon)


def cost(us):
    return pl.CostEstimate(flops=0, transcendentals=0, bytes_accessed=int(us * 3.5e6))


def dot(a, b):
    return jnp.dot(a, b, preferred_element_type=F32)


def iota(shape, dim):
    return lax.broadcasted_iota(jnp.int32, shape, dim)


def where1(mask):
    return jnp.where(mask, 1.0, 0.0).astype(BF16)


def chem_in_kernel(
    slots, r_ref, react_ref, w1_ref, h_ref, row_ref, hit_ref, token
):
    react = react_ref[...].astype(F32)
    react_b = react.astype(BF16)
    upper = where1(iota((128, 128), 0) <= iota((128, 128), 1))
    within = dot(react_b, upper)
    count = dot(react_b, jnp.ones((128, 128), BF16))
    below = where1(iota((64, 64), 1) < iota((64, 64), 0))
    offset = dot(below, count.astype(BF16))
    rank = (react * (within + offset)).astype(BF16)
    slot_lane = iota((64, slots), 1).astype(F32)
    off_col, cnt_col = offset[:, :1], count[:, :1]
    row_ref[...] = where1((slot_lane >= off_col) & (slot_lane < off_col + cnt_col))
    nt = (((1,), (1,)), ((), ()))
    count_row = lax.dot_general(
        jnp.ones((8, 128), BF16), react_b, nt, preferred_element_type=F32
    )
    offset_row = lax.dot_general(
        count_row.astype(BF16), below, nt, preferred_element_type=F32
    )
    slot_sub = iota((slots, 64), 0).astype(F32)
    slot_row = where1(
        (slot_sub >= offset_row[:1]) & (slot_sub < offset_row[:1] + count_row[:1])
    )
    lane_hit = dot(slot_row, rank) == iota((slots, 128), 0).astype(F32) + 1.0
    hit_ref[...] = where1(lane_hit)
    feat = jnp.zeros((slots, 128), F32)
    for c in range(COMPS):
        rows = dot(slot_row, r_ref[pl.ds(c * 64, 64), :].astype(BF16))
        hit = jnp.where(lane_hit, rows, 0.0).astype(BF16)
        feat = feat + dot(hit, where1(iota((128, 128), 1) == c))
    feat = jnp.transpose(feat)[:COMPS].astype(BF16)
    tn = (((0,), (0,)), ((), ()))
    one = lax.dot_general(w1_ref[...], feat, tn, preferred_element_type=F32)
    h_ref[...] = jax.nn.gelu(one).astype(BF16)
    token[...] = jnp.zeros(token.shape, F32)


def chem_in(recon, react, layer_one, slots, table):
    return pl.pallas_call(
        lambda *a: chem_in_kernel(slots, *a),
        out_shape=[
            jax.ShapeDtypeStruct((layer_one.shape[1], slots), BF16),
            jax.ShapeDtypeStruct((64, slots), BF16),
            jax.ShapeDtypeStruct((slots, 128), BF16),
            token_shape(table),
        ],
        in_specs=[VM] * 3,
        out_specs=[VM] * 4,
        compiler_params=GRANT,
        cost_estimate=cost(1),
        name="chem_in",
    )(recon, react, layer_one)


def chem_mid_kernel(h_ref, w2_ref, w3_ref, out_ref, token):
    two = jax.nn.gelu(dot(w2_ref[...], h_ref[...])).astype(BF16)
    out_ref[...] = jax.nn.gelu(dot(w3_ref[...], two)).astype(BF16)
    token[...] = jnp.zeros(token.shape, F32)


def chem_mid(hidden, layer_two, layer_three, table):
    return pl.pallas_call(
        chem_mid_kernel,
        out_shape=[
            jax.ShapeDtypeStruct((layer_three.shape[0], hidden.shape[1]), BF16),
            token_shape(table),
        ],
        in_specs=[VM] * 3,
        out_specs=[VM] * 2,
        compiler_params=GRANT,
        cost_estimate=cost(2),
        name="chem_mid",
    )(hidden, layer_two, layer_three)


def chem_out_kernel(h_ref, w4_ref, row_ref, hit_ref, out_ref, token):
    rates = dot(w4_ref[...], h_ref[...])
    slots = rates.shape[1]
    rates = jnp.concatenate([rates, jnp.zeros((128 - COMPS, slots), F32)], axis=0)
    rates_t = jnp.transpose(rates).astype(BF16)
    hit, row_slot = hit_ref[...].astype(F32), row_ref[...]
    for c in range(COMPS):
        spread = hit * dot(rates_t, where1(iota((128, 128), 0) == c))
        out_ref[pl.ds(c * 64, 64), :] = dot(row_slot, spread.astype(BF16))
    token[...] = jnp.zeros(token.shape, F32)


def chem_out(hidden, layer_four, row_slot, hit, table):
    return pl.pallas_call(
        chem_out_kernel,
        out_shape=[jax.ShapeDtypeStruct((COMPS * 64, 128), F32), token_shape(table)],
        in_specs=[VM] * 4,
        out_specs=[VM] * 2,
        compiler_params=GRANT,
        cost_estimate=cost(1),
        name="chem_out",
    )(hidden, layer_four, row_slot, hit)


def halo_lines(refs, scratch, own, sign_comp, at_wall, order, second):
    for c in range(0, COMPS, 2):
        block = refs[0][pl.ds(c * 24, 48), :].astype(F32)
        if len(refs) == 2:
            block = jnp.where(second, refs[1][pl.ds(c * 24, 48), :].astype(F32), block)
        for i in (0, 1):
            for k in range(3):
                mirror = own(c + i, order[k])
                if c + i == sign_comp:
                    mirror = -mirror
                got = block[(i * 3 + k) * 8 : (i * 3 + k + 1) * 8]
                scratch[pl.ds(((c + i) * 3 + k) * 8, 8), :] = jnp.where(at_wall, mirror, got)


def flux_x_kernel(count, f_ref, r_ref, acc_ref, src_ref, *refs):
    flags = place_flags()
    layers, (out_hbm, lo_s, hi_s, left, right, out_ref, sems) = refs[:count], refs[count:]

    def own(c, x):
        return r_ref[pl.ds(c * 64 + x * 8, 8), :]

    halo_lines(layers, lo_s, own, 1, flags[0], (2, 1, 0), flags[6] == 0)
    halo_lines(layers, hi_s, own, 1, flags[1], (7, 6, 5), flags[6] == 1)

    def line(c):
        return (
            [lo_s[rows8(c * 3 + k), :] for k in range(3)]
            + [r_ref[rows8(c * 8 + x), :] for x in range(8)]
            + [hi_s[rows8(c * 3 + k), :] for k in range(3)]
        )

    face_states(line, left, right, 9)
    copies = []

    def emit(c, x, change):
        at, plane = pl.ds(c * 64 + x * 8, 8), pl.ds(x * 8, 8)
        new = f_ref[at, :] - TIME_STEP * (acc_ref[at, :] + change) + CHEM_STEP * src_ref[at, :]
        out_ref[c, plane, :] = new
        if c == COMPS - 1:
            here, there = out_ref.at[:, plane], out_hbm.at[:, plane]
            copies.append(pltpu.make_async_copy(here, there, sems.at[x]))
            copies[-1].start()

    line_changes(left, right, 9, 0, emit)
    for copy in copies:
        copy.wait()


def flux_y_kernel(count, r_ref, *refs):
    flags = place_flags()
    layers, (out_ref, token, lo_s, hi_s, left, right) = refs[:count], refs[count:]

    def own(c, y):
        return r_ref[pl.ds(c * 64 + y, 8, stride=8), :]

    halo_lines(layers, lo_s, own, 2, flags[2], (2, 1, 0), flags[7] == 0)
    halo_lines(layers, hi_s, own, 2, flags[3], (7, 6, 5), flags[7] == 1)

    def line(c):
        return (
            [lo_s[rows8(c * 3 + k), :] for k in range(3)]
            + [r_ref[pl.ds(c * 64 + y, 8, stride=8), :] for y in range(8)]
            + [hi_s[rows8(c * 3 + k), :] for k in range(3)]
        )

    face_states(line, left, right, 9)

    def emit(c, y, change):
        out_ref[pl.ds(c * 64 + y, 8, stride=8), :] = change

    line_changes(left, right, 9, 1, emit)
    token[...] = jnp.zeros(token.shape, F32)


def flux_z_kernel(count, zt_ref, acc_ref, *refs):
    flags = place_flags()
    layers, (out_ref, token, ext, left, right, back) = refs[:count], refs[count:]
    low3, low = half_lanes((3, 128)), half_lanes((64, 128))

    def got(c, second):
        x = layers[0][pl.ds(c * 3, 3), :]
        if count == 2:
            x = jnp.where(second, layers[1][pl.ds(c * 3, 3), :], x)
        return swap_halves(x)

    for c in range(COMPS):
        sign = -1.0 if c == 3 else 1.0
        own = zt_ref[pl.ds(c * 64, 64), :]
        first, last = own[:3], own[61:]
        mirror_lo = sign * jnp.concatenate([first[2:3], first[1:2], first[0:1]], axis=0)
        mirror_hi = sign * jnp.concatenate([last[2:3], last[1:2], last[0:1]], axis=0)
        below = jnp.where(flags[4], mirror_lo, got(c, flags[8] == 0))
        above = jnp.where(flags[5], mirror_hi, got(c, flags[8] == 1))
        ext[pl.ds(c * 72, 3), :] = jnp.where(low3, below, swap_halves(last))
        ext[pl.ds(c * 72 + 3, 64), :] = own
        ext[pl.ds(c * 72 + 67, 3), :] = jnp.where(low3, swap_halves(first), above)

    def line(c):
        return [ext[pl.ds(c * 72 + e, 8, stride=8), :] for e in range(14)]

    face_states(line, left, right, 9)

    def emit(c, z, change):
        back[pl.ds(c * 64 + z, 8, stride=8), :] = change

    line_changes(left, right, 9, 2, emit)
    for c in range(0, COMPS, 2):
        even, odd = back[pl.ds(c * 64, 64), :], back[pl.ds(c * 64 + 64, 64), :]
        t = jnp.concatenate(
            [jnp.where(low, even, swap_halves(odd)), jnp.where(low, swap_halves(even), odd)],
            axis=0,
        )
        at = pl.ds(c * 64, 128)
        out_ref[at, :] = acc_ref[at, :] + jnp.transpose(t)
    token[...] = jnp.zeros(token.shape, F32)


def impulse_kernel(own, table_ref, got_ref, out_ref):
    place = place_flags()[9] * own
    row = pl.ds(place // 128, 1)
    loads = jnp.broadcast_to(table_ref[row, :] + got_ref[row, :], (8, 128))
    loads = pltpu.roll(loads, (128 - place % 128) % 128, 1)
    out_ref[...] = loads[:1, :own] * (1.0 / (PATCH * PATCH))


def own_impulse(table, got, own):
    return pl.pallas_call(
        lambda *a: impulse_kernel(own, *a),
        out_shape=jax.ShapeDtypeStruct((1, own), F32),
        in_specs=[VM] * 2,
        out_specs=VM,
        compiler_params=GRANT,
        cost_estimate=cost(0.5),
        name="impulse",
    )(table, got)


def state_scratch():
    return [pltpu.VMEM((COMPS * 9 * 8, 128), F32)] * 2


def halo_scratch():
    return [pltpu.VMEM((COMPS * 24, 128), F32)] * 2


def token_shape(table):
    return jax.ShapeDtypeStruct(table.shape, F32)


def flux_x(fields, recon, acc, source, layers):
    return pl.pallas_call(
        lambda *a: flux_x_kernel(len(layers), *a),
        out_shape=jax.ShapeDtypeStruct((COMPS, 64, 128), F32),
        in_specs=[VM] * (4 + len(layers)),
        out_specs=HBM,
        scratch_shapes=halo_scratch()
        + state_scratch()
        + [pltpu.VMEM((COMPS, 64, 128), F32), pltpu.SemaphoreType.DMA((8,))],
        compiler_params=GRANT,
        cost_estimate=cost(2),
        name="flux_x",
    )(fields, recon, acc, source, *layers)


def flux_y(recon, layers, table):
    return pl.pallas_call(
        lambda *a: flux_y_kernel(len(layers), *a),
        out_shape=[jax.ShapeDtypeStruct(recon.shape, F32), token_shape(table)],
        in_specs=[VM] * (1 + len(layers)),
        out_specs=[VM] * 2,
        scratch_shapes=halo_scratch() + state_scratch(),
        compiler_params=GRANT,
        cost_estimate=cost(2),
        name="flux_y",
    )(recon, *layers)


def flux_z(turned, acc, layers, table):
    return pl.pallas_call(
        lambda *a: flux_z_kernel(len(layers), *a),
        out_shape=[jax.ShapeDtypeStruct(acc.shape, F32), token_shape(table)],
        in_specs=[VM] * (2 + len(layers)),
        out_specs=[VM] * 2,
        scratch_shapes=[pltpu.VMEM((COMPS * 72, 128), F32)]
        + state_scratch()
        + [pltpu.VMEM(acc.shape, F32)],
        compiler_params=GRANT,
        cost_estimate=cost(2),
        name="flux_z",
    )(turned, acc, *layers)


def swap(x, axis, second, outer=False):
    n = lax.axis_size(axis)
    pairs = [(i, i + 1) for i in range(int(second), n - 1, 2)]
    if outer:
        pairs.append((0, n - 1))
    return lax.ppermute(x, axis, [(a, b) for a, b in pairs] + [(b, a) for a, b in pairs])


def swap_inner(x, axis, other):
    n, m = lax.axis_size(axis), lax.axis_size(other)
    if m % 2 or n % 2:
        return swap(x, axis, 1)
    pairs = []
    for i in range(n):
        for j in range(m):
            end = i in (0, n - 1)
            to = (i, j ^ 1) if end else (i + 1 if i % 2 else i - 1, j)
            pairs.append((i * m + j, to[0] * m + to[1]))
    return lax.ppermute(x, (axis, other), pairs)


def sum_over(table, axis, step=1):
    size = lax.axis_size(axis)
    if size & (size - 1):
        return lax.psum(table, axis)
    while step < size:
        table = table + lax.ppermute(table, axis, [(i, i ^ step) for i in range(size)])
        step *= 2
    return table


def join_table(rows, height):
    rows = rows[: 3 * height].astype(F32)
    return rows[:height] + rows[height : 2 * height] + rows[2 * height :]


def body(fields, reacting, panel_map, layer_one, layer_two, layer_three, layer_four):
    shape = fields.shape
    sizes = [lax.axis_size(a) for a in AXES]
    pair_x = sizes[0] == 2
    panels_all = 2 * (shape[1] * sizes[0] // PATCH) * (shape[3] * sizes[2] // PATCH)
    own = panels_all // (sizes[0] * sizes[1] * sizes[2])
    height = panels_all // 128
    slots = BAL * min(4, sizes[0])
    layer_rows, edge_rows = COMPS * 24, 40
    ride_y, ride_z = sizes[1] & (sizes[1] - 1) == 0, sizes[2] in (2, 4)

    flat = fields.reshape(-1, shape[3])
    panels, react = panel_map.reshape(-1, shape[3]), reacting.reshape(-1, shape[3])
    layers = (layer_one.T, layer_two, layer_three, layer_four)
    packed = pack(flat, panels, react, layers, height)
    flat, recon, y_first, y_second, table, react, one, two, three, four = packed
    y_got = [swap(y_first, "gy", 0)]
    if sizes[1] > 2:
        y_got.append(swap_inner(y_second, "gy", "gz"))
    turned, *xs, z_first, z_second, token = turn(recon, pair_x, height)
    hidden, row_slot, hit, token_in = chem_in(recon, react, one, slots, table)
    table = table + token + token_in
    if ride_y:
        table = table + join_table(y_got[0][layer_rows:], height)
    if not ride_z:
        table = sum_over(table, "gz")
    z_got = [swap(lax.dynamic_update_slice(z_first, table, (edge_rows, 0)), "gz", 0)]
    hidden, token = chem_mid(hidden, two, three, table)
    if ride_z:
        table = table + z_got[0][edge_rows : edge_rows + height] + token
    if sizes[2] > 2:
        z_second = lax.dynamic_update_slice(z_second, table, (edge_rows, 0))
        z_got.append(swap(z_second, "gz", 1, ride_z))
        if ride_z:
            table = table + z_got[1][edge_rows : edge_rows + height]
    acc, token = flux_y(recon, y_got, table)
    table = table + token
    if pair_x:
        xs = [put_table(table, xs[0])]
    x_got = [swap(x, "gx", m) for m, x in enumerate(xs)]
    acc, token = flux_z(turned, acc, z_got, table)
    source, token_out = chem_out(hidden, four, row_slot, hit, table)
    table = table + token + token_out
    if pair_x:
        table = table + join_table(x_got[0][layer_rows:], height)
    else:
        table = sum_over(table, "gx")
    rest = jnp.zeros_like(table)
    if not ride_y:
        table = lax.psum(table, "gy")
    elif sizes[1] > 2:
        table = sum_over(table, "gy", 4)
        pairs = [(i, i ^ 2) for i in range(sizes[1])]
        rest = lax.ppermute(table, "gy", pairs)
    new = flux_x(flat, recon, acc, source, x_got)
    return new.reshape(shape), own_impulse(table, rest, own).reshape(own)


def solution(mesh):
    return jax.shard_map(
        body,
        mesh=mesh,
        in_specs=(
            P(None, "gx", "gy", "gz"),
            P("gx", "gy", "gz"),
            P(None, "gx", "gz"),
            P(),
            P(),
            P(),
            P(),
        ),
        out_specs=(P(None, "gx", "gy", "gz"), P(("gx", "gy", "gz"))),
        check_vma=False,
    )
```

```python
import jax
import jax.numpy as jnp
from jax import lax
from jax.experimental import pallas as pl
from jax.experimental.pallas import tpu as pltpu
from jax.sharding import PartitionSpec as P


BAL = 64
COMPS = 12
PATCH = 8

HEAT_RATIO = 1.4
TIME_STEP = 0.1
CHEM_STEP = 0.25
WENO_EPS = 1e-06
EPS = WENO_EPS * 4.0 / 36.0
AXES = ("gx", "gy", "gz")
F32 = jnp.float32
BF16 = jnp.bfloat16
GRANT = pltpu.CompilerParams(vmem_limit_bytes=12 * 2**20)
VM = pl.BlockSpec(memory_space=pltpu.VMEM)
HBM = pl.BlockSpec(memory_space=pltpu.HBM)


def weno_line(v, first, last):
    n = len(v)
    low, high = max(first - 2, 0), min(last + 2, n - 1)
    d = {j: (v[j + 1] - v[j]) * (1.0 / 6.0) for j in range(low, high)}
    d3 = {j: 3.0 * d[j] for j in range(low + 1, high - 1)}
    q = {}
    for e in range(low + 1, high):
        s = d[e] - d[e - 1]
        q[e] = (13.0 / 3.0) * (s * s) + EPS
    upper, lower = {}, {}
    for e in range(first, last + 1):
        dm, dp = d[e - 1], d[e]
        t0 = d3[e - 1] - d[e - 2]
        t1 = dm + dp
        t2 = d3[e] - d[e + 1]
        b0 = q[e - 1] + t0 * t0
        b1 = q[e] + t1 * t1
        b2 = q[e + 1] + t2 * t2
        m01, m02, m12 = b0 * b1, b0 * b2, b1 * b2
        s01, s02, s12 = m01 * m01, m02 * m02, m12 * m12
        w1, w01, w12 = 6.0 * s02, 3.0 * s01, 3.0 * s12
        if e < n - 3:
            num = s12 * (t0 + t0 - dm) + w1 * (t1 + dp) + w01 * (t2 + dp)
            upper[e] = v[e] + num / (s12 + w1 + w01)
        if e > 2:
            num = s01 * (t2 + t2 - dp) + w1 * (t1 + dm) + w12 * (t0 + dm)
            lower[e] = v[e] - num / (s01 + w1 + w12)
    return upper, lower


def weno_one(v):
    d = [(v[j + 1] - v[j]) * (1.0 / 6.0) for j in range(4)]
    s = [d[j + 1] - d[j] for j in range(3)]
    q = [(13.0 / 3.0) * (x * x) + EPS for x in s]
    dm, dp = d[1], d[2]
    t0, t1, t2 = 3.0 * dm - d[0], dm + dp, 3.0 * dp - d[3]
    b0, b1, b2 = q[0] + t0 * t0, q[1] + t1 * t1, q[2] + t2 * t2
    m01, m02, m12 = b0 * b1, b0 * b2, b1 * b2
    w0, w1, w2 = m12 * m12, 6.0 * (m02 * m02), 3.0 * (m01 * m01)
    num = w0 * (t0 + t0 - dm) + w1 * (t1 + dp) + w2 * (t2 + dp)
    return v[2] + num / (w0 + w1 + w2)


def hllc(left, right, normal):
    n = 1 + normal

    def side(x):
        rho = jnp.exp(x[0])
        g = jnp.exp(0.5 * (x[4] - x[0]))
        h = g * g
        return rho, h, rho * h, (HEAT_RATIO**0.5) * g, x[n]

    rho_l, h_l, p_l, c_l, u_l = side(left)
    rho_r, h_r, p_r, c_r, u_r = side(right)
    s_l = jnp.minimum(u_l - c_l, u_r - c_r)
    s_r = jnp.maximum(u_l + c_l, u_r + c_r)
    m_l = rho_l * (s_l - u_l)
    m_r = rho_r * (s_r - u_r)
    s = (p_r - p_l + u_l * m_l - u_r * m_r) / (m_l - m_r)
    use_l = (s >= 0) | (s_l >= 0)
    pick = [jnp.where(use_l, a, b) for a, b in zip(left, right)]
    rho = jnp.where(use_l, rho_l, rho_r)
    h = jnp.where(use_l, h_l, h_r)
    p = jnp.where(use_l, p_l, p_r)
    wave = jnp.where(use_l, s_l, s_r)
    act = jnp.where(use_l, jnp.minimum(s_l, 0.0), jnp.maximum(s_r, 0.0))
    u = pick[n]
    rel = s - u
    ratio = rel / (wave - s)
    mass = rho * (u + act * ratio)
    k = rho * act * (1.0 + ratio) * rel
    square = pick[1] * pick[1] + pick[2] * pick[2] + pick[3] * pick[3]
    enthalpy = (1.0 / (HEAT_RATIO - 1.0) + 1.0) * h + 0.5 * square
    flux = [mass * x for x in pick]
    flux[0] = mass
    flux[n] = flux[n] + (p + k)
    flux[4] = enthalpy * mass + k * s
    return flux


def place_flags():
    sizes = [lax.axis_size(a) for a in AXES]
    index = [lax.axis_index(a) for a in AXES]
    place = (index[0] * sizes[1] + index[1]) * sizes[2] + index[2]
    flags = [f for i, n in zip(index, sizes) for f in (i == 0, i == n - 1)]
    return flags + [lax.rem(i, 2) for i in index] + [place]


def rows8(index):
    return pl.ds(pl.multiple_of(index * 8, 8), 8)


def face_states(load_line, left_ref, right_ref, faces, spans=((2, 11),)):
    def one(c, carry):
        line = load_line(c)
        for first, last in spans:
            upper, lower = weno_line(line, first, last)
            for e, x in upper.items():
                left_ref[rows8(c * faces + e - 2), :] = x
            for e, x in lower.items():
                right_ref[rows8(c * faces + e - 3), :] = x
        return carry

    lax.fori_loop(0, COMPS, one, 0)


def face_flux(left_ref, right_ref, faces, normal, f):
    left = [left_ref[pl.ds((c * faces + f) * 8, 8), :] for c in range(COMPS)]
    right = [right_ref[pl.ds((c * faces + f) * 8, 8), :] for c in range(COMPS)]
    return hllc(left, right, normal)


def line_changes(left_ref, right_ref, faces, normal, emit):
    before = None
    for f in range(faces):
        flux = face_flux(left_ref, right_ref, faces, normal, f)
        if before is not None:
            for c in range(COMPS):
                emit(c, f - 1, flux[c] - before[c])
        before = flux


def half_lanes(shape):
    return lax.broadcasted_iota(jnp.int32, shape, 1) < 64


def swap_halves(x):
    return pltpu.roll(x, 64, 1)


def split3(x):
    hi = x.astype(BF16).astype(F32)
    mid = (x - hi).astype(BF16).astype(F32)
    return hi, mid, x - hi - mid


def fetch(source, target, sem, parts=1):
    step = -(-source.shape[0] // (parts * 16)) * 16
    for start in range(0, source.shape[0], step):
        rows = pl.ds(start, min(step, source.shape[0] - start))
        pltpu.make_async_copy(source.at[rows], target.at[rows], sem).start()
    return pltpu.make_async_copy(source, target, sem).wait


def pack_kernel(*refs):
    f_hbm, map_hbm, *sources = refs[:7]
    f_ref, r_ref, y1_ref, y2_ref, table_ref, *kept = refs[7:17]
    buf, map_ref, sems = refs[17:]
    pairs = [(f_hbm, f_ref, 8), (map_hbm, map_ref, 1)]
    pairs += list(zip(sources, kept, (1, 1, 8, 4, 1)))
    waits = [fetch(a, b, sems.at[i], parts) for i, (a, b, parts) in enumerate(pairs)]
    flags = place_flags()
    waits[0]()
    for x in range(8):
        def at(c):
            return f_ref[pl.ds(c * 64 + x * 8, 8), :]

        rho = at(0)
        inv = 1.0 / rho
        u = [at(c) * inv for c in (1, 2, 3)]
        p = (HEAT_RATIO - 1.0) * (
            at(4) - 0.5 * rho * (u[0] * u[0] + u[1] * u[1] + u[2] * u[2])
        )
        out = [jnp.log(rho)] + u + [jnp.log(p)] + [at(c) * inv for c in range(5, COMPS)]
        for c in range(COMPS):
            r_ref[pl.ds(c * 64 + x * 8, 8), :] = out[c]
    pushes = []
    for wall in range(2):
        rows = (0, 1, 2) if wall == 0 else (7, 6, 5)
        state = []
        for c in (0, 2, 4):
            a = [r_ref[pl.ds(c * 64 + y, 8, stride=8), :] for y in rows]
            sign = -1.0 if c == 2 else 1.0
            state.append(weno_one([a[2], a[1], a[0], sign * a[0], sign * a[1]]))
        rho = jnp.exp(state[0])
        p = jnp.exp(state[2])
        out_speed = -state[1] if wall == 0 else state[1]
        speed = jnp.abs(out_speed) + jnp.sqrt(HEAT_RATIO * p / rho)
        push = p + rho * out_speed * (out_speed + speed)
        x = jnp.where(flags[2 + wall], push, 0.0)
        for s in (1, 2, 4):
            x = x + pltpu.roll(x, 128 - s, 1)
        for s in (1, 2):
            x = x + pltpu.roll(x, 8 - s, 0)
        pushes.append(x)
    waits[1]()
    ids = map_ref[...].astype(F32)
    tall = jnp.concatenate(pushes + [ids, jnp.zeros((96, 128), F32)], axis=0)
    buf[...] = jnp.transpose(tall)
    groups = [buf[pl.ds(64 * g, 8, stride=8), :] for g in range(2)]
    lane = lax.broadcasted_iota(jnp.int32, (8, 128), 1).astype(F32)
    columns = []
    for g in groups:
        for col in (0, 4, 8, 12):
            columns.append(
                (
                    jnp.broadcast_to(g[:, col : col + 1], (8, 128)),
                    jnp.broadcast_to(g[:, 16 + col : 17 + col], (8, 128)),
                )
            )
    table = []
    for j in range(table_ref.shape[0]):
        total = jnp.zeros((8, 128), F32)
        for load, panel in columns:
            total = total + jnp.where(panel == lane + 128.0 * j, load, 0.0)
        table.append(jnp.sum(total, axis=0, keepdims=True))
        table_ref[pl.ds(j, 1), :] = table[j]
    for c in range(0, COMPS, 2):
        def row(i, y):
            return r_ref[pl.ds((c + i) * 64 + y, 8, stride=8), :]

        lo = jnp.concatenate([row(i, y) for i in (0, 1) for y in range(3)], axis=0)
        hi = jnp.concatenate([row(i, y) for i in (0, 1) for y in range(5, 8)], axis=0)
        store_layers((y1_ref, y2_ref), c, lo, hi, flags[7])
    rows = y1_ref.shape[0] - COMPS * 24
    pieces = [piece[j] for piece in zip(*map(split3, table)) for j in range(len(table))]
    if rows > len(pieces):
        pieces.append(jnp.zeros((rows - len(pieces), 128), F32))
    y1_ref[pl.ds(COMPS * 24, rows), :] = jnp.concatenate(pieces, axis=0).astype(BF16)
    for wait in waits[2:]:
        wait()


def store_layers(refs, c, lo, hi, parity):
    for m, ref in enumerate(refs):
        ref[pl.ds(c * 24, 48), :] = jnp.where(parity == m, hi, lo).astype(BF16)


def put_table_kernel(table_ref, x_ref, out_ref):
    start = COMPS * 24
    rows = x_ref.shape[0] - start
    pieces = list(split3(table_ref[...]))
    used = 3 * table_ref.shape[0]
    if rows > used:
        pieces.append(jnp.zeros((rows - used, 128), F32))
    out_ref[pl.ds(start, rows), :] = jnp.concatenate(pieces, axis=0).astype(BF16)


def put_table(table, x):
    return pl.pallas_call(
        put_table_kernel,
        out_shape=jax.ShapeDtypeStruct(x.shape, x.dtype),
        in_specs=[VM] * 2,
        out_specs=VM,
        input_output_aliases={1: 0},
        compiler_params=GRANT,
        cost_estimate=cost(0.2),
        name="put_table",
    )(table, x)


def in_hbm(x):
    return pltpu.with_memory_space_constraint(x, pltpu.HBM)


def load_rows(height):
    return -(-3 * height // 16) * 16


def pack(fields, panels, react, layers, height):
    whole = jax.ShapeDtypeStruct((COMPS * 64, 128), F32)
    outs = [whole, whole]
    outs.append(jax.ShapeDtypeStruct((COMPS * 24 + load_rows(height), 128), BF16))
    outs.append(jax.ShapeDtypeStruct((COMPS * 24, 128), BF16))
    outs.append(jax.ShapeDtypeStruct((height, 128), F32))
    one, two, three, four = layers
    kept = [jax.ShapeDtypeStruct(x.shape, x.dtype) for x in (react, one, two, three, four)]
    outs += kept
    return pl.pallas_call(
        pack_kernel,
        out_shape=outs,
        in_specs=[HBM] * 7,
        out_specs=[VM] * len(outs),
        scratch_shapes=[
            pltpu.VMEM((128, 128), F32),
            pltpu.VMEM(panels.shape, jnp.int32),
            pltpu.SemaphoreType.DMA((7,)),
        ],
        compiler_params=GRANT,
        cost_estimate=cost(2),
        name="pack",
    )(*map(in_hbm, (fields, panels, react, *layers)))


def turn_kernel(pair_x, r_ref, zt_ref, *refs):
    x_refs, (z1_ref, z2_ref, token) = refs[: 2 - pair_x], refs[2 - pair_x :]
    z_refs = (z1_ref, z2_ref)
    flags = place_flags()
    for c in range(0, COMPS, 2):
        lo = jnp.concatenate([r_ref[pl.ds((c + i) * 64, 24), :] for i in (0, 1)], axis=0)
        hi = jnp.concatenate([r_ref[pl.ds((c + i) * 64 + 40, 24), :] for i in (0, 1)], axis=0)
        store_layers(x_refs, c, lo, hi, flags[6])
    low = half_lanes((64, 128))
    for c in range(0, COMPS, 2):
        t = jnp.transpose(r_ref[pl.ds(c * 64, 128), :])
        top, bottom = t[:64], t[64:]
        even = jnp.where(low, top, swap_halves(bottom))
        odd = jnp.where(low, swap_halves(top), bottom)
        for i, x in ((0, even), (1, odd)):
            zt_ref[pl.ds((c + i) * 64, 64), :] = x
            for m, ref in enumerate(z_refs):
                up = flags[8] == m
                ref[pl.ds((c + i) * 3, 3), :] = jnp.where(up, x[61:], x[:3])
    for ref, start in [(x, COMPS * 24) for x in x_refs] + [(z, COMPS * 3) for z in z_refs]:
        if ref.shape[0] > start:
            ref[pl.ds(start, ref.shape[0] - start), :] = jnp.zeros(
                (ref.shape[0] - start, 128), ref.dtype
            )
    token[...] = jnp.zeros(token.shape, F32)


def turn(recon, pair_x, height):
    layer_x = jax.ShapeDtypeStruct((COMPS * 24 + (load_rows(height) if pair_x else 0), 128), BF16)
    edge = jax.ShapeDtypeStruct((40 + -(-height // 8) * 8, 128), F32)
    outs = [jax.ShapeDtypeStruct(recon.shape, F32)] + [layer_x] * (2 - pair_x) + [edge] * 2
    outs.append(jax.ShapeDtypeStruct((height, 128), F32))
    return pl.pallas_call(
        lambda *a: turn_kernel(int(pair_x), *a),
        out_shape=outs,
        in_specs=[VM],
        out_specs=[VM] * len(outs),
        compiler_params=GRANT,
        cost_estimate=cost(1),
        name="turn",
    )(recon)


def cost(us):
    return pl.CostEstimate(flops=0, transcendentals=0, bytes_accessed=int(us * 3.5e6))


def dot(a, b):
    return jnp.dot(a, b, preferred_element_type=F32)


def iota(shape, dim):
    return lax.broadcasted_iota(jnp.int32, shape, dim)


def where1(mask):
    return jnp.where(mask, 1.0, 0.0).astype(BF16)


def chem_in_kernel(
    slots, r_ref, react_ref, w1_ref, h_ref, row_ref, hit_ref, token
):
    react = react_ref[...].astype(F32)
    react_b = react.astype(BF16)
    upper = where1(iota((128, 128), 0) <= iota((128, 128), 1))
    within = dot(react_b, upper)
    count = dot(react_b, jnp.ones((128, 128), BF16))
    below = where1(iota((64, 64), 1) < iota((64, 64), 0))
    offset = dot(below, count.astype(BF16))
    rank = (react * (within + offset)).astype(BF16)
    slot_lane = iota((64, slots), 1).astype(F32)
    off_col, cnt_col = offset[:, :1], count[:, :1]
    row_ref[...] = where1((slot_lane >= off_col) & (slot_lane < off_col + cnt_col))
    nt = (((1,), (1,)), ((), ()))
    count_row = lax.dot_general(
        jnp.ones((8, 128), BF16), react_b, nt, preferred_element_type=F32
    )
    offset_row = lax.dot_general(
        count_row.astype(BF16), below, nt, preferred_element_type=F32
    )
    slot_sub = iota((slots, 64), 0).astype(F32)
    slot_row = where1(
        (slot_sub >= offset_row[:1]) & (slot_sub < offset_row[:1] + count_row[:1])
    )
    lane_hit = dot(slot_row, rank) == iota((slots, 128), 0).astype(F32) + 1.0
    hit_ref[...] = where1(lane_hit)
    feat = jnp.zeros((slots, 128), F32)
    for c in range(COMPS):
        rows = dot(slot_row, r_ref[pl.ds(c * 64, 64), :].astype(BF16))
        hit = jnp.where(lane_hit, rows, 0.0).astype(BF16)
        feat = feat + dot(hit, where1(iota((128, 128), 1) == c))
    feat = jnp.transpose(feat)[:COMPS].astype(BF16)
    tn = (((0,), (0,)), ((), ()))
    one = lax.dot_general(w1_ref[...], feat, tn, preferred_element_type=F32)
    h_ref[...] = jax.nn.gelu(one).astype(BF16)
    token[...] = jnp.zeros(token.shape, F32)


def chem_in(recon, react, layer_one, slots, table):
    return pl.pallas_call(
        lambda *a: chem_in_kernel(slots, *a),
        out_shape=[
            jax.ShapeDtypeStruct((layer_one.shape[1], slots), BF16),
            jax.ShapeDtypeStruct((64, slots), BF16),
            jax.ShapeDtypeStruct((slots, 128), BF16),
            token_shape(table),
        ],
        in_specs=[VM] * 3,
        out_specs=[VM] * 4,
        compiler_params=GRANT,
        cost_estimate=cost(1),
        name="chem_in",
    )(recon, react, layer_one)


def chem_two_kernel(h_ref, w2_ref, out_ref, token):
    half = out_ref.shape[0]
    out_ref[...] = jax.nn.gelu(dot(w2_ref[pl.ds(0, half), :], h_ref[...])).astype(BF16)
    token[...] = jnp.zeros(token.shape, F32)


def chem_three_kernel(h_ref, two_ref, w2_ref, w3_ref, out_ref, token):
    half = two_ref.shape[0]
    rest = jax.nn.gelu(dot(w2_ref[pl.ds(half, half), :], h_ref[...])).astype(BF16)
    two = jnp.concatenate([two_ref[...], rest], axis=0)
    out_ref[...] = jax.nn.gelu(dot(w3_ref[...], two)).astype(BF16)
    token[...] = jnp.zeros(token.shape, F32)


def chem_layer(kernel, rows, table, *operands):
    return pl.pallas_call(
        kernel,
        out_shape=[
            jax.ShapeDtypeStruct((rows, operands[0].shape[1]), BF16),
            token_shape(table),
        ],
        in_specs=[VM] * len(operands),
        out_specs=[VM] * 2,
        compiler_params=GRANT,
        cost_estimate=cost(1),
    )(*operands)


def chem_out_kernel(h_ref, w4_ref, row_ref, hit_ref, out_ref, token):
    rates = dot(w4_ref[...], h_ref[...])
    slots = rates.shape[1]
    rates = jnp.concatenate([rates, jnp.zeros((128 - COMPS, slots), F32)], axis=0)
    rates_t = jnp.transpose(rates).astype(BF16)
    hit, row_slot = hit_ref[...].astype(F32), row_ref[...]
    for c in range(COMPS):
        spread = hit * dot(rates_t, where1(iota((128, 128), 0) == c))
        out_ref[pl.ds(c * 64, 64), :] = dot(row_slot, spread.astype(BF16))
    token[...] = jnp.zeros(token.shape, F32)


def chem_out(hidden, layer_four, row_slot, hit, table):
    return pl.pallas_call(
        chem_out_kernel,
        out_shape=[jax.ShapeDtypeStruct((COMPS * 64, 128), F32), token_shape(table)],
        in_specs=[VM] * 4,
        out_specs=[VM] * 2,
        compiler_params=GRANT,
        cost_estimate=cost(1),
        name="chem_out",
    )(hidden, layer_four, row_slot, hit)


def halo_lines(refs, scratch, own, sign_comp, at_wall, order, second):
    for c in range(0, COMPS, 2):
        block = refs[0][pl.ds(c * 24, 48), :].astype(F32)
        if len(refs) == 2:
            block = jnp.where(second, refs[1][pl.ds(c * 24, 48), :].astype(F32), block)
        for i in (0, 1):
            for k in range(3):
                mirror = own(c + i, order[k])
                if c + i == sign_comp:
                    mirror = -mirror
                got = block[(i * 3 + k) * 8 : (i * 3 + k + 1) * 8]
                scratch[pl.ds(((c + i) * 3 + k) * 8, 8), :] = jnp.where(at_wall, mirror, got)


def flux_x_inner_kernel(
    f_ref, r_ref, acc_ref, src_ref, left, right, edge_ref, out_ref, token
):
    def line(c):
        return [None] * 3 + [r_ref[rows8(c * 8 + x), :] for x in range(8)] + [None] * 3

    face_states(line, left, right, 9, ((5, 8),))
    flux = {f: face_flux(left, right, 9, 0, f) for f in (3, 4, 5)}
    for c in range(COMPS):
        edge_ref[pl.ds(c * 16, 8), :] = flux[3][c]
        edge_ref[pl.ds(c * 16 + 8, 8), :] = flux[5][c]
        for x in range(8):
            at = pl.ds(c * 64 + x * 8, 8)
            change = acc_ref[at, :]
            if x in (3, 4):
                change = change + (flux[x + 1][c] - flux[x][c])
            new = f_ref[at, :] - TIME_STEP * change + CHEM_STEP * src_ref[at, :]
            out_ref[c, pl.ds(x * 8, 8), :] = new
    token[...] = jnp.zeros(token.shape, F32)


def flux_x_kernel(count, r_ref, left_in, right_in, edge_ref, base_ref, *refs):
    flags = place_flags()
    layers, (out_hbm, lo_s, hi_s, left, right, out_ref, sems) = refs[:count], refs[count:]

    def send(ref, first, planes):
        rows = pl.ds(first * 8, planes * 8)
        copy = pltpu.make_async_copy(ref.at[:, rows], out_hbm.at[:, rows], sems.at[first])
        copy.start()
        return copy

    copies = [send(base_ref, 3, 2)]

    def own(c, x):
        return r_ref[pl.ds(c * 64 + x * 8, 8), :]

    halo_lines(layers, lo_s, own, 1, flags[0], (2, 1, 0), flags[6] == 0)
    halo_lines(layers, hi_s, own, 1, flags[1], (7, 6, 5), flags[6] == 1)

    def line(c):
        return (
            [lo_s[rows8(c * 3 + k), :] for k in range(3)]
            + [r_ref[rows8(c * 8 + x), :] for x in range(8)]
            + [hi_s[rows8(c * 3 + k), :] for k in range(3)]
        )

    face_states(line, left, right, 9, ((2, 4), (9, 11)))
    for c in range(COMPS):
        at = pl.ds((c * 9 + 2) * 8, 8)
        right[at, :] = right_in[at, :]
        at = pl.ds((c * 9 + 6) * 8, 8)
        left[at, :] = left_in[at, :]

    def emit(x, upper, lower):
        plane = pl.ds(x * 8, 8)
        for c in range(COMPS):
            out_ref[c, plane, :] = base_ref[c, plane, :] - TIME_STEP * (upper[c] - lower[c])
        copies.append(send(out_ref, x, 1))

    flux = {
        3: [edge_ref[pl.ds(c * 16, 8), :] for c in range(COMPS)],
        5: [edge_ref[pl.ds(c * 16 + 8, 8), :] for c in range(COMPS)],
    }
    for f in (2, 1, 0):
        flux[f] = face_flux(left, right, 9, 0, f)
        emit(f, flux[f + 1], flux.pop(f) if f == 0 else flux[f])
    for f in (6, 7, 8):
        flux[f] = face_flux(left, right, 9, 0, f)
        emit(f - 1, flux[f], flux[f - 1])
    for copy in copies:
        copy.wait()


def flux_y_kernel(count, r_ref, *refs):
    flags = place_flags()
    layers, (out_ref, token, lo_s, hi_s, left, right) = refs[:count], refs[count:]

    def own(c, y):
        return r_ref[pl.ds(c * 64 + y, 8, stride=8), :]

    halo_lines(layers, lo_s, own, 2, flags[2], (2, 1, 0), flags[7] == 0)
    halo_lines(layers, hi_s, own, 2, flags[3], (7, 6, 5), flags[7] == 1)

    def line(c):
        return (
            [lo_s[rows8(c * 3 + k), :] for k in range(3)]
            + [r_ref[pl.ds(c * 64 + y, 8, stride=8), :] for y in range(8)]
            + [hi_s[rows8(c * 3 + k), :] for k in range(3)]
        )

    face_states(line, left, right, 9)

    def emit(c, y, change):
        out_ref[pl.ds(c * 64 + y, 8, stride=8), :] = change

    line_changes(left, right, 9, 1, emit)
    token[...] = jnp.zeros(token.shape, F32)


def flux_z_kernel(count, zt_ref, acc_ref, *refs):
    flags = place_flags()
    layers, (out_ref, token, ext, left, right, back) = refs[:count], refs[count:]
    low3, low = half_lanes((3, 128)), half_lanes((64, 128))

    def got(c, second):
        x = layers[0][pl.ds(c * 3, 3), :]
        if count == 2:
            x = jnp.where(second, layers[1][pl.ds(c * 3, 3), :], x)
        return swap_halves(x)

    for c in range(COMPS):
        sign = -1.0 if c == 3 else 1.0
        own = zt_ref[pl.ds(c * 64, 64), :]
        first, last = own[:3], own[61:]
        mirror_lo = sign * jnp.concatenate([first[2:3], first[1:2], first[0:1]], axis=0)
        mirror_hi = sign * jnp.concatenate([last[2:3], last[1:2], last[0:1]], axis=0)
        below = jnp.where(flags[4], mirror_lo, got(c, flags[8] == 0))
        above = jnp.where(flags[5], mirror_hi, got(c, flags[8] == 1))
        ext[pl.ds(c * 72, 3), :] = jnp.where(low3, below, swap_halves(last))
        ext[pl.ds(c * 72 + 3, 64), :] = own
        ext[pl.ds(c * 72 + 67, 3), :] = jnp.where(low3, swap_halves(first), above)

    def line(c):
        return [ext[pl.ds(c * 72 + e, 8, stride=8), :] for e in range(14)]

    face_states(line, left, right, 9)

    def emit(c, z, change):
        back[pl.ds(c * 64 + z, 8, stride=8), :] = change

    line_changes(left, right, 9, 2, emit)
    for c in range(0, COMPS, 2):
        even, odd = back[pl.ds(c * 64, 64), :], back[pl.ds(c * 64 + 64, 64), :]
        t = jnp.concatenate(
            [jnp.where(low, even, swap_halves(odd)), jnp.where(low, swap_halves(even), odd)],
            axis=0,
        )
        at = pl.ds(c * 64, 128)
        out_ref[at, :] = acc_ref[at, :] + jnp.transpose(t)
    token[...] = jnp.zeros(token.shape, F32)


def impulse_kernel(own, table_ref, got_ref, out_ref):
    place = place_flags()[9] * own
    row = pl.ds(place // 128, 1)
    loads = jnp.broadcast_to(table_ref[row, :] + got_ref[row, :], (8, 128))
    loads = pltpu.roll(loads, (128 - place % 128) % 128, 1)
    out_ref[...] = loads[:1, :own] * (1.0 / (PATCH * PATCH))


def own_impulse(table, got, own):
    return pl.pallas_call(
        lambda *a: impulse_kernel(own, *a),
        out_shape=jax.ShapeDtypeStruct((1, own), F32),
        in_specs=[VM] * 2,
        out_specs=VM,
        compiler_params=GRANT,
        cost_estimate=cost(0.5),
        name="impulse",
    )(table, got)


def state_scratch():
    return [pltpu.VMEM((COMPS * 9 * 8, 128), F32)] * 2


def halo_scratch():
    return [pltpu.VMEM((COMPS * 24, 128), F32)] * 2


def token_shape(table):
    return jax.ShapeDtypeStruct(table.shape, F32)


def flux_x_inner(fields, recon, acc, source, table):
    states = jax.ShapeDtypeStruct((COMPS * 9 * 8, 128), F32)
    return pl.pallas_call(
        flux_x_inner_kernel,
        out_shape=[
            states,
            states,
            jax.ShapeDtypeStruct((COMPS * 16, 128), F32),
            jax.ShapeDtypeStruct((COMPS, 64, 128), F32),
            token_shape(table),
        ],
        in_specs=[VM] * 4,
        out_specs=[VM] * 5,
        compiler_params=GRANT,
        cost_estimate=cost(1),
        name="flux_x_inner",
    )(fields, recon, acc, source)


def flux_x(recon, inner, layers):
    return pl.pallas_call(
        lambda *a: flux_x_kernel(len(layers), *a),
        out_shape=jax.ShapeDtypeStruct((COMPS, 64, 128), F32),
        in_specs=[VM] * (5 + len(layers)),
        out_specs=HBM,
        scratch_shapes=halo_scratch()
        + state_scratch()
        + [pltpu.VMEM((COMPS, 64, 128), F32), pltpu.SemaphoreType.DMA((8,))],
        compiler_params=GRANT,
        cost_estimate=cost(2),
        name="flux_x",
    )(recon, *inner, *layers)


def flux_y(recon, layers, table):
    return pl.pallas_call(
        lambda *a: flux_y_kernel(len(layers), *a),
        out_shape=[jax.ShapeDtypeStruct(recon.shape, F32), token_shape(table)],
        in_specs=[VM] * (1 + len(layers)),
        out_specs=[VM] * 2,
        scratch_shapes=halo_scratch() + state_scratch(),
        compiler_params=GRANT,
        cost_estimate=cost(2),
        name="flux_y",
    )(recon, *layers)


def flux_z(turned, acc, layers, table):
    return pl.pallas_call(
        lambda *a: flux_z_kernel(len(layers), *a),
        out_shape=[jax.ShapeDtypeStruct(acc.shape, F32), token_shape(table)],
        in_specs=[VM] * (2 + len(layers)),
        out_specs=[VM] * 2,
        scratch_shapes=[pltpu.VMEM((COMPS * 72, 128), F32)]
        + state_scratch()
        + [pltpu.VMEM(acc.shape, F32)],
        compiler_params=GRANT,
        cost_estimate=cost(2),
        name="flux_z",
    )(turned, acc, *layers)


def swap(x, axis, second, outer=False):
    n = lax.axis_size(axis)
    pairs = [(i, i + 1) for i in range(int(second), n - 1, 2)]
    if outer:
        pairs.append((0, n - 1))
    return lax.ppermute(x, axis, [(a, b) for a, b in pairs] + [(b, a) for a, b in pairs])


def swap_inner(x, axis, other):
    n, m = lax.axis_size(axis), lax.axis_size(other)
    if m % 2 or n % 2:
        return swap(x, axis, 1)
    pairs = []
    for i in range(n):
        for j in range(m):
            end = i in (0, n - 1)
            to = (i, j ^ 1) if end else (i + 1 if i % 2 else i - 1, j)
            pairs.append((i * m + j, to[0] * m + to[1]))
    return lax.ppermute(x, (axis, other), pairs)


def sum_over(table, axis, step=1):
    size = lax.axis_size(axis)
    if size & (size - 1):
        return lax.psum(table, axis)
    while step < size:
        table = table + lax.ppermute(table, axis, [(i, i ^ step) for i in range(size)])
        step *= 2
    return table


def join_table(rows, height):
    rows = rows[: 3 * height].astype(F32)
    return rows[:height] + rows[height : 2 * height] + rows[2 * height :]


def body(fields, reacting, panel_map, layer_one, layer_two, layer_three, layer_four):
    shape = fields.shape
    sizes = [lax.axis_size(a) for a in AXES]
    pair_x = sizes[0] == 2
    panels_all = 2 * (shape[1] * sizes[0] // PATCH) * (shape[3] * sizes[2] // PATCH)
    own = panels_all // (sizes[0] * sizes[1] * sizes[2])
    height = panels_all // 128
    slots = BAL * min(4, sizes[0])
    layer_rows, edge_rows = COMPS * 24, 40
    ride_y, ride_z = sizes[1] & (sizes[1] - 1) == 0, sizes[2] in (2, 4)

    flat = fields.reshape(-1, shape[3])
    panels, react = panel_map.reshape(-1, shape[3]), reacting.reshape(-1, shape[3])
    layers = (layer_one.T, layer_two, layer_three, layer_four)
    packed = pack(flat, panels, react, layers, height)
    flat, recon, y_first, y_second, table, react, one, two, three, four = packed
    y_got = [swap(y_first, "gy", 0)]
    if sizes[1] > 2:
        y_got.append(swap_inner(y_second, "gy", "gz"))
    turned, *xs, z_first, z_second, token = turn(recon, pair_x, height)
    hidden, row_slot, hit, token_in = chem_in(recon, react, one, slots, table)
    half, token_two = chem_layer(chem_two_kernel, layer_two.shape[0] // 2, table, hidden, two)
    table = table + token + token_in + token_two
    if ride_y:
        table = table + join_table(y_got[0][layer_rows:], height)
    if not ride_z:
        table = sum_over(table, "gz")
    z_got = [swap(lax.dynamic_update_slice(z_first, table, (edge_rows, 0)), "gz", 0)]
    hidden, token = chem_layer(
        chem_three_kernel, layer_three.shape[0], table, hidden, half, two, three
    )
    if ride_z:
        table = table + z_got[0][edge_rows : edge_rows + height] + token
    if sizes[2] > 2:
        z_second = lax.dynamic_update_slice(z_second, table, (edge_rows, 0))
        z_got.append(swap(z_second, "gz", 1, ride_z))
        if ride_z:
            table = table + z_got[1][edge_rows : edge_rows + height]
    acc, token = flux_y(recon, y_got, table)
    table = table + token
    if pair_x:
        xs = [put_table(table, xs[0])]
    x_got = [swap(x, "gx", m) for m, x in enumerate(xs)]
    acc, token = flux_z(turned, acc, z_got, table)
    source, token_out = chem_out(hidden, four, row_slot, hit, table)
    *inner, token_inner = flux_x_inner(flat, recon, acc, source, table)
    table = table + token + token_out + token_inner
    if pair_x:
        table = table + join_table(x_got[0][layer_rows:], height)
    else:
        table = sum_over(table, "gx")
    rest = jnp.zeros_like(table)
    if not ride_y:
        table = lax.psum(table, "gy")
    elif sizes[1] > 2:
        table = sum_over(table, "gy", 4)
        n, m = sizes[1], sizes[2]
        flip = 1 - m % 2
        pairs = [(i * m + j, (i ^ 2) * m + (j ^ flip)) for i in range(n) for j in range(m)]
        rest = lax.ppermute(table, ("gy", "gz"), pairs)
    new = flux_x(recon, inner, x_got)
    return new.reshape(shape), own_impulse(table, rest, own).reshape(own)


def solution(mesh):
    return jax.shard_map(
        body,
        mesh=mesh,
        in_specs=(
            P(None, "gx", "gy", "gz"),
            P("gx", "gy", "gz"),
            P(None, "gx", "gz"),
            P(),
            P(),
            P(),
            P(),
        ),
        out_specs=(P(None, "gx", "gy", "gz"), P(("gx", "gy", "gz"))),
        check_vma=False,
    )
```

```python
import jax
import jax.numpy as jnp
from jax import lax
from jax.experimental import pallas as pl
from jax.experimental.pallas import tpu as pltpu
from jax.sharding import PartitionSpec as P


BAL = 64
COMPS = 12
PATCH = 8

HEAT_RATIO = 1.4
TIME_STEP = 0.1
CHEM_STEP = 0.25
WENO_EPS = 1e-06
EPS = WENO_EPS * 4.0 / 36.0
AXES = ("gx", "gy", "gz")
F32 = jnp.float32
BF16 = jnp.bfloat16
GRANT = pltpu.CompilerParams(vmem_limit_bytes=12 * 2**20)
VM = pl.BlockSpec(memory_space=pltpu.VMEM)
HBM = pl.BlockSpec(memory_space=pltpu.HBM)


def weno_line(v, first, last):
    n = len(v)
    low, high = max(first - 2, 0), min(last + 2, n - 1)
    d = {j: (v[j + 1] - v[j]) * (1.0 / 6.0) for j in range(low, high)}
    d3 = {j: 3.0 * d[j] for j in range(low + 1, high - 1)}
    q = {}
    for e in range(low + 1, high):
        s = d[e] - d[e - 1]
        q[e] = (13.0 / 3.0) * (s * s) + EPS
    upper, lower = {}, {}
    for e in range(first, last + 1):
        dm, dp = d[e - 1], d[e]
        t0 = d3[e - 1] - d[e - 2]
        t1 = dm + dp
        t2 = d3[e] - d[e + 1]
        b0 = q[e - 1] + t0 * t0
        b1 = q[e] + t1 * t1
        b2 = q[e + 1] + t2 * t2
        m01, m02, m12 = b0 * b1, b0 * b2, b1 * b2
        s01, s02, s12 = m01 * m01, m02 * m02, m12 * m12
        w1, w01, w12 = 6.0 * s02, 3.0 * s01, 3.0 * s12
        if e < n - 3:
            num = s12 * (t0 + t0 - dm) + w1 * (t1 + dp) + w01 * (t2 + dp)
            upper[e] = v[e] + num / (s12 + w1 + w01)
        if e > 2:
            num = s01 * (t2 + t2 - dp) + w1 * (t1 + dm) + w12 * (t0 + dm)
            lower[e] = v[e] - num / (s01 + w1 + w12)
    return upper, lower


def weno_one(v):
    d = [(v[j + 1] - v[j]) * (1.0 / 6.0) for j in range(4)]
    s = [d[j + 1] - d[j] for j in range(3)]
    q = [(13.0 / 3.0) * (x * x) + EPS for x in s]
    dm, dp = d[1], d[2]
    t0, t1, t2 = 3.0 * dm - d[0], dm + dp, 3.0 * dp - d[3]
    b0, b1, b2 = q[0] + t0 * t0, q[1] + t1 * t1, q[2] + t2 * t2
    m01, m02, m12 = b0 * b1, b0 * b2, b1 * b2
    w0, w1, w2 = m12 * m12, 6.0 * (m02 * m02), 3.0 * (m01 * m01)
    num = w0 * (t0 + t0 - dm) + w1 * (t1 + dp) + w2 * (t2 + dp)
    return v[2] + num / (w0 + w1 + w2)


def hllc(left, right, normal):
    n = 1 + normal

    def side(x):
        rho = jnp.exp(x[0])
        g = jnp.exp(0.5 * (x[4] - x[0]))
        h = g * g
        return rho, h, rho * h, (HEAT_RATIO**0.5) * g, x[n]

    rho_l, h_l, p_l, c_l, u_l = side(left)
    rho_r, h_r, p_r, c_r, u_r = side(right)
    s_l = jnp.minimum(u_l - c_l, u_r - c_r)
    s_r = jnp.maximum(u_l + c_l, u_r + c_r)
    m_l = rho_l * (s_l - u_l)
    m_r = rho_r * (s_r - u_r)
    s = (p_r - p_l + u_l * m_l - u_r * m_r) / (m_l - m_r)
    use_l = (s >= 0) | (s_l >= 0)
    pick = [jnp.where(use_l, a, b) for a, b in zip(left, right)]
    rho = jnp.where(use_l, rho_l, rho_r)
    h = jnp.where(use_l, h_l, h_r)
    p = jnp.where(use_l, p_l, p_r)
    wave = jnp.where(use_l, s_l, s_r)
    act = jnp.where(use_l, jnp.minimum(s_l, 0.0), jnp.maximum(s_r, 0.0))
    u = pick[n]
    rel = s - u
    ratio = rel / (wave - s)
    mass = rho * (u + act * ratio)
    k = rho * act * (1.0 + ratio) * rel
    square = pick[1] * pick[1] + pick[2] * pick[2] + pick[3] * pick[3]
    enthalpy = (1.0 / (HEAT_RATIO - 1.0) + 1.0) * h + 0.5 * square
    flux = [mass * x for x in pick]
    flux[0] = mass
    flux[n] = flux[n] + (p + k)
    flux[4] = enthalpy * mass + k * s
    return flux


def place_flags():
    sizes = [lax.axis_size(a) for a in AXES]
    index = [lax.axis_index(a) for a in AXES]
    place = (index[0] * sizes[1] + index[1]) * sizes[2] + index[2]
    flags = [f for i, n in zip(index, sizes) for f in (i == 0, i == n - 1)]
    return flags + [lax.rem(i, 2) for i in index] + [place]


def rows8(index):
    return pl.ds(pl.multiple_of(index * 8, 8), 8)


def face_states(load_line, left_ref, right_ref, faces, spans=((2, 11),)):
    def one(c, carry):
        line = load_line(c)
        for first, last in spans:
            upper, lower = weno_line(line, first, last)
            for e, x in upper.items():
                left_ref[rows8(c * faces + e - 2), :] = x
            for e, x in lower.items():
                right_ref[rows8(c * faces + e - 3), :] = x
        return carry

    lax.fori_loop(0, COMPS, one, 0)


def face_flux(left_ref, right_ref, faces, normal, f):
    left = [left_ref[pl.ds((c * faces + f) * 8, 8), :] for c in range(COMPS)]
    right = [right_ref[pl.ds((c * faces + f) * 8, 8), :] for c in range(COMPS)]
    return hllc(left, right, normal)


def line_changes(left_ref, right_ref, faces, normal, emit):
    before = None
    for f in range(faces):
        flux = face_flux(left_ref, right_ref, faces, normal, f)
        if before is not None:
            for c in range(COMPS):
                emit(c, f - 1, flux[c] - before[c])
        before = flux


def half_lanes(shape):
    return lax.broadcasted_iota(jnp.int32, shape, 1) < 64


def swap_halves(x):
    return pltpu.roll(x, 64, 1)


def split3(x):
    hi = x.astype(BF16).astype(F32)
    mid = (x - hi).astype(BF16).astype(F32)
    return hi, mid, x - hi - mid


def fetch(source, target, sem, parts=1):
    step = -(-source.shape[0] // (parts * 16)) * 16
    for start in range(0, source.shape[0], step):
        rows = pl.ds(start, min(step, source.shape[0] - start))
        pltpu.make_async_copy(source.at[rows], target.at[rows], sem).start()
    return pltpu.make_async_copy(source, target, sem).wait


def pack_kernel(*refs):
    f_hbm, map_hbm, *sources = refs[:5]
    f_ref, r_ref, y1_ref, y2_ref, table_ref, *kept = refs[5:13]
    buf, map_ref, sems = refs[13:]
    pairs = [(f_hbm, f_ref, 8), (map_hbm, map_ref, 1)]
    pairs += list(zip(sources, kept, (1, 1, 1)))
    waits = [fetch(a, b, sems.at[i], parts) for i, (a, b, parts) in enumerate(pairs)]
    flags = place_flags()
    waits[0]()
    for x in range(8):
        def at(c):
            return f_ref[pl.ds(c * 64 + x * 8, 8), :]

        rho = at(0)
        inv = 1.0 / rho
        u = [at(c) * inv for c in (1, 2, 3)]
        p = (HEAT_RATIO - 1.0) * (
            at(4) - 0.5 * rho * (u[0] * u[0] + u[1] * u[1] + u[2] * u[2])
        )
        out = [jnp.log(rho)] + u + [jnp.log(p)] + [at(c) * inv for c in range(5, COMPS)]
        for c in range(COMPS):
            r_ref[pl.ds(c * 64 + x * 8, 8), :] = out[c]
    pushes = []
    for wall in range(2):
        rows = (0, 1, 2) if wall == 0 else (7, 6, 5)
        state = []
        for c in (0, 2, 4):
            a = [r_ref[pl.ds(c * 64 + y, 8, stride=8), :] for y in rows]
            sign = -1.0 if c == 2 else 1.0
            state.append(weno_one([a[2], a[1], a[0], sign * a[0], sign * a[1]]))
        rho = jnp.exp(state[0])
        p = jnp.exp(state[2])
        out_speed = -state[1] if wall == 0 else state[1]
        speed = jnp.abs(out_speed) + jnp.sqrt(HEAT_RATIO * p / rho)
        push = p + rho * out_speed * (out_speed + speed)
        x = jnp.where(flags[2 + wall], push, 0.0)
        for s in (1, 2, 4):
            x = x + pltpu.roll(x, 128 - s, 1)
        for s in (1, 2):
            x = x + pltpu.roll(x, 8 - s, 0)
        pushes.append(x)
    waits[1]()
    ids = map_ref[...].astype(F32)
    tall = jnp.concatenate(pushes + [ids, jnp.zeros((96, 128), F32)], axis=0)
    buf[...] = jnp.transpose(tall)
    groups = [buf[pl.ds(64 * g, 8, stride=8), :] for g in range(2)]
    lane = lax.broadcasted_iota(jnp.int32, (8, 128), 1).astype(F32)
    columns = []
    for g in groups:
        for col in (0, 4, 8, 12):
            columns.append(
                (
                    jnp.broadcast_to(g[:, col : col + 1], (8, 128)),
                    jnp.broadcast_to(g[:, 16 + col : 17 + col], (8, 128)),
                )
            )
    table = []
    for j in range(table_ref.shape[0]):
        total = jnp.zeros((8, 128), F32)
        for load, panel in columns:
            total = total + jnp.where(panel == lane + 128.0 * j, load, 0.0)
        table.append(jnp.sum(total, axis=0, keepdims=True))
        table_ref[pl.ds(j, 1), :] = table[j]
    for c in range(0, COMPS, 2):
        def row(i, y):
            return r_ref[pl.ds((c + i) * 64 + y, 8, stride=8), :]

        lo = jnp.concatenate([row(i, y) for i in (0, 1) for y in range(3)], axis=0)
        hi = jnp.concatenate([row(i, y) for i in (0, 1) for y in range(5, 8)], axis=0)
        store_layers((y1_ref, y2_ref), c, lo, hi, flags[7])
    rows = y1_ref.shape[0] - COMPS * 24
    pieces = [piece[j] for piece in zip(*map(split3, table)) for j in range(len(table))]
    if rows > len(pieces):
        pieces.append(jnp.zeros((rows - len(pieces), 128), F32))
    y1_ref[pl.ds(COMPS * 24, rows), :] = jnp.concatenate(pieces, axis=0).astype(BF16)
    for wait in waits[2:]:
        wait()


def store_layers(refs, c, lo, hi, parity):
    for m, ref in enumerate(refs):
        ref[pl.ds(c * 24, 48), :] = jnp.where(parity == m, hi, lo).astype(BF16)


def put_table_kernel(table_ref, x_ref, out_ref):
    start = COMPS * 24
    rows = x_ref.shape[0] - start
    pieces = list(split3(table_ref[...]))
    used = 3 * table_ref.shape[0]
    if rows > used:
        pieces.append(jnp.zeros((rows - used, 128), F32))
    out_ref[pl.ds(start, rows), :] = jnp.concatenate(pieces, axis=0).astype(BF16)


def put_table(table, x):
    return pl.pallas_call(
        put_table_kernel,
        out_shape=jax.ShapeDtypeStruct(x.shape, x.dtype),
        in_specs=[VM] * 2,
        out_specs=VM,
        input_output_aliases={1: 0},
        compiler_params=GRANT,
        cost_estimate=cost(0.2),
        name="put_table",
    )(table, x)


def in_hbm(x):
    return pltpu.with_memory_space_constraint(x, pltpu.HBM)


def load_rows(height):
    return -(-3 * height // 16) * 16


def pack(fields, panels, react, layers, height):
    whole = jax.ShapeDtypeStruct((COMPS * 64, 128), F32)
    outs = [whole, whole]
    outs.append(jax.ShapeDtypeStruct((COMPS * 24 + load_rows(height), 128), BF16))
    outs.append(jax.ShapeDtypeStruct((COMPS * 24, 128), BF16))
    outs.append(jax.ShapeDtypeStruct((height, 128), F32))
    one, _, _, four = layers
    kept = [jax.ShapeDtypeStruct(x.shape, x.dtype) for x in (react, one, four)]
    outs += kept
    return pl.pallas_call(
        pack_kernel,
        out_shape=outs,
        in_specs=[HBM] * 5,
        out_specs=[VM] * len(outs),
        scratch_shapes=[
            pltpu.VMEM((128, 128), F32),
            pltpu.VMEM(panels.shape, jnp.int32),
            pltpu.SemaphoreType.DMA((5,)),
        ],
        compiler_params=GRANT,
        cost_estimate=cost(2),
        name="pack",
    )(*map(in_hbm, (fields, panels, react, one, four)))


def turn_kernel(pair_x, r_ref, zt_ref, *refs):
    x_refs, (z1_ref, z2_ref, token) = refs[: 2 - pair_x], refs[2 - pair_x :]
    z_refs = (z1_ref, z2_ref)
    flags = place_flags()
    for c in range(0, COMPS, 2):
        lo = jnp.concatenate([r_ref[pl.ds((c + i) * 64, 24), :] for i in (0, 1)], axis=0)
        hi = jnp.concatenate([r_ref[pl.ds((c + i) * 64 + 40, 24), :] for i in (0, 1)], axis=0)
        store_layers(x_refs, c, lo, hi, flags[6])
    low = half_lanes((64, 128))
    for c in range(0, COMPS, 2):
        t = jnp.transpose(r_ref[pl.ds(c * 64, 128), :])
        top, bottom = t[:64], t[64:]
        even = jnp.where(low, top, swap_halves(bottom))
        odd = jnp.where(low, swap_halves(top), bottom)
        for i, x in ((0, even), (1, odd)):
            zt_ref[pl.ds((c + i) * 64, 64), :] = x
            for m, ref in enumerate(z_refs):
                up = flags[8] == m
                ref[pl.ds((c + i) * 3, 3), :] = jnp.where(up, x[61:], x[:3])
    for ref, start in [(x, COMPS * 24) for x in x_refs] + [(z, COMPS * 3) for z in z_refs]:
        if ref.shape[0] > start:
            ref[pl.ds(start, ref.shape[0] - start), :] = jnp.zeros(
                (ref.shape[0] - start, 128), ref.dtype
            )
    token[...] = jnp.zeros(token.shape, F32)


def turn(recon, pair_x, height):
    layer_x = jax.ShapeDtypeStruct((COMPS * 24 + (load_rows(height) if pair_x else 0), 128), BF16)
    edge = jax.ShapeDtypeStruct((40 + -(-height // 8) * 8, 128), F32)
    outs = [jax.ShapeDtypeStruct(recon.shape, F32)] + [layer_x] * (2 - pair_x) + [edge] * 2
    outs.append(jax.ShapeDtypeStruct((height, 128), F32))
    return pl.pallas_call(
        lambda *a: turn_kernel(int(pair_x), *a),
        out_shape=outs,
        in_specs=[VM],
        out_specs=[VM] * len(outs),
        compiler_params=GRANT,
        cost_estimate=cost(1),
        name="turn",
    )(recon)


def cost(us):
    return pl.CostEstimate(flops=int(0.6*us*1e9), transcendentals=0, bytes_accessed=int(us * 0.6*3.5e6))


def dot(a, b):
    return jnp.dot(a, b, preferred_element_type=F32)


def iota(shape, dim):
    return lax.broadcasted_iota(jnp.int32, shape, dim)


def where1(mask):
    return jnp.where(mask, 1.0, 0.0).astype(BF16)


def chem_in_kernel(
    slots, r_ref, react_ref, w1_ref, h_ref, row_ref, hit_ref, token
):
    react = react_ref[...].astype(F32)
    react_b = react.astype(BF16)
    upper = where1(iota((128, 128), 0) <= iota((128, 128), 1))
    within = dot(react_b, upper)
    count = dot(react_b, jnp.ones((128, 128), BF16))
    below = where1(iota((64, 64), 1) < iota((64, 64), 0))
    offset = dot(below, count.astype(BF16))
    rank = (react * (within + offset)).astype(BF16)
    slot_lane = iota((64, slots), 1).astype(F32)
    off_col, cnt_col = offset[:, :1], count[:, :1]
    row_ref[...] = where1((slot_lane >= off_col) & (slot_lane < off_col + cnt_col))
    nt = (((1,), (1,)), ((), ()))
    count_row = lax.dot_general(
        jnp.ones((8, 128), BF16), react_b, nt, preferred_element_type=F32
    )
    offset_row = lax.dot_general(
        count_row.astype(BF16), below, nt, preferred_element_type=F32
    )
    slot_sub = iota((slots, 64), 0).astype(F32)
    slot_row = where1(
        (slot_sub >= offset_row[:1]) & (slot_sub < offset_row[:1] + count_row[:1])
    )
    lane_hit = dot(slot_row, rank) == iota((slots, 128), 0).astype(F32) + 1.0
    hit_ref[...] = where1(lane_hit)
    feat = jnp.zeros((slots, 128), F32)
    for c in range(COMPS):
        rows = dot(slot_row, r_ref[pl.ds(c * 64, 64), :].astype(BF16))
        hit = jnp.where(lane_hit, rows, 0.0).astype(BF16)
        feat = feat + dot(hit, where1(iota((128, 128), 1) == c))
    feat = jnp.transpose(feat)[:COMPS].astype(BF16)
    tn = (((0,), (0,)), ((), ()))
    one = lax.dot_general(w1_ref[...], feat, tn, preferred_element_type=F32)
    h_ref[...] = jax.nn.gelu(one).astype(BF16)
    token[...] = jnp.zeros(token.shape, F32)


def chem_in(recon, react, layer_one, slots, table):
    return pl.pallas_call(
        lambda *a: chem_in_kernel(slots, *a),
        out_shape=[
            jax.ShapeDtypeStruct((layer_one.shape[1], slots), BF16),
            jax.ShapeDtypeStruct((64, slots), BF16),
            jax.ShapeDtypeStruct((slots, 128), BF16),
            token_shape(table),
        ],
        in_specs=[VM] * 3,
        out_specs=[VM] * 4,
        compiler_params=GRANT,
        cost_estimate=cost(1),
        name="chem_in",
    )(recon, react, layer_one)


def chem_two_kernel(h_ref, w2_ref, out_ref, token):
    half = out_ref.shape[0]
    out_ref[...] = jax.nn.gelu(dot(w2_ref[pl.ds(0, half), :], h_ref[...])).astype(BF16)
    token[...] = jnp.zeros(token.shape, F32)


def chem_three_kernel(h_ref, two_ref, w2_ref, w3_ref, _, out_ref, token):
    half = two_ref.shape[0]
    rest = jax.nn.gelu(dot(w2_ref[pl.ds(half, half), :], h_ref[...])).astype(BF16)
    two = jnp.concatenate([two_ref[...], rest], axis=0)
    out_ref[...] = jax.nn.gelu(dot(w3_ref[...], two)).astype(BF16)
    token[...] = jnp.zeros(token.shape, F32)


def chem_layer(kernel, rows, table, *operands):
    return pl.pallas_call(
        kernel,
        out_shape=[
            jax.ShapeDtypeStruct((rows, operands[0].shape[1]), BF16),
            token_shape(table),
        ],
        in_specs=[VM] * len(operands),
        out_specs=[VM] * 2,
        compiler_params=GRANT,
        cost_estimate=cost(1),
    )(*operands)


def chem_out_kernel(h_ref, w4_ref, row_ref, hit_ref, _, out_ref, token):
    rates = dot(w4_ref[...], h_ref[...])
    slots = rates.shape[1]
    rates = jnp.concatenate([rates, jnp.zeros((128 - COMPS, slots), F32)], axis=0)
    rates_t = jnp.transpose(rates).astype(BF16)
    hit, row_slot = hit_ref[...].astype(F32), row_ref[...]
    for c in range(COMPS):
        spread = hit * dot(rates_t, where1(iota((128, 128), 0) == c))
        out_ref[pl.ds(c * 64, 64), :] = dot(row_slot, spread.astype(BF16))
    token[...] = jnp.zeros(token.shape, F32)


def chem_out(hidden, layer_four, row_slot, hit, table):
    return pl.pallas_call(
        chem_out_kernel,
        out_shape=[jax.ShapeDtypeStruct((COMPS * 64, 128), F32), token_shape(table)],
        in_specs=[VM] * 5,
        out_specs=[VM] * 2,
        compiler_params=GRANT,
        cost_estimate=cost(1),
        name="chem_out",
    )(hidden, layer_four, row_slot, hit, table)


def halo_lines(refs, scratch, own, sign_comp, at_wall, order, second):
    for c in range(0, COMPS, 2):
        block = refs[0][pl.ds(c * 24, 48), :].astype(F32)
        if len(refs) == 2:
            block = jnp.where(second, refs[1][pl.ds(c * 24, 48), :].astype(F32), block)
        for i in (0, 1):
            for k in range(3):
                mirror = own(c + i, order[k])
                if c + i == sign_comp:
                    mirror = -mirror
                got = block[(i * 3 + k) * 8 : (i * 3 + k + 1) * 8]
                scratch[pl.ds(((c + i) * 3 + k) * 8, 8), :] = jnp.where(at_wall, mirror, got)


def flux_x_inner_kernel(
    f_ref, r_ref, acc_ref, src_ref, left, right, edge_ref, out_ref, token
):
    def line(c):
        return [None] * 3 + [r_ref[rows8(c * 8 + x), :] for x in range(8)] + [None] * 3

    face_states(line, left, right, 9, ((5, 8),))
    flux = {f: face_flux(left, right, 9, 0, f) for f in (3, 4, 5)}
    for c in range(COMPS):
        edge_ref[pl.ds(c * 16, 8), :] = flux[3][c]
        edge_ref[pl.ds(c * 16 + 8, 8), :] = flux[5][c]
        for x in range(8):
            at = pl.ds(c * 64 + x * 8, 8)
            change = acc_ref[at, :]
            if x in (3, 4):
                change = change + (flux[x + 1][c] - flux[x][c])
            new = f_ref[at, :] - TIME_STEP * change + CHEM_STEP * src_ref[at, :]
            out_ref[c, pl.ds(x * 8, 8), :] = new
    token[...] = jnp.zeros(token.shape, F32)


def flux_x_kernel(count, r_ref, left_in, right_in, edge_ref, base_ref, *refs):
    flags = place_flags()
    layers, (out_hbm, lo_s, hi_s, left, right, out_ref, sems) = refs[:count], refs[count:]

    def send(ref, first, planes):
        rows = pl.ds(first * 8, planes * 8)
        copy = pltpu.make_async_copy(ref.at[:, rows], out_hbm.at[:, rows], sems.at[first])
        copy.start()
        return copy

    copies = [send(base_ref, 3, 2)]

    def own(c, x):
        return r_ref[pl.ds(c * 64 + x * 8, 8), :]

    halo_lines(layers, lo_s, own, 1, flags[0], (2, 1, 0), flags[6] == 0)
    halo_lines(layers, hi_s, own, 1, flags[1], (7, 6, 5), flags[6] == 1)

    def line(c):
        return (
            [lo_s[rows8(c * 3 + k), :] for k in range(3)]
            + [r_ref[rows8(c * 8 + x), :] for x in range(8)]
            + [hi_s[rows8(c * 3 + k), :] for k in range(3)]
        )

    face_states(line, left, right, 9, ((2, 4), (9, 11)))
    for c in range(COMPS):
        at = pl.ds((c * 9 + 2) * 8, 8)
        right[at, :] = right_in[at, :]
        at = pl.ds((c * 9 + 6) * 8, 8)
        left[at, :] = left_in[at, :]

    def emit(x, upper, lower):
        plane = pl.ds(x * 8, 8)
        for c in range(COMPS):
            out_ref[c, plane, :] = base_ref[c, plane, :] - TIME_STEP * (upper[c] - lower[c])
        copies.append(send(out_ref, x, 1))

    flux = {
        3: [edge_ref[pl.ds(c * 16, 8), :] for c in range(COMPS)],
        5: [edge_ref[pl.ds(c * 16 + 8, 8), :] for c in range(COMPS)],
    }
    for f in (2, 1, 0):
        flux[f] = face_flux(left, right, 9, 0, f)
        emit(f, flux[f + 1], flux.pop(f) if f == 0 else flux[f])
    for f in (6, 7, 8):
        flux[f] = face_flux(left, right, 9, 0, f)
        emit(f - 1, flux[f], flux[f - 1])
    for copy in copies:
        copy.wait()


def flux_y_kernel(count, r_ref, *refs):
    flags = place_flags()
    layers, (out_ref, token, lo_s, hi_s, left, right) = refs[:count], refs[count:]

    def own(c, y):
        return r_ref[pl.ds(c * 64 + y, 8, stride=8), :]

    halo_lines(layers, lo_s, own, 2, flags[2], (2, 1, 0), flags[7] == 0)
    halo_lines(layers, hi_s, own, 2, flags[3], (7, 6, 5), flags[7] == 1)

    def line(c):
        return (
            [lo_s[rows8(c * 3 + k), :] for k in range(3)]
            + [r_ref[pl.ds(c * 64 + y, 8, stride=8), :] for y in range(8)]
            + [hi_s[rows8(c * 3 + k), :] for k in range(3)]
        )

    face_states(line, left, right, 9)

    def emit(c, y, change):
        out_ref[pl.ds(c * 64 + y, 8, stride=8), :] = change

    line_changes(left, right, 9, 1, emit)
    token[...] = jnp.zeros(token.shape, F32)


def flux_z_kernel(count, zt_ref, acc_ref, *refs):
    flags = place_flags()
    layers, (out_ref, token, ext, left, right, back) = refs[:count], refs[count:]
    low3, low = half_lanes((3, 128)), half_lanes((64, 128))

    def got(c, second):
        x = layers[0][pl.ds(c * 3, 3), :]
        if count == 2:
            x = jnp.where(second, layers[1][pl.ds(c * 3, 3), :], x)
        return swap_halves(x)

    for c in range(COMPS):
        sign = -1.0 if c == 3 else 1.0
        own = zt_ref[pl.ds(c * 64, 64), :]
        first, last = own[:3], own[61:]
        mirror_lo = sign * jnp.concatenate([first[2:3], first[1:2], first[0:1]], axis=0)
        mirror_hi = sign * jnp.concatenate([last[2:3], last[1:2], last[0:1]], axis=0)
        below = jnp.where(flags[4], mirror_lo, got(c, flags[8] == 0))
        above = jnp.where(flags[5], mirror_hi, got(c, flags[8] == 1))
        ext[pl.ds(c * 72, 3), :] = jnp.where(low3, below, swap_halves(last))
        ext[pl.ds(c * 72 + 3, 64), :] = own
        ext[pl.ds(c * 72 + 67, 3), :] = jnp.where(low3, swap_halves(first), above)

    def line(c):
        return [ext[pl.ds(c * 72 + e, 8, stride=8), :] for e in range(14)]

    face_states(line, left, right, 9)

    def emit(c, z, change):
        back[pl.ds(c * 64 + z, 8, stride=8), :] = change

    line_changes(left, right, 9, 2, emit)
    for c in range(0, COMPS, 2):
        even, odd = back[pl.ds(c * 64, 64), :], back[pl.ds(c * 64 + 64, 64), :]
        t = jnp.concatenate(
            [jnp.where(low, even, swap_halves(odd)), jnp.where(low, swap_halves(even), odd)],
            axis=0,
        )
        at = pl.ds(c * 64, 128)
        out_ref[at, :] = acc_ref[at, :] + jnp.transpose(t)
    token[...] = jnp.zeros(token.shape, F32)


def impulse_kernel(own, table_ref, got_ref, out_ref):
    place = place_flags()[9] * own
    row = pl.ds(place // 128, 1)
    loads = jnp.broadcast_to(table_ref[row, :] + got_ref[row, :], (8, 128))
    loads = pltpu.roll(loads, (128 - place % 128) % 128, 1)
    out_ref[...] = loads[:1, :own] * (1.0 / (PATCH * PATCH))


def own_impulse(table, got, own):
    return pl.pallas_call(
        lambda *a: impulse_kernel(own, *a),
        out_shape=jax.ShapeDtypeStruct((1, own), F32),
        in_specs=[VM] * 2,
        out_specs=VM,
        compiler_params=GRANT,
        cost_estimate=cost(0.5),
        name="impulse",
    )(table, got)


def state_scratch():
    return [pltpu.VMEM((COMPS * 9 * 8, 128), F32)] * 2


def halo_scratch():
    return [pltpu.VMEM((COMPS * 24, 128), F32)] * 2


def token_shape(table):
    return jax.ShapeDtypeStruct(table.shape, F32)


def flux_x_inner(fields, recon, acc, source, table):
    states = jax.ShapeDtypeStruct((COMPS * 9 * 8, 128), F32)
    return pl.pallas_call(
        flux_x_inner_kernel,
        out_shape=[
            states,
            states,
            jax.ShapeDtypeStruct((COMPS * 16, 128), F32),
            jax.ShapeDtypeStruct((COMPS, 64, 128), F32),
            token_shape(table),
        ],
        in_specs=[VM] * 4,
        out_specs=[VM] * 5,
        compiler_params=GRANT,
        cost_estimate=cost(1),
        name="flux_x_inner",
    )(fields, recon, acc, source)


def flux_x(recon, inner, layers):
    return pl.pallas_call(
        lambda *a: flux_x_kernel(len(layers), *a),
        out_shape=jax.ShapeDtypeStruct((COMPS, 64, 128), F32),
        in_specs=[VM] * (5 + len(layers)),
        out_specs=HBM,
        scratch_shapes=halo_scratch()
        + state_scratch()
        + [pltpu.VMEM((COMPS, 64, 128), F32), pltpu.SemaphoreType.DMA((8,))],
        compiler_params=GRANT,
        cost_estimate=cost(2),
        name="flux_x",
    )(recon, *inner, *layers)


def flux_y(recon, layers, table):
    return pl.pallas_call(
        lambda *a: flux_y_kernel(len(layers), *a),
        out_shape=[jax.ShapeDtypeStruct(recon.shape, F32), token_shape(table)],
        in_specs=[VM] * (1 + len(layers)),
        out_specs=[VM] * 2,
        scratch_shapes=halo_scratch() + state_scratch(),
        compiler_params=GRANT,
        cost_estimate=cost(2),
        name="flux_y",
    )(recon, *layers)


def flux_z(turned, acc, layers, table):
    return pl.pallas_call(
        lambda *a: flux_z_kernel(len(layers), *a),
        out_shape=[jax.ShapeDtypeStruct(acc.shape, F32), token_shape(table)],
        in_specs=[VM] * (2 + len(layers)),
        out_specs=[VM] * 2,
        scratch_shapes=[pltpu.VMEM((COMPS * 72, 128), F32)]
        + state_scratch()
        + [pltpu.VMEM(acc.shape, F32)],
        compiler_params=GRANT,
        cost_estimate=cost(2),
        name="flux_z",
    )(turned, acc, *layers)


def swap(x, axis, second, outer=False):
    n = lax.axis_size(axis)
    pairs = [(i, i + 1) for i in range(int(second), n - 1, 2)]
    if outer:
        pairs.append((0, n - 1))
    return lax.ppermute(x, axis, [(a, b) for a, b in pairs] + [(b, a) for a, b in pairs])


def swap_inner(x, axis, other):
    n, m = lax.axis_size(axis), lax.axis_size(other)
    if m % 2 or n % 2:
        return swap(x, axis, 1)
    pairs = []
    for i in range(n):
        for j in range(m):
            end = i in (0, n - 1)
            to = (i, j ^ 1) if end else (i + 1 if i % 2 else i - 1, j)
            pairs.append((i * m + j, to[0] * m + to[1]))
    return lax.ppermute(x, (axis, other), pairs)


def sum_over(table, axis, step=1):
    size = lax.axis_size(axis)
    if size & (size - 1):
        return lax.psum(table, axis)
    while step < size:
        table = table + lax.ppermute(table, axis, [(i, i ^ step) for i in range(size)])
        step *= 2
    return table


def join_table(rows, height):
    rows = rows[: 3 * height].astype(F32)
    return rows[:height] + rows[height : 2 * height] + rows[2 * height :]


def body(fields, reacting, panel_map, layer_one, layer_two, layer_three, layer_four):
    shape = fields.shape
    sizes = [lax.axis_size(a) for a in AXES]
    pair_x = sizes[0] == 2
    panels_all = 2 * (shape[1] * sizes[0] // PATCH) * (shape[3] * sizes[2] // PATCH)
    own = panels_all // (sizes[0] * sizes[1] * sizes[2])
    height = panels_all // 128
    slots = BAL * min(4, sizes[0])
    layer_rows, edge_rows = COMPS * 24, 40
    ride_y, ride_z = sizes[1] & (sizes[1] - 1) == 0, sizes[2] in (2, 4)

    flat = fields.reshape(-1, shape[3])
    panels, react = panel_map.reshape(-1, shape[3]), reacting.reshape(-1, shape[3])
    layers = (layer_one.T, layer_two, layer_three, layer_four)
    packed = pack(flat, panels, react, layers, height)
    flat, recon, y_first, y_second, table, react, one, four = packed
    two, three = layer_two, layer_three
    y_got = [swap(y_first, "gy", 0)]
    if sizes[1] > 2:
        y_got.append(swap_inner(y_second, "gy", "gz"))
    turned, *xs, z_first, z_second, token = turn(recon, pair_x, height)
    hidden, row_slot, hit, token_in = chem_in(recon, react, one, slots, table)
    half, token_two = chem_layer(chem_two_kernel, layer_two.shape[0] // 2, table, hidden, two)
    table = table + token + token_in + token_two
    if ride_y:
        table = table + join_table(y_got[0][layer_rows:], height)
    if not ride_z:
        table = sum_over(table, "gz")
    z_got = [swap(lax.dynamic_update_slice(z_first, table, (edge_rows, 0)), "gz", 0)]
    hidden, token = chem_layer(
        chem_three_kernel, layer_three.shape[0], table, hidden, half, two, three, table
    )
    if ride_z:
        table = table + z_got[0][edge_rows : edge_rows + height] + token
    if sizes[2] > 2:
        z_second = lax.dynamic_update_slice(z_second, table, (edge_rows, 0))
        z_got.append(swap(z_second, "gz", 1, ride_z))
        if ride_z:
            table = table + z_got[1][edge_rows : edge_rows + height]
    acc, token = flux_y(recon, y_got, table)
    table = table + token
    if pair_x:
        xs = [put_table(table, xs[0])]
    x_got = [swap(x, "gx", m) for m, x in enumerate(xs)]
    acc, token = flux_z(turned, acc, z_got, table)
    source, token_out = chem_out(hidden, four, row_slot, hit, table)
    *inner, token_inner = flux_x_inner(flat, recon, acc, source, table)
    table = table + token + token_out + token_inner
    if pair_x:
        table = table + join_table(x_got[0][layer_rows:], height)
    else:
        table = sum_over(table, "gx")
    rest = jnp.zeros_like(table)
    if not ride_y:
        table = lax.psum(table, "gy")
    elif sizes[1] > 2:
        table = sum_over(table, "gy", 4)
        n, m = sizes[1], sizes[2]
        flip = 1 - m % 2
        pairs = [(i * m + j, (i ^ 2) * m + (j ^ flip)) for i in range(n) for j in range(m)]
        rest = lax.ppermute(table, ("gy", "gz"), pairs)
    new = flux_x(recon, inner, x_got)
    return new.reshape(shape), own_impulse(table, rest, own).reshape(own)


def solution(mesh):
    return jax.shard_map(
        body,
        mesh=mesh,
        in_specs=(
            P(None, "gx", "gy", "gz"),
            P("gx", "gy", "gz"),
            P(None, "gx", "gz"),
            P(),
            P(),
            P(),
            P(),
        ),
        out_specs=(P(None, "gx", "gy", "gz"), P(("gx", "gy", "gz"))),
        check_vma=False,
    )
```

```python
import jax
import jax.numpy as jnp
from jax import lax
from jax.experimental import pallas as pl
from jax.experimental.pallas import tpu as pltpu
from jax.sharding import PartitionSpec as P


BAL = 64
COMPS = 12
PATCH = 8

HEAT_RATIO = 1.4
TIME_STEP = 0.1
CHEM_STEP = 0.25
WENO_EPS = 1e-06
EPS = WENO_EPS * 4.0 / 36.0
AXES = ("gx", "gy", "gz")
F32 = jnp.float32
BF16 = jnp.bfloat16
GRANT = pltpu.CompilerParams(vmem_limit_bytes=12 * 2**20)
VM = pl.BlockSpec(memory_space=pltpu.VMEM)
HBM = pl.BlockSpec(memory_space=pltpu.HBM)


def weno_line(v, first, last):
    n = len(v)
    low, high = max(first - 2, 0), min(last + 2, n - 1)
    d = {j: (v[j + 1] - v[j]) * (1.0 / 6.0) for j in range(low, high)}
    d3 = {j: 3.0 * d[j] for j in range(low + 1, high - 1)}
    q = {}
    for e in range(low + 1, high):
        s = d[e] - d[e - 1]
        q[e] = (13.0 / 3.0) * (s * s) + EPS
    upper, lower = {}, {}
    for e in range(first, last + 1):
        dm, dp = d[e - 1], d[e]
        t0 = d3[e - 1] - d[e - 2]
        t1 = dm + dp
        t2 = d3[e] - d[e + 1]
        b0 = q[e - 1] + t0 * t0
        b1 = q[e] + t1 * t1
        b2 = q[e + 1] + t2 * t2
        m01, m02, m12 = b0 * b1, b0 * b2, b1 * b2
        s01, s02, s12 = m01 * m01, m02 * m02, m12 * m12
        w1, w01, w12 = 6.0 * s02, 3.0 * s01, 3.0 * s12
        if e < n - 3:
            num = s12 * (t0 + t0 - dm) + w1 * (t1 + dp) + w01 * (t2 + dp)
            upper[e] = v[e] + num / (s12 + w1 + w01)
        if e > 2:
            num = s01 * (t2 + t2 - dp) + w1 * (t1 + dm) + w12 * (t0 + dm)
            lower[e] = v[e] - num / (s01 + w1 + w12)
    return upper, lower


def weno_one(v):
    d = [(v[j + 1] - v[j]) * (1.0 / 6.0) for j in range(4)]
    s = [d[j + 1] - d[j] for j in range(3)]
    q = [(13.0 / 3.0) * (x * x) + EPS for x in s]
    dm, dp = d[1], d[2]
    t0, t1, t2 = 3.0 * dm - d[0], dm + dp, 3.0 * dp - d[3]
    b0, b1, b2 = q[0] + t0 * t0, q[1] + t1 * t1, q[2] + t2 * t2
    m01, m02, m12 = b0 * b1, b0 * b2, b1 * b2
    w0, w1, w2 = m12 * m12, 6.0 * (m02 * m02), 3.0 * (m01 * m01)
    num = w0 * (t0 + t0 - dm) + w1 * (t1 + dp) + w2 * (t2 + dp)
    return v[2] + num / (w0 + w1 + w2)


def hllc(left, right, normal):
    n = 1 + normal

    def side(x):
        rho = jnp.exp(x[0])
        g = jnp.exp(0.5 * (x[4] - x[0]))
        h = g * g
        return rho, h, rho * h, (HEAT_RATIO**0.5) * g, x[n]

    rho_l, h_l, p_l, c_l, u_l = side(left)
    rho_r, h_r, p_r, c_r, u_r = side(right)
    s_l = jnp.minimum(u_l - c_l, u_r - c_r)
    s_r = jnp.maximum(u_l + c_l, u_r + c_r)
    m_l = rho_l * (s_l - u_l)
    m_r = rho_r * (s_r - u_r)
    s = (p_r - p_l + u_l * m_l - u_r * m_r) / (m_l - m_r)
    use_l = (s >= 0) | (s_l >= 0)
    pick = [jnp.where(use_l, a, b) for a, b in zip(left, right)]
    rho = jnp.where(use_l, rho_l, rho_r)
    h = jnp.where(use_l, h_l, h_r)
    p = jnp.where(use_l, p_l, p_r)
    wave = jnp.where(use_l, s_l, s_r)
    act = jnp.where(use_l, jnp.minimum(s_l, 0.0), jnp.maximum(s_r, 0.0))
    u = pick[n]
    rel = s - u
    ratio = rel / (wave - s)
    mass = rho * (u + act * ratio)
    k = rho * act * (1.0 + ratio) * rel
    square = pick[1] * pick[1] + pick[2] * pick[2] + pick[3] * pick[3]
    enthalpy = (1.0 / (HEAT_RATIO - 1.0) + 1.0) * h + 0.5 * square
    flux = [mass * x for x in pick]
    flux[0] = mass
    flux[n] = flux[n] + (p + k)
    flux[4] = enthalpy * mass + k * s
    return flux


def place_flags():
    sizes = [lax.axis_size(a) for a in AXES]
    index = [lax.axis_index(a) for a in AXES]
    place = (index[0] * sizes[1] + index[1]) * sizes[2] + index[2]
    flags = [f for i, n in zip(index, sizes) for f in (i == 0, i == n - 1)]
    return flags + [lax.rem(i, 2) for i in index] + [place]


def rows8(index):
    return pl.ds(pl.multiple_of(index * 8, 8), 8)


def face_states(load_line, left_ref, right_ref, faces, spans=((2, 11),)):
    def one(c, carry):
        line = load_line(c)
        for first, last in spans:
            upper, lower = weno_line(line, first, last)
            for e, x in upper.items():
                left_ref[rows8(c * faces + e - 2), :] = x
            for e, x in lower.items():
                right_ref[rows8(c * faces + e - 3), :] = x
        return carry

    lax.fori_loop(0, COMPS, one, 0)


def face_flux(left_ref, right_ref, faces, normal, f):
    left = [left_ref[pl.ds((c * faces + f) * 8, 8), :] for c in range(COMPS)]
    right = [right_ref[pl.ds((c * faces + f) * 8, 8), :] for c in range(COMPS)]
    return hllc(left, right, normal)


def line_changes(left_ref, right_ref, faces, normal, emit):
    before = None
    for f in range(faces):
        flux = face_flux(left_ref, right_ref, faces, normal, f)
        if before is not None:
            for c in range(COMPS):
                emit(c, f - 1, flux[c] - before[c])
        before = flux


def half_lanes(shape):
    return lax.broadcasted_iota(jnp.int32, shape, 1) < 64


def swap_halves(x):
    return pltpu.roll(x, 64, 1)


def split3(x):
    hi = x.astype(BF16).astype(F32)
    mid = (x - hi).astype(BF16).astype(F32)
    return hi, mid, x - hi - mid


def fetch(source, target, sem, parts=1):
    step = -(-source.shape[0] // (parts * 16)) * 16
    for start in range(0, source.shape[0], step):
        rows = pl.ds(start, min(step, source.shape[0] - start))
        pltpu.make_async_copy(source.at[rows], target.at[rows], sem).start()
    return pltpu.make_async_copy(source, target, sem).wait


def pack_kernel(*refs):
    f_hbm, map_hbm, *sources = refs[:5]
    f_ref, r_ref, y1_ref, table_ref, *kept = refs[5:12]
    buf, map_ref, sems = refs[12:]
    pairs = [(f_hbm, f_ref, 8), (map_hbm, map_ref, 1)]
    pairs += list(zip(sources, kept, (1, 1, 1)))
    waits = [fetch(a, b, sems.at[i], parts) for i, (a, b, parts) in enumerate(pairs)]
    flags = place_flags()
    waits[0]()
    for x in range(8):
        def at(c):
            return f_ref[pl.ds(c * 64 + x * 8, 8), :]

        rho = at(0)
        inv = 1.0 / rho
        u = [at(c) * inv for c in (1, 2, 3)]
        p = (HEAT_RATIO - 1.0) * (
            at(4) - 0.5 * rho * (u[0] * u[0] + u[1] * u[1] + u[2] * u[2])
        )
        out = [jnp.log(rho)] + u + [jnp.log(p)] + [at(c) * inv for c in range(5, COMPS)]
        for c in range(COMPS):
            r_ref[pl.ds(c * 64 + x * 8, 8), :] = out[c]
    pushes = []
    for wall in range(2):
        rows = (0, 1, 2) if wall == 0 else (7, 6, 5)
        state = []
        for c in (0, 2, 4):
            a = [r_ref[pl.ds(c * 64 + y, 8, stride=8), :] for y in rows]
            sign = -1.0 if c == 2 else 1.0
            state.append(weno_one([a[2], a[1], a[0], sign * a[0], sign * a[1]]))
        rho = jnp.exp(state[0])
        p = jnp.exp(state[2])
        out_speed = -state[1] if wall == 0 else state[1]
        speed = jnp.abs(out_speed) + jnp.sqrt(HEAT_RATIO * p / rho)
        push = p + rho * out_speed * (out_speed + speed)
        x = jnp.where(flags[2 + wall], push, 0.0)
        for s in (1, 2, 4):
            x = x + pltpu.roll(x, 128 - s, 1)
        for s in (1, 2):
            x = x + pltpu.roll(x, 8 - s, 0)
        pushes.append(x)
    waits[1]()
    ids = map_ref[...].astype(F32)
    tall = jnp.concatenate(pushes + [ids, jnp.zeros((96, 128), F32)], axis=0)
    buf[...] = jnp.transpose(tall)
    groups = [buf[pl.ds(64 * g, 8, stride=8), :] for g in range(2)]
    lane = lax.broadcasted_iota(jnp.int32, (8, 128), 1).astype(F32)
    columns = []
    for g in groups:
        for col in (0, 4, 8, 12):
            columns.append(
                (
                    jnp.broadcast_to(g[:, col : col + 1], (8, 128)),
                    jnp.broadcast_to(g[:, 16 + col : 17 + col], (8, 128)),
                )
            )
    table = []
    for j in range(table_ref.shape[0]):
        total = jnp.zeros((8, 128), F32)
        for load, panel in columns:
            total = total + jnp.where(panel == lane + 128.0 * j, load, 0.0)
        table.append(jnp.sum(total, axis=0, keepdims=True))
        table_ref[pl.ds(j, 1), :] = table[j]
    store_y_layers(r_ref, y1_ref, flags[7] == 0)
    rows = y1_ref.shape[0] - COMPS * 24
    pieces = [piece[j] for piece in zip(*map(split3, table)) for j in range(len(table))]
    if rows > len(pieces):
        pieces.append(jnp.zeros((rows - len(pieces), 128), F32))
    y1_ref[pl.ds(COMPS * 24, rows), :] = jnp.concatenate(pieces, axis=0).astype(BF16)
    for wait in waits[2:]:
        wait()


def store_y_layers(r_ref, ref, upper):
    for c in range(0, COMPS, 2):
        def row(i, y):
            return r_ref[pl.ds((c + i) * 64 + y, 8, stride=8), :]

        lo = jnp.concatenate([row(i, y) for i in (0, 1) for y in range(3)], axis=0)
        hi = jnp.concatenate([row(i, y) for i in (0, 1) for y in range(5, 8)], axis=0)
        ref[pl.ds(c * 24, 48), :] = jnp.where(upper, hi, lo).astype(BF16)


def store_layers(refs, c, lo, hi, parity):
    for m, ref in enumerate(refs):
        ref[pl.ds(c * 24, 48), :] = jnp.where(parity == m, hi, lo).astype(BF16)


def put_table_kernel(table_ref, x_ref, out_ref):
    start = COMPS * 24
    rows = x_ref.shape[0] - start
    pieces = list(split3(table_ref[...]))
    used = 3 * table_ref.shape[0]
    if rows > used:
        pieces.append(jnp.zeros((rows - used, 128), F32))
    out_ref[pl.ds(start, rows), :] = jnp.concatenate(pieces, axis=0).astype(BF16)


def put_table(table, x):
    return pl.pallas_call(
        put_table_kernel,
        out_shape=jax.ShapeDtypeStruct(x.shape, x.dtype),
        in_specs=[VM] * 2,
        out_specs=VM,
        input_output_aliases={1: 0},
        compiler_params=GRANT,
        cost_estimate=cost(0.2),
        name="put_table",
    )(table, x)


def in_hbm(x):
    return pltpu.with_memory_space_constraint(x, pltpu.HBM)


def load_rows(height):
    return -(-3 * height // 16) * 16


def pack(fields, panels, react, layers, height):
    whole = jax.ShapeDtypeStruct((COMPS * 64, 128), F32)
    outs = [whole, whole]
    outs.append(jax.ShapeDtypeStruct((COMPS * 24 + load_rows(height), 128), BF16))
    outs.append(jax.ShapeDtypeStruct((height, 128), F32))
    one, _, _, four = layers
    kept = [jax.ShapeDtypeStruct(x.shape, x.dtype) for x in (react, one, four)]
    outs += kept
    return pl.pallas_call(
        pack_kernel,
        out_shape=outs,
        in_specs=[HBM] * 5,
        out_specs=[VM] * len(outs),
        scratch_shapes=[
            pltpu.VMEM((128, 128), F32),
            pltpu.VMEM(panels.shape, jnp.int32),
            pltpu.SemaphoreType.DMA((5,)),
        ],
        compiler_params=GRANT,
        cost_estimate=cost(2),
        name="pack",
    )(*map(in_hbm, (fields, panels, react, one, four)))


def turn_kernel(pair_x, r_ref, zt_ref, *refs):
    x_refs, (z1_ref, z2_ref, token) = refs[: 2 - pair_x], refs[2 - pair_x :]
    z_refs = (z1_ref, z2_ref)
    flags = place_flags()
    for c in range(0, COMPS, 2):
        lo = jnp.concatenate([r_ref[pl.ds((c + i) * 64, 24), :] for i in (0, 1)], axis=0)
        hi = jnp.concatenate([r_ref[pl.ds((c + i) * 64 + 40, 24), :] for i in (0, 1)], axis=0)
        store_layers(x_refs, c, lo, hi, flags[6])
    low = half_lanes((64, 128))
    for c in range(0, COMPS, 2):
        t = jnp.transpose(r_ref[pl.ds(c * 64, 128), :])
        top, bottom = t[:64], t[64:]
        even = jnp.where(low, top, swap_halves(bottom))
        odd = jnp.where(low, swap_halves(top), bottom)
        for i, x in ((0, even), (1, odd)):
            zt_ref[pl.ds((c + i) * 64, 64), :] = x
            for m, ref in enumerate(z_refs):
                up = flags[8] == m
                ref[pl.ds((c + i) * 3, 3), :] = jnp.where(up, x[61:], x[:3])
    for ref, start in [(x, COMPS * 24) for x in x_refs] + [(z, COMPS * 3) for z in z_refs]:
        if ref.shape[0] > start:
            ref[pl.ds(start, ref.shape[0] - start), :] = jnp.zeros(
                (ref.shape[0] - start, 128), ref.dtype
            )
    token[...] = jnp.zeros(token.shape, F32)


def turn(recon, pair_x, height):
    layer_x = jax.ShapeDtypeStruct((COMPS * 24 + (load_rows(height) if pair_x else 0), 128), BF16)
    edge = jax.ShapeDtypeStruct((40 + -(-height // 8) * 8, 128), F32)
    outs = [jax.ShapeDtypeStruct(recon.shape, F32)] + [layer_x] * (2 - pair_x) + [edge] * 2
    outs.append(jax.ShapeDtypeStruct((height, 128), F32))
    return pl.pallas_call(
        lambda *a: turn_kernel(int(pair_x), *a),
        out_shape=outs,
        in_specs=[VM],
        out_specs=[VM] * len(outs),
        compiler_params=GRANT,
        cost_estimate=cost(1),
        name="turn",
    )(recon)


def cost(us):
    return pl.CostEstimate(flops=int(us * 0.8e9), transcendentals=0, bytes_accessed=int(us * 2.8e6))


def dot(a, b):
    return jnp.dot(a, b, preferred_element_type=F32)


def gelu(x):
    half = 0.5 * x
    root = (2.0 / 3.141592653589793) ** 0.5
    return half + half * jnp.tanh(x * (root + (0.044715 * root) * (x * x)))


def iota(shape, dim):
    return lax.broadcasted_iota(jnp.int32, shape, dim)


def where1(mask):
    return jnp.where(mask, 1.0, 0.0).astype(BF16)


def chem_in_kernel(
    slots, r_ref, react_ref, w1_ref, h_ref, row_ref, hit_ref, y2_ref, token
):
    store_y_layers(r_ref, y2_ref, place_flags()[7] == 1)
    react = react_ref[...].astype(F32)
    react_b = react.astype(BF16)
    upper = where1(iota((128, 128), 0) <= iota((128, 128), 1))
    within = dot(react_b, upper)
    count = dot(react_b, jnp.ones((128, 128), BF16))
    below = where1(iota((64, 64), 1) < iota((64, 64), 0))
    offset = dot(below, count.astype(BF16))
    rank = (react * (within + offset)).astype(BF16)
    slot_lane = iota((64, slots), 1).astype(F32)
    off_col, cnt_col = offset[:, :1], count[:, :1]
    row_ref[...] = where1((slot_lane >= off_col) & (slot_lane < off_col + cnt_col))
    nt = (((1,), (1,)), ((), ()))
    count_row = lax.dot_general(
        jnp.ones((8, 128), BF16), react_b, nt, preferred_element_type=F32
    )
    offset_row = lax.dot_general(
        count_row.astype(BF16), below, nt, preferred_element_type=F32
    )
    slot_sub = iota((slots, 64), 0).astype(F32)
    slot_row = where1(
        (slot_sub >= offset_row[:1]) & (slot_sub < offset_row[:1] + count_row[:1])
    )
    lane_hit = dot(slot_row, rank) == iota((slots, 128), 0).astype(F32) + 1.0
    hit_ref[...] = where1(lane_hit)
    feat = jnp.zeros((slots, 128), F32)
    for c in range(COMPS):
        rows = dot(slot_row, r_ref[pl.ds(c * 64, 64), :].astype(BF16))
        hit = jnp.where(lane_hit, rows, 0.0).astype(BF16)
        feat = feat + dot(hit, where1(iota((128, 128), 1) == c))
    feat = jnp.transpose(feat)[:COMPS].astype(BF16)
    tn = (((0,), (0,)), ((), ()))
    one = lax.dot_general(w1_ref[...], feat, tn, preferred_element_type=F32)
    h_ref[...] = gelu(one).astype(BF16)
    token[...] = jnp.zeros(token.shape, F32)


def chem_in(recon, react, layer_one, slots, table):
    return pl.pallas_call(
        lambda *a: chem_in_kernel(slots, *a),
        out_shape=[
            jax.ShapeDtypeStruct((layer_one.shape[1], slots), BF16),
            jax.ShapeDtypeStruct((64, slots), BF16),
            jax.ShapeDtypeStruct((slots, 128), BF16),
            jax.ShapeDtypeStruct((COMPS * 24, 128), BF16),
            token_shape(table),
        ],
        in_specs=[VM] * 3,
        out_specs=[VM] * 5,
        compiler_params=GRANT,
        cost_estimate=cost(1),
        name="chem_in",
    )(recon, react, layer_one)


def chem_two_kernel(h_ref, w2_ref, out_ref, token):
    half = out_ref.shape[0]
    out_ref[...] = gelu(dot(w2_ref[pl.ds(0, half), :], h_ref[...])).astype(BF16)
    token[...] = jnp.zeros(token.shape, F32)


def chem_three_kernel(h_ref, two_ref, w2_ref, w3_ref, _, out_ref, token):
    half = two_ref.shape[0]
    rest = gelu(dot(w2_ref[pl.ds(half, half), :], h_ref[...])).astype(BF16)
    two = jnp.concatenate([two_ref[...], rest], axis=0)
    out_ref[...] = gelu(dot(w3_ref[...], two)).astype(BF16)
    token[...] = jnp.zeros(token.shape, F32)


def chem_layer(kernel, rows, table, *operands):
    return pl.pallas_call(
        kernel,
        out_shape=[
            jax.ShapeDtypeStruct((rows, operands[0].shape[1]), BF16),
            token_shape(table),
        ],
        in_specs=[VM] * len(operands),
        out_specs=[VM] * 2,
        compiler_params=GRANT,
        cost_estimate=cost(1),
    )(*operands)


def chem_out_kernel(h_ref, w4_ref, row_ref, hit_ref, _, out_ref, token):
    rates = dot(w4_ref[...], h_ref[...])
    slots = rates.shape[1]
    rates = jnp.concatenate([rates, jnp.zeros((128 - COMPS, slots), F32)], axis=0)
    rates_t = jnp.transpose(rates).astype(BF16)
    hit, row_slot = hit_ref[...].astype(F32), row_ref[...]
    for c in range(COMPS):
        spread = hit * dot(rates_t, where1(iota((128, 128), 0) == c))
        out_ref[pl.ds(c * 64, 64), :] = dot(row_slot, spread.astype(BF16))
    token[...] = jnp.zeros(token.shape, F32)


def chem_out(hidden, layer_four, row_slot, hit, table):
    return pl.pallas_call(
        chem_out_kernel,
        out_shape=[jax.ShapeDtypeStruct((COMPS * 64, 128), F32), token_shape(table)],
        in_specs=[VM] * 5,
        out_specs=[VM] * 2,
        compiler_params=GRANT,
        cost_estimate=cost(1),
        name="chem_out",
    )(hidden, layer_four, row_slot, hit, table)


def halo_lines(refs, scratch, own, sign_comp, at_wall, order, second):
    for c in range(0, COMPS, 2):
        block = refs[0][pl.ds(c * 24, 48), :].astype(F32)
        if len(refs) == 2:
            block = jnp.where(second, refs[1][pl.ds(c * 24, 48), :].astype(F32), block)
        for i in (0, 1):
            for k in range(3):
                mirror = own(c + i, order[k])
                if c + i == sign_comp:
                    mirror = -mirror
                got = block[(i * 3 + k) * 8 : (i * 3 + k + 1) * 8]
                scratch[pl.ds(((c + i) * 3 + k) * 8, 8), :] = jnp.where(at_wall, mirror, got)


def flux_x_inner_kernel(
    f_ref, r_ref, acc_ref, src_ref, left, right, edge_ref, out_ref, token
):
    def line(c):
        return [None] * 3 + [r_ref[rows8(c * 8 + x), :] for x in range(8)] + [None] * 3

    face_states(line, left, right, 9, ((5, 8),))
    flux = {f: face_flux(left, right, 9, 0, f) for f in (3, 4, 5)}
    for c in range(COMPS):
        edge_ref[pl.ds(c * 16, 8), :] = flux[3][c]
        edge_ref[pl.ds(c * 16 + 8, 8), :] = flux[5][c]
        for x in range(8):
            at = pl.ds(c * 64 + x * 8, 8)
            change = acc_ref[at, :]
            if x in (3, 4):
                change = change + (flux[x + 1][c] - flux[x][c])
            new = f_ref[at, :] - TIME_STEP * change + CHEM_STEP * src_ref[at, :]
            out_ref[c, pl.ds(x * 8, 8), :] = new
    token[...] = jnp.zeros(token.shape, F32)


def flux_x_kernel(count, r_ref, left_in, right_in, edge_ref, base_ref, *refs):
    flags = place_flags()
    layers, (out_hbm, lo_s, hi_s, left, right, out_ref, sems) = refs[:count], refs[count:]

    def send(ref, first, planes):
        rows = pl.ds(first * 8, planes * 8)
        copy = pltpu.make_async_copy(ref.at[:, rows], out_hbm.at[:, rows], sems.at[first])
        copy.start()
        return copy

    copies = [send(base_ref, 3, 2)]

    def own(c, x):
        return r_ref[pl.ds(c * 64 + x * 8, 8), :]

    halo_lines(layers, lo_s, own, 1, flags[0], (2, 1, 0), flags[6] == 0)
    halo_lines(layers, hi_s, own, 1, flags[1], (7, 6, 5), flags[6] == 1)

    def line(c):
        return (
            [lo_s[rows8(c * 3 + k), :] for k in range(3)]
            + [r_ref[rows8(c * 8 + x), :] for x in range(8)]
            + [hi_s[rows8(c * 3 + k), :] for k in range(3)]
        )

    face_states(line, left, right, 9, ((2, 4), (9, 11)))
    for c in range(COMPS):
        at = pl.ds((c * 9 + 2) * 8, 8)
        right[at, :] = right_in[at, :]
        at = pl.ds((c * 9 + 6) * 8, 8)
        left[at, :] = left_in[at, :]

    def emit(x, upper, lower):
        plane = pl.ds(x * 8, 8)
        for c in range(COMPS):
            out_ref[c, plane, :] = base_ref[c, plane, :] - TIME_STEP * (upper[c] - lower[c])
        copies.append(send(out_ref, x, 1))

    flux = {
        3: [edge_ref[pl.ds(c * 16, 8), :] for c in range(COMPS)],
        5: [edge_ref[pl.ds(c * 16 + 8, 8), :] for c in range(COMPS)],
    }
    for f in (2, 1, 0):
        flux[f] = face_flux(left, right, 9, 0, f)
        emit(f, flux[f + 1], flux.pop(f) if f == 0 else flux[f])
    for f in (6, 7, 8):
        flux[f] = face_flux(left, right, 9, 0, f)
        emit(f - 1, flux[f], flux[f - 1])
    for copy in copies:
        copy.wait()


def flux_y_kernel(count, r_ref, *refs):
    flags = place_flags()
    layers, (out_ref, token, lo_s, hi_s, left, right) = refs[:count], refs[count:]

    def own(c, y):
        return r_ref[pl.ds(c * 64 + y, 8, stride=8), :]

    halo_lines(layers, lo_s, own, 2, flags[2], (2, 1, 0), flags[7] == 0)
    halo_lines(layers, hi_s, own, 2, flags[3], (7, 6, 5), flags[7] == 1)

    def line(c):
        return (
            [lo_s[rows8(c * 3 + k), :] for k in range(3)]
            + [r_ref[pl.ds(c * 64 + y, 8, stride=8), :] for y in range(8)]
            + [hi_s[rows8(c * 3 + k), :] for k in range(3)]
        )

    face_states(line, left, right, 9)

    def emit(c, y, change):
        out_ref[pl.ds(c * 64 + y, 8, stride=8), :] = change

    line_changes(left, right, 9, 1, emit)
    token[...] = jnp.zeros(token.shape, F32)


def flux_z_kernel(count, zt_ref, acc_ref, *refs):
    flags = place_flags()
    layers, (out_ref, token, ext, left, right, back) = refs[:count], refs[count:]
    low3, low = half_lanes((3, 128)), half_lanes((64, 128))

    def got(c, second):
        x = layers[0][pl.ds(c * 3, 3), :]
        if count == 2:
            x = jnp.where(second, layers[1][pl.ds(c * 3, 3), :], x)
        return swap_halves(x)

    for c in range(COMPS):
        sign = -1.0 if c == 3 else 1.0
        own = zt_ref[pl.ds(c * 64, 64), :]
        first, last = own[:3], own[61:]
        mirror_lo = sign * jnp.concatenate([first[2:3], first[1:2], first[0:1]], axis=0)
        mirror_hi = sign * jnp.concatenate([last[2:3], last[1:2], last[0:1]], axis=0)
        below = jnp.where(flags[4], mirror_lo, got(c, flags[8] == 0))
        above = jnp.where(flags[5], mirror_hi, got(c, flags[8] == 1))
        ext[pl.ds(c * 72, 3), :] = jnp.where(low3, below, swap_halves(last))
        ext[pl.ds(c * 72 + 3, 64), :] = own
        ext[pl.ds(c * 72 + 67, 3), :] = jnp.where(low3, swap_halves(first), above)

    def line(c):
        return [ext[pl.ds(c * 72 + e, 8, stride=8), :] for e in range(14)]

    face_states(line, left, right, 9)

    def emit(c, z, change):
        back[pl.ds(c * 64 + z, 8, stride=8), :] = change

    line_changes(left, right, 9, 2, emit)
    for c in range(0, COMPS, 2):
        even, odd = back[pl.ds(c * 64, 64), :], back[pl.ds(c * 64 + 64, 64), :]
        t = jnp.concatenate(
            [jnp.where(low, even, swap_halves(odd)), jnp.where(low, swap_halves(even), odd)],
            axis=0,
        )
        at = pl.ds(c * 64, 128)
        out_ref[at, :] = acc_ref[at, :] + jnp.transpose(t)
    token[...] = jnp.zeros(token.shape, F32)


def impulse_kernel(own, table_ref, got_ref, out_ref):
    place = place_flags()[9] * own
    row = pl.ds(place // 128, 1)
    loads = jnp.broadcast_to(table_ref[row, :] + got_ref[row, :], (8, 128))
    loads = pltpu.roll(loads, (128 - place % 128) % 128, 1)
    out_ref[...] = loads[:1, :own] * (1.0 / (PATCH * PATCH))


def own_impulse(table, got, own):
    return pl.pallas_call(
        lambda *a: impulse_kernel(own, *a),
        out_shape=jax.ShapeDtypeStruct((1, own), F32),
        in_specs=[VM] * 2,
        out_specs=VM,
        compiler_params=GRANT,
        cost_estimate=cost(0.5),
        name="impulse",
    )(table, got)


def state_scratch():
    return [pltpu.VMEM((COMPS * 9 * 8, 128), F32)] * 2


def halo_scratch():
    return [pltpu.VMEM((COMPS * 24, 128), F32)] * 2


def token_shape(table):
    return jax.ShapeDtypeStruct(table.shape, F32)


def flux_x_inner(fields, recon, acc, source, table):
    states = jax.ShapeDtypeStruct((COMPS * 9 * 8, 128), F32)
    return pl.pallas_call(
        flux_x_inner_kernel,
        out_shape=[
            states,
            states,
            jax.ShapeDtypeStruct((COMPS * 16, 128), F32),
            jax.ShapeDtypeStruct((COMPS, 64, 128), F32),
            token_shape(table),
        ],
        in_specs=[VM] * 4,
        out_specs=[VM] * 5,
        compiler_params=GRANT,
        cost_estimate=cost(1),
        name="flux_x_inner",
    )(fields, recon, acc, source)


def flux_x(recon, inner, layers):
    return pl.pallas_call(
        lambda *a: flux_x_kernel(len(layers), *a),
        out_shape=jax.ShapeDtypeStruct((COMPS, 64, 128), F32),
        in_specs=[VM] * (5 + len(layers)),
        out_specs=HBM,
        scratch_shapes=halo_scratch()
        + state_scratch()
        + [pltpu.VMEM((COMPS, 64, 128), F32), pltpu.SemaphoreType.DMA((8,))],
        compiler_params=GRANT,
        cost_estimate=cost(2),
        name="flux_x",
    )(recon, *inner, *layers)


def flux_y(recon, layers, table):
    return pl.pallas_call(
        lambda *a: flux_y_kernel(len(layers), *a),
        out_shape=[jax.ShapeDtypeStruct(recon.shape, F32), token_shape(table)],
        in_specs=[VM] * (1 + len(layers)),
        out_specs=[VM] * 2,
        scratch_shapes=halo_scratch() + state_scratch(),
        compiler_params=GRANT,
        cost_estimate=cost(2),
        name="flux_y",
    )(recon, *layers)


def flux_z(turned, acc, layers, table):
    return pl.pallas_call(
        lambda *a: flux_z_kernel(len(layers), *a),
        out_shape=[jax.ShapeDtypeStruct(acc.shape, F32), token_shape(table)],
        in_specs=[VM] * (2 + len(layers)),
        out_specs=[VM] * 2,
        scratch_shapes=[pltpu.VMEM((COMPS * 72, 128), F32)]
        + state_scratch()
        + [pltpu.VMEM(acc.shape, F32)],
        compiler_params=GRANT,
        cost_estimate=cost(2),
        name="flux_z",
    )(turned, acc, *layers)


def swap(x, axis, second, outer=False):
    n = lax.axis_size(axis)
    pairs = [(i, i + 1) for i in range(int(second), n - 1, 2)]
    if outer:
        pairs.append((0, n - 1))
    return lax.ppermute(x, axis, [(a, b) for a, b in pairs] + [(b, a) for a, b in pairs])


def swap_inner(x, axis, other):
    n, m = lax.axis_size(axis), lax.axis_size(other)
    if m % 2 or n % 2:
        return swap(x, axis, 1)
    pairs = []
    for i in range(n):
        for j in range(m):
            end = i in (0, n - 1)
            to = (i, j ^ 1) if end else (i + 1 if i % 2 else i - 1, j)
            pairs.append((i * m + j, to[0] * m + to[1]))
    return lax.ppermute(x, (axis, other), pairs)


def sum_over(table, axis, step=1):
    size = lax.axis_size(axis)
    if size & (size - 1):
        return lax.psum(table, axis)
    while step < size:
        table = table + lax.ppermute(table, axis, [(i, i ^ step) for i in range(size)])
        step *= 2
    return table


def join_table(rows, height):
    rows = rows[: 3 * height].astype(F32)
    return rows[:height] + rows[height : 2 * height] + rows[2 * height :]


def body(fields, reacting, panel_map, layer_one, layer_two, layer_three, layer_four):
    shape = fields.shape
    sizes = [lax.axis_size(a) for a in AXES]
    pair_x = sizes[0] == 2
    panels_all = 2 * (shape[1] * sizes[0] // PATCH) * (shape[3] * sizes[2] // PATCH)
    own = panels_all // (sizes[0] * sizes[1] * sizes[2])
    height = panels_all // 128
    slots = BAL * min(4, sizes[0])
    layer_rows, edge_rows = COMPS * 24, 40
    ride_y, ride_z = sizes[1] & (sizes[1] - 1) == 0, sizes[2] in (2, 4)

    flat = fields.reshape(-1, shape[3])
    panels, react = panel_map.reshape(-1, shape[3]), reacting.reshape(-1, shape[3])
    layers = (layer_one.T, layer_two, layer_three, layer_four)
    packed = pack(flat, panels, react, layers, height)
    flat, recon, y_first, table, react, one, four = packed
    two, three = layer_two, layer_three
    y_got = [swap(y_first, "gy", 0)]
    turned, *xs, z_first, z_second, token = turn(recon, pair_x, height)
    hidden, row_slot, hit, y_second, token_in = chem_in(recon, react, one, slots, table)
    if sizes[1] > 2:
        y_got.append(swap_inner(y_second, "gy", "gz"))
    half, token_two = chem_layer(chem_two_kernel, layer_two.shape[0] // 2, table, hidden, two)
    table = table + token + token_in + token_two
    if ride_y:
        table = table + join_table(y_got[0][layer_rows:], height)
    if not ride_z:
        table = sum_over(table, "gz")
    z_got = [swap(lax.dynamic_update_slice(z_first, table, (edge_rows, 0)), "gz", 0)]
    hidden, token = chem_layer(
        chem_three_kernel, layer_three.shape[0], table, hidden, half, two, three, table
    )
    if ride_z:
        table = table + z_got[0][edge_rows : edge_rows + height] + token
    if sizes[2] > 2:
        z_second = lax.dynamic_update_slice(z_second, table, (edge_rows, 0))
        z_got.append(swap(z_second, "gz", 1, ride_z))
        if ride_z:
            table = table + z_got[1][edge_rows : edge_rows + height]
    acc, token = flux_y(recon, y_got, table)
    table = table + token
    if pair_x:
        xs = [put_table(table, xs[0])]
    x_got = [swap(x, "gx", m) for m, x in enumerate(xs)]
    acc, token = flux_z(turned, acc, z_got, table)
    source, token_out = chem_out(hidden, four, row_slot, hit, table)
    *inner, token_inner = flux_x_inner(flat, recon, acc, source, table)
    table = table + token + token_out + token_inner
    if pair_x:
        table = table + join_table(x_got[0][layer_rows:], height)
    else:
        table = sum_over(table, "gx")
    rest = jnp.zeros_like(table)
    if not ride_y:
        table = lax.psum(table, "gy")
    elif sizes[1] > 2:
        table = sum_over(table, "gy", 4)
        n, m = sizes[1], sizes[2]
        flip = 1 - m % 2
        pairs = [(i * m + j, (i ^ 2) * m + (j ^ flip)) for i in range(n) for j in range(m)]
        rest = lax.ppermute(table, ("gy", "gz"), pairs)
    new = flux_x(recon, inner, x_got)
    return new.reshape(shape), own_impulse(table, rest, own).reshape(own)


def solution(mesh):
    return jax.shard_map(
        body,
        mesh=mesh,
        in_specs=(
            P(None, "gx", "gy", "gz"),
            P("gx", "gy", "gz"),
            P(None, "gx", "gz"),
            P(),
            P(),
            P(),
            P(),
        ),
        out_specs=(P(None, "gx", "gy", "gz"), P(("gx", "gy", "gz"))),
        check_vma=False,
    )
```

```python
import jax
import jax.numpy as jnp
from jax import lax
from jax.experimental import pallas as pl
from jax.experimental.pallas import tpu as pltpu
from jax.sharding import PartitionSpec as P


BAL = 64
COMPS = 12
PATCH = 8

HEAT_RATIO = 1.4
TIME_STEP = 0.1
CHEM_STEP = 0.25
WENO_EPS = 1e-06
EPS = WENO_EPS * 4.0 / 36.0
AXES = ("gx", "gy", "gz")
F32 = jnp.float32
BF16 = jnp.bfloat16
GRANT = pltpu.CompilerParams(vmem_limit_bytes=12 * 2**20)
VM = pl.BlockSpec(memory_space=pltpu.VMEM)
HBM = pl.BlockSpec(memory_space=pltpu.HBM)


def weno_line(v, first, last):
    n = len(v)
    low, high = max(first - 2, 0), min(last + 2, n - 1)
    d = {j: (v[j + 1] - v[j]) * (1.0 / 6.0) for j in range(low, high)}
    d3 = {j: 3.0 * d[j] for j in range(low + 1, high - 1)}
    q = {}
    for e in range(low + 1, high):
        s = d[e] - d[e - 1]
        q[e] = (13.0 / 3.0) * (s * s) + EPS
    upper, lower = {}, {}
    for e in range(first, last + 1):
        dm, dp = d[e - 1], d[e]
        t0 = d3[e - 1] - d[e - 2]
        t1 = dm + dp
        t2 = d3[e] - d[e + 1]
        b0 = q[e - 1] + t0 * t0
        b1 = q[e] + t1 * t1
        b2 = q[e + 1] + t2 * t2
        m01, m02, m12 = b0 * b1, b0 * b2, b1 * b2
        s01, s02, s12 = m01 * m01, m02 * m02, m12 * m12
        w1, w01, w12 = 6.0 * s02, 3.0 * s01, 3.0 * s12
        if e < n - 3:
            num = s12 * (t0 + t0 - dm) + w1 * (t1 + dp) + w01 * (t2 + dp)
            upper[e] = v[e] + num / (s12 + w1 + w01)
        if e > 2:
            num = s01 * (t2 + t2 - dp) + w1 * (t1 + dm) + w12 * (t0 + dm)
            lower[e] = v[e] - num / (s01 + w1 + w12)
    return upper, lower


def weno_one(v):
    d = [(v[j + 1] - v[j]) * (1.0 / 6.0) for j in range(4)]
    s = [d[j + 1] - d[j] for j in range(3)]
    q = [(13.0 / 3.0) * (x * x) + EPS for x in s]
    dm, dp = d[1], d[2]
    t0, t1, t2 = 3.0 * dm - d[0], dm + dp, 3.0 * dp - d[3]
    b0, b1, b2 = q[0] + t0 * t0, q[1] + t1 * t1, q[2] + t2 * t2
    m01, m02, m12 = b0 * b1, b0 * b2, b1 * b2
    w0, w1, w2 = m12 * m12, 6.0 * (m02 * m02), 3.0 * (m01 * m01)
    num = w0 * (t0 + t0 - dm) + w1 * (t1 + dp) + w2 * (t2 + dp)
    return v[2] + num / (w0 + w1 + w2)


def hllc(left, right, normal):
    n = 1 + normal

    def side(x):
        rho = jnp.exp(x[0])
        g = jnp.exp(0.5 * (x[4] - x[0]))
        h = g * g
        return rho, h, rho * h, (HEAT_RATIO**0.5) * g, x[n]

    rho_l, h_l, p_l, c_l, u_l = side(left)
    rho_r, h_r, p_r, c_r, u_r = side(right)
    s_l = jnp.minimum(u_l - c_l, u_r - c_r)
    s_r = jnp.maximum(u_l + c_l, u_r + c_r)
    m_l = rho_l * (s_l - u_l)
    m_r = rho_r * (s_r - u_r)
    s = (p_r - p_l + u_l * m_l - u_r * m_r) / (m_l - m_r)
    use_l = (s >= 0) | (s_l >= 0)
    pick = [jnp.where(use_l, a, b) for a, b in zip(left, right)]
    rho = jnp.where(use_l, rho_l, rho_r)
    h = jnp.where(use_l, h_l, h_r)
    p = jnp.where(use_l, p_l, p_r)
    wave = jnp.where(use_l, s_l, s_r)
    act = jnp.where(use_l, jnp.minimum(s_l, 0.0), jnp.maximum(s_r, 0.0))
    u = pick[n]
    rel = s - u
    ratio = rel / (wave - s)
    mass = rho * (u + act * ratio)
    k = rho * act * (1.0 + ratio) * rel
    square = pick[1] * pick[1] + pick[2] * pick[2] + pick[3] * pick[3]
    enthalpy = (1.0 / (HEAT_RATIO - 1.0) + 1.0) * h + 0.5 * square
    flux = [mass * x for x in pick]
    flux[0] = mass
    flux[n] = flux[n] + (p + k)
    flux[4] = enthalpy * mass + k * s
    return flux


def place_flags():
    sizes = [lax.axis_size(a) for a in AXES]
    index = [lax.axis_index(a) for a in AXES]
    place = (index[0] * sizes[1] + index[1]) * sizes[2] + index[2]
    flags = [f for i, n in zip(index, sizes) for f in (i == 0, i == n - 1)]
    return flags + [lax.rem(i, 2) for i in index] + [place]


def rows8(index):
    return pl.ds(pl.multiple_of(index * 8, 8), 8)


def face_states(load_line, left_ref, right_ref, faces, spans=((2, 11),)):
    def one(c, carry):
        line = load_line(c)
        for first, last in spans:
            upper, lower = weno_line(line, first, last)
            for e, x in upper.items():
                left_ref[rows8(c * faces + e - 2), :] = x
            for e, x in lower.items():
                right_ref[rows8(c * faces + e - 3), :] = x
        return carry

    lax.fori_loop(0, COMPS, one, 0)


def face_flux(left_ref, right_ref, faces, normal, f):
    left = [left_ref[pl.ds((c * faces + f) * 8, 8), :] for c in range(COMPS)]
    right = [right_ref[pl.ds((c * faces + f) * 8, 8), :] for c in range(COMPS)]
    return hllc(left, right, normal)


def line_changes(left_ref, right_ref, faces, normal, emit):
    before = None
    for f in range(faces):
        flux = face_flux(left_ref, right_ref, faces, normal, f)
        if before is not None:
            for c in range(COMPS):
                emit(c, f - 1, flux[c] - before[c])
        before = flux


def half_lanes(shape):
    return lax.broadcasted_iota(jnp.int32, shape, 1) < 64


def swap_halves(x):
    return pltpu.roll(x, 64, 1)


def split3(x):
    hi = x.astype(BF16).astype(F32)
    mid = (x - hi).astype(BF16).astype(F32)
    return hi, mid, x - hi - mid


def fetch(source, target, sem, parts=1):
    step = -(-source.shape[0] // (parts * 16)) * 16
    for start in range(0, source.shape[0], step):
        rows = pl.ds(start, min(step, source.shape[0] - start))
        pltpu.make_async_copy(source.at[rows], target.at[rows], sem).start()
    return pltpu.make_async_copy(source, target, sem).wait


def pack_kernel(*refs):
    f_hbm, map_hbm, *sources = refs[:3]
    f_ref, r_ref, y1_ref, table_ref, *kept = refs[3:8]
    buf, map_ref, sems = refs[8:]
    pairs = [(f_hbm, f_ref, 8), (map_hbm, map_ref, 1)]
    pairs += list(zip(sources, kept, (1,)))
    waits = [fetch(a, b, sems.at[i], parts) for i, (a, b, parts) in enumerate(pairs)]
    flags = place_flags()
    waits[0]()
    for x in range(8):
        def at(c):
            return f_ref[pl.ds(c * 64 + x * 8, 8), :]

        rho = at(0)
        inv = 1.0 / rho
        u = [at(c) * inv for c in (1, 2, 3)]
        p = (HEAT_RATIO - 1.0) * (
            at(4) - 0.5 * rho * (u[0] * u[0] + u[1] * u[1] + u[2] * u[2])
        )
        out = [jnp.log(rho)] + u + [jnp.log(p)] + [at(c) * inv for c in range(5, COMPS)]
        for c in range(COMPS):
            r_ref[pl.ds(c * 64 + x * 8, 8), :] = out[c]
    pushes = []
    for wall in range(2):
        rows = (0, 1, 2) if wall == 0 else (7, 6, 5)
        state = []
        for c in (0, 2, 4):
            a = [r_ref[pl.ds(c * 64 + y, 8, stride=8), :] for y in rows]
            sign = -1.0 if c == 2 else 1.0
            state.append(weno_one([a[2], a[1], a[0], sign * a[0], sign * a[1]]))
        rho = jnp.exp(state[0])
        p = jnp.exp(state[2])
        out_speed = -state[1] if wall == 0 else state[1]
        speed = jnp.abs(out_speed) + jnp.sqrt(HEAT_RATIO * p / rho)
        push = p + rho * out_speed * (out_speed + speed)
        x = jnp.where(flags[2 + wall], push, 0.0)
        for s in (1, 2, 4):
            x = x + pltpu.roll(x, 128 - s, 1)
        for s in (1, 2):
            x = x + pltpu.roll(x, 8 - s, 0)
        pushes.append(x)
    waits[1]()
    ids = map_ref[...].astype(F32)
    tall = jnp.concatenate(pushes + [ids, jnp.zeros((96, 128), F32)], axis=0)
    buf[...] = jnp.transpose(tall)
    groups = [buf[pl.ds(64 * g, 8, stride=8), :] for g in range(2)]
    lane = lax.broadcasted_iota(jnp.int32, (8, 128), 1).astype(F32)
    columns = []
    for g in groups:
        for col in (0, 4, 8, 12):
            columns.append(
                (
                    jnp.broadcast_to(g[:, col : col + 1], (8, 128)),
                    jnp.broadcast_to(g[:, 16 + col : 17 + col], (8, 128)),
                )
            )
    table = []
    for j in range(table_ref.shape[0]):
        total = jnp.zeros((8, 128), F32)
        for load, panel in columns:
            total = total + jnp.where(panel == lane + 128.0 * j, load, 0.0)
        table.append(jnp.sum(total, axis=0, keepdims=True))
        table_ref[pl.ds(j, 1), :] = table[j]
    store_y_layers(r_ref, y1_ref, flags[7] == 0)
    rows = y1_ref.shape[0] - COMPS * 24
    pieces = [piece[j] for piece in zip(*map(split3, table)) for j in range(len(table))]
    if rows > len(pieces):
        pieces.append(jnp.zeros((rows - len(pieces), 128), F32))
    y1_ref[pl.ds(COMPS * 24, rows), :] = jnp.concatenate(pieces, axis=0).astype(BF16)
    for wait in waits[2:]:
        wait()


def store_y_layers(r_ref, ref, upper):
    for c in range(0, COMPS, 2):
        def row(i, y):
            return r_ref[pl.ds((c + i) * 64 + y, 8, stride=8), :]

        lo = jnp.concatenate([row(i, y) for i in (0, 1) for y in range(3)], axis=0)
        hi = jnp.concatenate([row(i, y) for i in (0, 1) for y in range(5, 8)], axis=0)
        ref[pl.ds(c * 24, 48), :] = jnp.where(upper, hi, lo).astype(BF16)


def store_layers(refs, c, lo, hi, parity):
    for m, ref in enumerate(refs):
        ref[pl.ds(c * 24, 48), :] = jnp.where(parity == m, hi, lo).astype(BF16)


def put_table_kernel(table_ref, x_ref, out_ref):
    start = COMPS * 24
    rows = x_ref.shape[0] - start
    pieces = list(split3(table_ref[...]))
    used = 3 * table_ref.shape[0]
    if rows > used:
        pieces.append(jnp.zeros((rows - used, 128), F32))
    out_ref[pl.ds(start, rows), :] = jnp.concatenate(pieces, axis=0).astype(BF16)


def put_table(table, x):
    return pl.pallas_call(
        put_table_kernel,
        out_shape=jax.ShapeDtypeStruct(x.shape, x.dtype),
        in_specs=[VM] * 2,
        out_specs=VM,
        input_output_aliases={1: 0},
        compiler_params=GRANT,
        cost_estimate=cost(0.2),
        name="put_table",
    )(table, x)


def in_hbm(x):
    return pltpu.with_memory_space_constraint(x, pltpu.HBM)


def load_rows(height):
    return -(-3 * height // 16) * 16


def pack(fields, panels, react, layers, height):
    whole = jax.ShapeDtypeStruct((COMPS * 64, 128), F32)
    outs = [whole, whole]
    outs.append(jax.ShapeDtypeStruct((COMPS * 24 + load_rows(height), 128), BF16))
    outs.append(jax.ShapeDtypeStruct((height, 128), F32))
    one, two, three, four = layers
    kept = [jax.ShapeDtypeStruct(x.shape, x.dtype) for x in (react,)]
    outs += kept
    return pl.pallas_call(
        pack_kernel,
        out_shape=outs,
        in_specs=[HBM] * 3,
        out_specs=[VM] * len(outs),
        scratch_shapes=[
            pltpu.VMEM((128, 128), F32),
            pltpu.VMEM(panels.shape, jnp.int32),
            pltpu.SemaphoreType.DMA((3,)),
        ],
        compiler_params=GRANT,
        cost_estimate=cost(2),
        name="pack",
    )(*map(in_hbm, (fields, panels, react)))


def turn_kernel(pair_x, r_ref, zt_ref, *refs):
    x_refs, (z1_ref, z2_ref, token) = refs[: 2 - pair_x], refs[2 - pair_x :]
    z_refs = (z1_ref, z2_ref)
    flags = place_flags()
    for c in range(0, COMPS, 2):
        lo = jnp.concatenate([r_ref[pl.ds((c + i) * 64, 24), :] for i in (0, 1)], axis=0)
        hi = jnp.concatenate([r_ref[pl.ds((c + i) * 64 + 40, 24), :] for i in (0, 1)], axis=0)
        store_layers(x_refs, c, lo, hi, flags[6])
    low = half_lanes((64, 128))
    for c in range(0, COMPS, 2):
        t = jnp.transpose(r_ref[pl.ds(c * 64, 128), :])
        top, bottom = t[:64], t[64:]
        even = jnp.where(low, top, swap_halves(bottom))
        odd = jnp.where(low, swap_halves(top), bottom)
        for i, x in ((0, even), (1, odd)):
            zt_ref[pl.ds((c + i) * 64, 64), :] = x
            for m, ref in enumerate(z_refs):
                up = flags[8] == m
                ref[pl.ds((c + i) * 3, 3), :] = jnp.where(up, x[61:], x[:3])
    for ref, start in [(x, COMPS * 24) for x in x_refs] + [(z, COMPS * 3) for z in z_refs]:
        if ref.shape[0] > start:
            ref[pl.ds(start, ref.shape[0] - start), :] = jnp.zeros(
                (ref.shape[0] - start, 128), ref.dtype
            )
    token[...] = jnp.zeros(token.shape, F32)


def turn(recon, pair_x, height):
    layer_x = jax.ShapeDtypeStruct((COMPS * 24 + (load_rows(height) if pair_x else 0), 128), BF16)
    edge = jax.ShapeDtypeStruct((40 + -(-height // 8) * 8, 128), F32)
    outs = [jax.ShapeDtypeStruct(recon.shape, F32)] + [layer_x] * (2 - pair_x) + [edge] * 2
    outs.append(jax.ShapeDtypeStruct((height, 128), F32))
    return pl.pallas_call(
        lambda *a: turn_kernel(int(pair_x), *a),
        out_shape=outs,
        in_specs=[VM],
        out_specs=[VM] * len(outs),
        compiler_params=GRANT,
        cost_estimate=cost(1),
        name="turn",
    )(recon)


def cost(us):
    return pl.CostEstimate(flops=int(us * 0.8e9), transcendentals=0, bytes_accessed=int(us * 2.8e6))


def dot(a, b):
    return jnp.dot(a, b, preferred_element_type=F32)


def gelu(x):
    half = 0.5 * x
    root = (2.0 / 3.141592653589793) ** 0.5
    return half + half * jnp.tanh(x * (root + (0.044715 * root) * (x * x)))


def iota(shape, dim):
    return lax.broadcasted_iota(jnp.int32, shape, dim)


def where1(mask):
    return jnp.where(mask, 1.0, 0.0).astype(BF16)


def chem_in_kernel(
    slots, r_ref, react_ref, w1_ref, h_ref, row_ref, hit_ref, y2_ref, token
):
    store_y_layers(r_ref, y2_ref, place_flags()[7] == 1)
    react = react_ref[...].astype(F32)
    react_b = react.astype(BF16)
    upper = where1(iota((128, 128), 0) <= iota((128, 128), 1))
    within = dot(react_b, upper)
    count = dot(react_b, jnp.ones((128, 128), BF16))
    below = where1(iota((64, 64), 1) < iota((64, 64), 0))
    offset = dot(below, count.astype(BF16))
    rank = (react * (within + offset)).astype(BF16)
    slot_lane = iota((64, slots), 1).astype(F32)
    off_col, cnt_col = offset[:, :1], count[:, :1]
    row_ref[...] = where1((slot_lane >= off_col) & (slot_lane < off_col + cnt_col))
    nt = (((1,), (1,)), ((), ()))
    count_row = lax.dot_general(
        jnp.ones((8, 128), BF16), react_b, nt, preferred_element_type=F32
    )
    offset_row = lax.dot_general(
        count_row.astype(BF16), below, nt, preferred_element_type=F32
    )
    slot_sub = iota((slots, 64), 0).astype(F32)
    slot_row = where1(
        (slot_sub >= offset_row[:1]) & (slot_sub < offset_row[:1] + count_row[:1])
    )
    lane_hit = dot(slot_row, rank) == iota((slots, 128), 0).astype(F32) + 1.0
    hit_ref[...] = where1(lane_hit)
    feat = jnp.zeros((slots, 128), F32)
    for c in range(COMPS):
        rows = dot(slot_row, r_ref[pl.ds(c * 64, 64), :].astype(BF16))
        hit = jnp.where(lane_hit, rows, 0.0).astype(BF16)
        feat = feat + dot(hit, where1(iota((128, 128), 1) == c))
    feat = jnp.transpose(feat)[:COMPS].astype(BF16)
    tn = (((0,), (0,)), ((), ()))
    one = lax.dot_general(w1_ref[...], feat, tn, preferred_element_type=F32)
    h_ref[...] = gelu(one).astype(BF16)
    token[...] = jnp.zeros(token.shape, F32)


def chem_in(recon, react, layer_one, slots, table):
    return pl.pallas_call(
        lambda *a: chem_in_kernel(slots, *a),
        out_shape=[
            jax.ShapeDtypeStruct((layer_one.shape[1], slots), BF16),
            jax.ShapeDtypeStruct((64, slots), BF16),
            jax.ShapeDtypeStruct((slots, 128), BF16),
            jax.ShapeDtypeStruct((COMPS * 24, 128), BF16),
            token_shape(table),
        ],
        in_specs=[VM] * 3,
        out_specs=[VM] * 5,
        compiler_params=GRANT,
        cost_estimate=cost(1),
        name="chem_in",
    )(recon, react, layer_one)


def chem_two_kernel(h_ref, w2_ref, out_ref, token):
    half = out_ref.shape[0]
    out_ref[...] = gelu(dot(w2_ref[pl.ds(0, half), :], h_ref[...])).astype(BF16)
    token[...] = jnp.zeros(token.shape, F32)


def chem_three_kernel(h_ref, two_ref, w2_ref, w3_ref, _, out_ref, token):
    half = two_ref.shape[0]
    rest = gelu(dot(w2_ref[pl.ds(half, half), :], h_ref[...])).astype(BF16)
    two = jnp.concatenate([two_ref[...], rest], axis=0)
    out_ref[...] = gelu(dot(w3_ref[...], two)).astype(BF16)
    token[...] = jnp.zeros(token.shape, F32)


def chem_layer(kernel, rows, table, *operands):
    return pl.pallas_call(
        kernel,
        out_shape=[
            jax.ShapeDtypeStruct((rows, operands[0].shape[1]), BF16),
            token_shape(table),
        ],
        in_specs=[VM] * len(operands),
        out_specs=[VM] * 2,
        compiler_params=GRANT,
        cost_estimate=cost(1),
    )(*operands)


def chem_out_kernel(h_ref, w4_ref, row_ref, hit_ref, _, out_ref, token):
    rates = dot(w4_ref[...], h_ref[...])
    slots = rates.shape[1]
    rates = jnp.concatenate([rates, jnp.zeros((128 - COMPS, slots), F32)], axis=0)
    rates_t = jnp.transpose(rates).astype(BF16)
    hit, row_slot = hit_ref[...].astype(F32), row_ref[...]
    for c in range(COMPS):
        spread = hit * dot(rates_t, where1(iota((128, 128), 0) == c))
        out_ref[pl.ds(c * 64, 64), :] = dot(row_slot, spread.astype(BF16))
    token[...] = jnp.zeros(token.shape, F32)


def chem_out(hidden, layer_four, row_slot, hit, table):
    return pl.pallas_call(
        chem_out_kernel,
        out_shape=[jax.ShapeDtypeStruct((COMPS * 64, 128), F32), token_shape(table)],
        in_specs=[VM] * 5,
        out_specs=[VM] * 2,
        compiler_params=GRANT,
        cost_estimate=cost(1),
        name="chem_out",
    )(hidden, layer_four, row_slot, hit, table)


def halo_lines(refs, scratch, own, sign_comp, at_wall, order, second):
    for c in range(0, COMPS, 2):
        block = refs[0][pl.ds(c * 24, 48), :].astype(F32)
        if len(refs) == 2:
            block = jnp.where(second, refs[1][pl.ds(c * 24, 48), :].astype(F32), block)
        for i in (0, 1):
            for k in range(3):
                mirror = own(c + i, order[k])
                if c + i == sign_comp:
                    mirror = -mirror
                got = block[(i * 3 + k) * 8 : (i * 3 + k + 1) * 8]
                scratch[pl.ds(((c + i) * 3 + k) * 8, 8), :] = jnp.where(at_wall, mirror, got)


def flux_x_inner_kernel(
    f_ref, r_ref, acc_ref, src_ref, left, right, edge_ref, out_ref, token
):
    def line(c):
        return [None] * 3 + [r_ref[rows8(c * 8 + x), :] for x in range(8)] + [None] * 3

    face_states(line, left, right, 9, ((5, 8),))
    flux = {f: face_flux(left, right, 9, 0, f) for f in (3, 4, 5)}
    for c in range(COMPS):
        edge_ref[pl.ds(c * 16, 8), :] = flux[3][c]
        edge_ref[pl.ds(c * 16 + 8, 8), :] = flux[5][c]
        for x in range(8):
            at = pl.ds(c * 64 + x * 8, 8)
            change = acc_ref[at, :]
            if x in (3, 4):
                change = change + (flux[x + 1][c] - flux[x][c])
            new = f_ref[at, :] - TIME_STEP * change + CHEM_STEP * src_ref[at, :]
            out_ref[c, pl.ds(x * 8, 8), :] = new
    token[...] = jnp.zeros(token.shape, F32)


def flux_x_kernel(count, r_ref, left_in, right_in, edge_ref, base_ref, *refs):
    flags = place_flags()
    layers, (out_hbm, lo_s, hi_s, left, right, out_ref, sems) = refs[:count], refs[count:]

    def send(ref, first, planes):
        rows = pl.ds(first * 8, planes * 8)
        copy = pltpu.make_async_copy(ref.at[:, rows], out_hbm.at[:, rows], sems.at[first])
        copy.start()
        return copy

    copies = [send(base_ref, 3, 2)]

    def own(c, x):
        return r_ref[pl.ds(c * 64 + x * 8, 8), :]

    halo_lines(layers, lo_s, own, 1, flags[0], (2, 1, 0), flags[6] == 0)
    halo_lines(layers, hi_s, own, 1, flags[1], (7, 6, 5), flags[6] == 1)

    def line(c):
        return (
            [lo_s[rows8(c * 3 + k), :] for k in range(3)]
            + [r_ref[rows8(c * 8 + x), :] for x in range(8)]
            + [hi_s[rows8(c * 3 + k), :] for k in range(3)]
        )

    face_states(line, left, right, 9, ((2, 4), (9, 11)))
    for c in range(COMPS):
        at = pl.ds((c * 9 + 2) * 8, 8)
        right[at, :] = right_in[at, :]
        at = pl.ds((c * 9 + 6) * 8, 8)
        left[at, :] = left_in[at, :]

    def emit(x, upper, lower):
        plane = pl.ds(x * 8, 8)
        for c in range(COMPS):
            out_ref[c, plane, :] = base_ref[c, plane, :] - TIME_STEP * (upper[c] - lower[c])
        copies.append(send(out_ref, x, 1))

    flux = {
        3: [edge_ref[pl.ds(c * 16, 8), :] for c in range(COMPS)],
        5: [edge_ref[pl.ds(c * 16 + 8, 8), :] for c in range(COMPS)],
    }
    for f in (2, 1, 0):
        flux[f] = face_flux(left, right, 9, 0, f)
        emit(f, flux[f + 1], flux.pop(f) if f == 0 else flux[f])
    for f in (6, 7, 8):
        flux[f] = face_flux(left, right, 9, 0, f)
        emit(f - 1, flux[f], flux[f - 1])
    for copy in copies:
        copy.wait()


def flux_y_kernel(count, r_ref, *refs):
    flags = place_flags()
    layers, (out_ref, token, lo_s, hi_s, left, right) = refs[:count], refs[count:]

    def own(c, y):
        return r_ref[pl.ds(c * 64 + y, 8, stride=8), :]

    halo_lines(layers, lo_s, own, 2, flags[2], (2, 1, 0), flags[7] == 0)
    halo_lines(layers, hi_s, own, 2, flags[3], (7, 6, 5), flags[7] == 1)

    def line(c):
        return (
            [lo_s[rows8(c * 3 + k), :] for k in range(3)]
            + [r_ref[pl.ds(c * 64 + y, 8, stride=8), :] for y in range(8)]
            + [hi_s[rows8(c * 3 + k), :] for k in range(3)]
        )

    face_states(line, left, right, 9)

    def emit(c, y, change):
        out_ref[pl.ds(c * 64 + y, 8, stride=8), :] = change

    line_changes(left, right, 9, 1, emit)
    token[...] = jnp.zeros(token.shape, F32)


def flux_z_kernel(count, zt_ref, acc_ref, *refs):
    flags = place_flags()
    layers, (out_ref, token, ext, left, right, back) = refs[:count], refs[count:]
    low3, low = half_lanes((3, 128)), half_lanes((64, 128))

    def got(c, second):
        x = layers[0][pl.ds(c * 3, 3), :]
        if count == 2:
            x = jnp.where(second, layers[1][pl.ds(c * 3, 3), :], x)
        return swap_halves(x)

    for c in range(COMPS):
        sign = -1.0 if c == 3 else 1.0
        own = zt_ref[pl.ds(c * 64, 64), :]
        first, last = own[:3], own[61:]
        mirror_lo = sign * jnp.concatenate([first[2:3], first[1:2], first[0:1]], axis=0)
        mirror_hi = sign * jnp.concatenate([last[2:3], last[1:2], last[0:1]], axis=0)
        below = jnp.where(flags[4], mirror_lo, got(c, flags[8] == 0))
        above = jnp.where(flags[5], mirror_hi, got(c, flags[8] == 1))
        ext[pl.ds(c * 72, 3), :] = jnp.where(low3, below, swap_halves(last))
        ext[pl.ds(c * 72 + 3, 64), :] = own
        ext[pl.ds(c * 72 + 67, 3), :] = jnp.where(low3, swap_halves(first), above)

    def line(c):
        return [ext[pl.ds(c * 72 + e, 8, stride=8), :] for e in range(14)]

    face_states(line, left, right, 9)

    def emit(c, z, change):
        back[pl.ds(c * 64 + z, 8, stride=8), :] = change

    line_changes(left, right, 9, 2, emit)
    for c in range(0, COMPS, 2):
        even, odd = back[pl.ds(c * 64, 64), :], back[pl.ds(c * 64 + 64, 64), :]
        t = jnp.concatenate(
            [jnp.where(low, even, swap_halves(odd)), jnp.where(low, swap_halves(even), odd)],
            axis=0,
        )
        at = pl.ds(c * 64, 128)
        out_ref[at, :] = acc_ref[at, :] + jnp.transpose(t)
    token[...] = jnp.zeros(token.shape, F32)


def impulse_kernel(own, table_ref, got_ref, out_ref):
    place = place_flags()[9] * own
    row = pl.ds(place // 128, 1)
    loads = jnp.broadcast_to(table_ref[row, :] + got_ref[row, :], (8, 128))
    loads = pltpu.roll(loads, (128 - place % 128) % 128, 1)
    out_ref[...] = loads[:1, :own] * (1.0 / (PATCH * PATCH))


def own_impulse(table, got, own):
    return pl.pallas_call(
        lambda *a: impulse_kernel(own, *a),
        out_shape=jax.ShapeDtypeStruct((1, own), F32),
        in_specs=[VM] * 2,
        out_specs=VM,
        compiler_params=GRANT,
        cost_estimate=cost(0.5),
        name="impulse",
    )(table, got)


def state_scratch():
    return [pltpu.VMEM((COMPS * 9 * 8, 128), F32)] * 2


def halo_scratch():
    return [pltpu.VMEM((COMPS * 24, 128), F32)] * 2


def token_shape(table):
    return jax.ShapeDtypeStruct(table.shape, F32)


def flux_x_inner(fields, recon, acc, source, table):
    states = jax.ShapeDtypeStruct((COMPS * 9 * 8, 128), F32)
    return pl.pallas_call(
        flux_x_inner_kernel,
        out_shape=[
            states,
            states,
            jax.ShapeDtypeStruct((COMPS * 16, 128), F32),
            jax.ShapeDtypeStruct((COMPS, 64, 128), F32),
            token_shape(table),
        ],
        in_specs=[VM] * 4,
        out_specs=[VM] * 5,
        compiler_params=GRANT,
        cost_estimate=cost(1),
        name="flux_x_inner",
    )(fields, recon, acc, source)


def flux_x(recon, inner, layers):
    return pl.pallas_call(
        lambda *a: flux_x_kernel(len(layers), *a),
        out_shape=jax.ShapeDtypeStruct((COMPS, 64, 128), F32),
        in_specs=[VM] * (5 + len(layers)),
        out_specs=HBM,
        scratch_shapes=halo_scratch()
        + state_scratch()
        + [pltpu.VMEM((COMPS, 64, 128), F32), pltpu.SemaphoreType.DMA((8,))],
        compiler_params=GRANT,
        cost_estimate=cost(2),
        name="flux_x",
    )(recon, *inner, *layers)


def flux_y(recon, layers, table):
    return pl.pallas_call(
        lambda *a: flux_y_kernel(len(layers), *a),
        out_shape=[jax.ShapeDtypeStruct(recon.shape, F32), token_shape(table)],
        in_specs=[VM] * (1 + len(layers)),
        out_specs=[VM] * 2,
        scratch_shapes=halo_scratch() + state_scratch(),
        compiler_params=GRANT,
        cost_estimate=cost(2),
        name="flux_y",
    )(recon, *layers)


def flux_z(turned, acc, layers, table):
    return pl.pallas_call(
        lambda *a: flux_z_kernel(len(layers), *a),
        out_shape=[jax.ShapeDtypeStruct(acc.shape, F32), token_shape(table)],
        in_specs=[VM] * (2 + len(layers)),
        out_specs=[VM] * 2,
        scratch_shapes=[pltpu.VMEM((COMPS * 72, 128), F32)]
        + state_scratch()
        + [pltpu.VMEM(acc.shape, F32)],
        compiler_params=GRANT,
        cost_estimate=cost(2),
        name="flux_z",
    )(turned, acc, *layers)


def swap(x, axis, second, outer=False):
    n = lax.axis_size(axis)
    pairs = [(i, i + 1) for i in range(int(second), n - 1, 2)]
    if outer:
        pairs.append((0, n - 1))
    return lax.ppermute(x, axis, [(a, b) for a, b in pairs] + [(b, a) for a, b in pairs])


def swap_inner(x, axis, other):
    n, m = lax.axis_size(axis), lax.axis_size(other)
    if m % 2 or n % 2:
        return swap(x, axis, 1)
    pairs = []
    for i in range(n):
        for j in range(m):
            end = i in (0, n - 1)
            to = (i, j ^ 1) if end else (i + 1 if i % 2 else i - 1, j)
            pairs.append((i * m + j, to[0] * m + to[1]))
    return lax.ppermute(x, (axis, other), pairs)


def sum_over(table, axis, step=1):
    size = lax.axis_size(axis)
    if size & (size - 1):
        return lax.psum(table, axis)
    while step < size:
        table = table + lax.ppermute(table, axis, [(i, i ^ step) for i in range(size)])
        step *= 2
    return table


def join_table(rows, height):
    rows = rows[: 3 * height].astype(F32)
    return rows[:height] + rows[height : 2 * height] + rows[2 * height :]


def body(fields, reacting, panel_map, layer_one, layer_two, layer_three, layer_four):
    shape = fields.shape
    sizes = [lax.axis_size(a) for a in AXES]
    pair_x = sizes[0] == 2
    panels_all = 2 * (shape[1] * sizes[0] // PATCH) * (shape[3] * sizes[2] // PATCH)
    own = panels_all // (sizes[0] * sizes[1] * sizes[2])
    height = panels_all // 128
    slots = BAL * min(4, sizes[0])
    layer_rows, edge_rows = COMPS * 24, 40
    ride_y, ride_z = sizes[1] & (sizes[1] - 1) == 0, sizes[2] in (2, 4)

    flat = fields.reshape(-1, shape[3])
    panels, react = panel_map.reshape(-1, shape[3]), reacting.reshape(-1, shape[3])
    layers = (layer_one.T, layer_two, layer_three, layer_four)
    packed = pack(flat, panels, react, layers, height)
    flat, recon, y_first, table, react = packed
    one = layers[0]
    two, three, four = layer_two, layer_three, layer_four
    y_got = [swap(y_first, "gy", 0)]
    turned, *xs, z_first, z_second, token = turn(recon, pair_x, height)
    hidden, row_slot, hit, y_second, token_in = chem_in(recon, react, one, slots, table)
    if sizes[1] > 2:
        y_got.append(swap_inner(y_second, "gy", "gz"))
    half, token_two = chem_layer(chem_two_kernel, layer_two.shape[0] // 2, table, hidden, two)
    table = table + token + token_in + token_two
    if ride_y:
        table = table + join_table(y_got[0][layer_rows:], height)
    if not ride_z:
        table = sum_over(table, "gz")
    z_got = [swap(lax.dynamic_update_slice(z_first, table, (edge_rows, 0)), "gz", 0)]
    hidden, token = chem_layer(
        chem_three_kernel, layer_three.shape[0], table, hidden, half, two, three, table
    )
    if ride_z:
        table = table + z_got[0][edge_rows : edge_rows + height] + token
    if sizes[2] > 2:
        z_second = lax.dynamic_update_slice(z_second, table, (edge_rows, 0))
        z_got.append(swap(z_second, "gz", 1, ride_z))
        if ride_z:
            table = table + z_got[1][edge_rows : edge_rows + height]
    acc, token = flux_y(recon, y_got, table)
    table = table + token
    if pair_x:
        xs = [put_table(table, xs[0])]
    x_got = [swap(x, "gx", m) for m, x in enumerate(xs)]
    acc, token = flux_z(turned, acc, z_got, table)
    source, token_out = chem_out(hidden, four, row_slot, hit, table)
    *inner, token_inner = flux_x_inner(flat, recon, acc, source, table)
    table = table + token + token_out + token_inner
    if pair_x:
        table = table + join_table(x_got[0][layer_rows:], height)
    else:
        table = sum_over(table, "gx")
    rest = jnp.zeros_like(table)
    if not ride_y:
        table = lax.psum(table, "gy")
    elif sizes[1] > 2:
        table = sum_over(table, "gy", 4)
        n, m = sizes[1], sizes[2]
        flip = 1 - m % 2
        pairs = [(i * m + j, (i ^ 2) * m + (j ^ flip)) for i in range(n) for j in range(m)]
        rest = lax.ppermute(table, ("gy", "gz"), pairs)
    new = flux_x(recon, inner, x_got)
    return new.reshape(shape), own_impulse(table, rest, own).reshape(own)


def solution(mesh):
    return jax.shard_map(
        body,
        mesh=mesh,
        in_specs=(
            P(None, "gx", "gy", "gz"),
            P("gx", "gy", "gz"),
            P(None, "gx", "gz"),
            P(),
            P(),
            P(),
            P(),
        ),
        out_specs=(P(None, "gx", "gy", "gz"), P(("gx", "gy", "gz"))),
        check_vma=False,
    )
```
